32 devices in a mesh: row: 4 (over y, x), col: 8 (over z, core).
Axes of the slice: x: 2, y: 2, z: 4, core: 2. Of those that a mesh axis runs over, the one named last changes fastest.
Arguments:
- theta_one: bfloat16 [8192, 4096], P('row', 'col'), may hold values from -4 to 4
- theta_two: bfloat16 [4096, 32768], P('row', 'col'), may hold values from -4 to 4
- cost_one: bfloat16 [8192, 4096], P('row', 'col'), may hold values from -3 to 3
- cost_two: bfloat16 [4096, 32768], P('row', 'col'), may hold values from -3 to 3
- depot_price: float32 [8192], P('row'), may hold values from 0.5 to 2
- hub_price: float32 [4096], replicated, may hold values from -3 to 3
- zone_price: float32 [32768], P('col'), may hold values from 0.5 to 2
- mask_one: int32 [64, 32], P('row', 'col'), may hold values 0 or 1
- mask_two: int32 [32, 256], P('row', 'col'), may hold values 0 or 1
- supply: int32 [8192], P('row'), may hold values from 1 to 4
- demand: int32 [32768], P('col'), may hold values from 1 to 4
- capacity: int32 [4096], replicated, may hold values from 1 to 8
- cot_flow_one: bfloat16 [8192, 4096], P('row', 'col'), may hold values from -6 to 6
- cot_flow_two: bfloat16 [4096, 32768], P('row', 'col'), may hold values from -6 to 6
- cot_depot: float32 [8192], P('row'), may hold values from -6 to 6
- cot_hub: float32 [4096], replicated, may hold values from -6 to 6
- cot_zone: float32 [32768], P('col'), may hold values from -6 to 6
Outputs:
- grad_theta_one: float32 [8192, 4096], P('row', 'col')
- grad_theta_two: float32 [4096, 32768], P('row', 'col')
- grad_cost_one: float32 [8192, 4096], P('row', 'col')
- grad_cost_two: float32 [4096, 32768], P('row', 'col')
- grad_depot: float32 [8192], P('row')
- grad_hub: float32 [4096], replicated
- grad_zone: float32 [32768], P('col')
The draws below stay inside these ranges and needn't reach their ends.
All inputs are finite; a program needn't handle non-finite values. No bound on the sum of `mask_one` or of `mask_two` on one device may be relied on, other than what follows from the above.
Results may differ from the reference program's by a relative error of at most 0.0003.
Values sent between devices are 32-bit elements; how exact they have to be, the bound alone decides.
No kernel may reach another device: no remote copies, remote signals or barrier semaphores. Data moves between devices by JAX's collectives and lax.ppermute only.
A program may use at most 128 MiB of HBM per device.

```python
import math
import jax
import jax.numpy as jnp

DEP = 8192
HUB = 4096
ZONE = 32768
TILE = 128
ITERS = 2


def set_ends(array, own_key, least, high):
    place = [jax.random.randint(jax.random.fold_in(own_key, axis), (), 0, length) for axis, length in enumerate(array.shape)]
    longest = array.shape.index(max(array.shape))
    next_to = place[:longest] + [(place[longest] + 1) % array.shape[longest]] + place[longest + 1:]
    return array.at[tuple(place)].set(least).at[tuple(next_to)].set(high)


def steps_of(stream_key, shape, split, smallest, high):
    loudness = 1.0
    for position, shards_of in split:
        draws = jax.random.uniform(jax.random.fold_in(jax.random.fold_in(stream_key, 6), position), (shards_of,), jnp.float32, smallest / len(split), high / len(split))
        loudness = loudness * jnp.repeat(jnp.exp(draws), shape[position] // shards_of).reshape((-1,) + (1,) * (len(shape) - 1 - position))
    return loudness


def normal_values(own_key, extent, scale, bound, cuts=(), dtype=jnp.bfloat16):
    loudness = steps_of(own_key, extent, cuts, -0.22, 0.18) if cuts else 1.0
    values = jax.random.normal(own_key, extent, jnp.float32) * scale * loudness
    return jnp.minimum(jnp.maximum(values, -bound), bound).astype(dtype)


def setup_inputs(seed: int = 0) -> dict:
    arg_keys = jax.random.split(jax.random.key(seed), 18)
    theta_one = normal_values(arg_keys[0], (DEP, HUB), 1.0, 4.0, ((0, 4), (1, 8)))
    theta_two = normal_values(arg_keys[1], (HUB, ZONE), 1.0, 4.0, ((0, 4), (1, 8)))
    cost_one = normal_values(arg_keys[2], (DEP, HUB), 0.5, 3.0, ((0, 4), (1, 8)))
    cost_two = normal_values(arg_keys[3], (HUB, ZONE), 0.5, 3.0, ((0, 4), (1, 8)))
    depot_price = jnp.clip(jnp.exp(math.log(2.0) - 1.3862944 * jax.random.uniform(arg_keys[4], (DEP,), jnp.float32) ** steps_of(arg_keys[4], (DEP,), ((0, 4),), -0.2, 0.2)), 0.5, 2.0)
    hub_price = normal_values(arg_keys[5], (HUB,), 0.5, 3.0, (), jnp.float32)
    zone_price = jnp.clip(jnp.exp(math.log(2.0) - 1.3862944 * jax.random.uniform(arg_keys[6], (ZONE,), jnp.float32) ** steps_of(arg_keys[6], (ZONE,), ((0, 8),), -0.2, 0.2)), 0.5, 2.0)
    mask_one = set_ends((jax.random.randint(arg_keys[7], (DEP // TILE, HUB // TILE), 0, 3) < 2).astype(jnp.int32), jax.random.fold_in(arg_keys[7], 1), 0, 1)
    mask_two = set_ends((jax.random.randint(arg_keys[8], (HUB // TILE, ZONE // TILE), 0, 3) < 2).astype(jnp.int32), jax.random.fold_in(arg_keys[8], 1), 0, 1)
    supply = set_ends(jax.random.randint(arg_keys[9], (DEP,), 1, 5), jax.random.fold_in(arg_keys[9], 1), 1, 4).astype(jnp.int32)
    demand = set_ends(jax.random.randint(arg_keys[10], (ZONE,), 1, 5), jax.random.fold_in(arg_keys[10], 1), 1, 4).astype(jnp.int32)
    capacity = set_ends(jax.random.randint(arg_keys[11], (HUB,), 1, 9), jax.random.fold_in(arg_keys[11], 1), 1, 8).astype(jnp.int32)
    cot_flow_one = normal_values(arg_keys[12], (DEP, HUB), 1.0, 6.0, ((0, 4), (1, 8)))
    cot_flow_two = normal_values(arg_keys[13], (HUB, ZONE), 1.0, 6.0, ((0, 4), (1, 8)))
    cot_depot = normal_values(arg_keys[14], (DEP,), 1.0, 6.0, ((0, 4),), jnp.float32)
    cot_hub = normal_values(arg_keys[15], (HUB,), 1.0, 6.0, (), jnp.float32)
    cot_zone = normal_values(arg_keys[16], (ZONE,), 1.0, 6.0, ((0, 8),), jnp.float32)
    return {"theta_one": theta_one, "theta_two": theta_two, "cost_one": cost_one, "cost_two": cost_two, "depot_price": depot_price, "hub_price": hub_price, "zone_price": zone_price, "mask_one": mask_one, "mask_two": mask_two, "supply": supply, "demand": demand, "capacity": capacity, "cot_flow_one": cot_flow_one, "cot_flow_two": cot_flow_two, "cot_depot": cot_depot, "cot_hub": cot_hub, "cot_zone": cot_zone}


STEP_PRIMAL = 0.5
STEP_DUAL = 0.5
HUB_RATE = 4.0


def expand(tiles, tile_size):
    block_rows, block_cols = tiles.shape
    spread = jnp.broadcast_to(tiles.astype(jnp.float32)[:, None, :, None], (block_rows, tile_size, block_cols, tile_size))
    return spread.reshape(block_rows * tile_size, block_cols * tile_size)


def logistic(values):
    return 1.0 / (1.0 + jnp.exp(-values))


def slope(values):
    sigma = logistic(values)
    return sigma * (1.0 - sigma)


def reference(theta_one, theta_two, cost_one, cost_two, depot_price, hub_price, zone_price, mask_one, mask_two, supply, demand, capacity, cot_flow_one, cot_flow_two, cot_depot, cot_hub, cot_zone):
    levels = capacity.astype(jnp.float32)
    keep_one = expand(mask_one, TILE) * levels[None, :]
    keep_two = expand(mask_two, TILE) * (0.25 * levels)[:, None]
    supply_level = 0.5 * supply.astype(jnp.float32)
    demand_level = 0.125 * demand.astype(jnp.float32)
    cost_first = cost_one.astype(jnp.float32)
    cost_second = cost_two.astype(jnp.float32)
    states_one = [theta_one.astype(jnp.float32)]
    states_two = [theta_two.astype(jnp.float32)]
    depot_now, hub_now, zone_now = depot_price, hub_price, zone_price
    depot_saved, zone_saved, depot_grow, zone_grow = [], [], [], []
    for counter in range(ITERS):
        old_one = states_one[-1]
        old_two = states_two[-1]
        next_one = old_one - STEP_PRIMAL * (cost_first + depot_now[:, None] + hub_now[None, :])
        next_two = old_two - STEP_PRIMAL * (cost_second - hub_now[:, None] - zone_now[None, :])
        bar_one = keep_one * (2.0 * logistic(next_one) - logistic(old_one))
        bar_two = keep_two * (2.0 * logistic(next_two) - logistic(old_two))
        growth_depot = jnp.exp(STEP_DUAL * (jnp.sum(bar_one, axis=1) / HUB - supply_level))
        growth_zone = jnp.exp(STEP_DUAL * (demand_level - jnp.sum(bar_two, axis=0) / HUB))
        depot_now = depot_now * growth_depot
        zone_now = zone_now * growth_zone
        hub_now = hub_now + HUB_RATE * (jnp.sum(bar_one, axis=0) - jnp.sum(bar_two, axis=1)) / DEP
        depot_saved.append(depot_now)
        zone_saved.append(zone_now)
        depot_grow.append(growth_depot)
        zone_grow.append(growth_zone)
        states_one.append(next_one)
        states_two.append(next_two)
    adj_one = cot_flow_one.astype(jnp.float32) * keep_one * slope(states_one[-1])
    adj_two = cot_flow_two.astype(jnp.float32) * keep_two * slope(states_two[-1])
    adj_depot, adj_hub, adj_zone = cot_depot, cot_hub, cot_zone
    grad_first = jnp.zeros_like(adj_one)
    grad_second = jnp.zeros_like(adj_two)
    for counter in range(ITERS - 1, -1, -1):
        push_depot = adj_depot * depot_saved[counter] * (STEP_DUAL / HUB)
        push_zone = -adj_zone * zone_saved[counter] * (STEP_DUAL / HUB)
        push_hub = adj_hub * (HUB_RATE / DEP)
        weight_one = push_depot[:, None] + push_hub[None, :]
        weight_two = push_zone[None, :] - push_hub[:, None]
        total_one = adj_one + 2.0 * weight_one * keep_one * slope(states_one[counter + 1])
        total_two = adj_two + 2.0 * weight_two * keep_two * slope(states_two[counter + 1])
        adj_one = total_one - weight_one * keep_one * slope(states_one[counter])
        adj_two = total_two - weight_two * keep_two * slope(states_two[counter])
        grad_first = grad_first - STEP_PRIMAL * total_one
        grad_second = grad_second - STEP_PRIMAL * total_two
        adj_depot = adj_depot * depot_grow[counter] - STEP_PRIMAL * jnp.sum(total_one, axis=1)
        adj_hub = adj_hub + STEP_PRIMAL * (jnp.sum(total_two, axis=1) - jnp.sum(total_one, axis=0))
        adj_zone = adj_zone * zone_grow[counter] + STEP_PRIMAL * jnp.sum(total_two, axis=0)
    return (adj_one, adj_two, grad_first, grad_second, adj_depot, adj_hub, adj_zone)
```

```python
import functools

import jax
import jax.numpy as jnp
from jax import lax
from jax.experimental import pallas as pl
from jax.experimental.pallas import tpu as pltpu
from jax.sharding import PartitionSpec as P

STEP_PRIMAL = 0.5
STEP_DUAL = 0.5
HUB_RATE = 4.0
LANES = 128
SUB = 32
F32 = jnp.float32
BF16 = jnp.bfloat16


def swap(value, axis, size, distance):
    if size & (size - 1) == 0:
        pairs = [(i, i ^ distance) for i in range(size)]
    else:
        pairs = [(i, (i + distance) % size) for i in range(size)]
    return lax.ppermute(value, axis, pairs)


def gather_terms(value, axis, size, distances=None):
    return [value] + [swap(value, axis, size, k) for k in distances or range(1, size)]


def col_terms(value, size):
    if size & (size - 1) or size < 4:
        return gather_terms(value, "col", size)
    both = value + swap(value, "col", size, 1)
    return gather_terms(both, "col", size, range(2, size, 2))


def add_all(terms):
    total = terms[0]
    for term in terms[1:]:
        total = total + term
    return total


def as_rows(line):
    return jnp.broadcast_to(line, (LANES, LANES)).T


def as_line(block):
    return jnp.sum(block.T, axis=0, keepdims=True)


def fold(value):
    return jnp.sum(value.reshape(-1, 8, LANES), axis=0)


def fold_line(value):
    return jnp.sum(value, axis=0, keepdims=True)


def piece(ref, row, lane):
    return ref[pl.ds(row, SUB), pl.ds(lane, LANES)].astype(F32)


class Sizes:
    def __init__(self, dep_rows, hub_cols, hub_rows, zone_cols, hubs, deps):
        self.dep_rows, self.hub_cols, self.hub_rows, self.zone_cols = dep_rows, hub_cols, hub_rows, zone_cols
        self.hubs, self.deps = hubs, deps
        self.dep_lines, self.one_lines = dep_rows // LANES, hub_cols // LANES
        self.two_lines, self.zone_lines = hub_rows // LANES, zone_cols // LANES
        self.hub_lines = hubs // LANES
        self.steps = self.two_lines
        self.per = self.dep_lines // self.steps
        assert self.per * self.steps == self.dep_lines

    def one(self):
        return pl.BlockSpec((self.per * LANES, self.hub_cols), lambda i: (i, 0))

    def two(self):
        return pl.BlockSpec((LANES, self.zone_cols), lambda i: (i, 0))


def whole(lines):
    return pl.BlockSpec((lines, LANES), lambda i: (0, 0))


def smem():
    return pl.BlockSpec(memory_space=pltpu.SMEM)


def line_shape(lines):
    return jax.ShapeDtypeStruct((lines, LANES), F32)


PARAMS = pltpu.CompilerParams(dimension_semantics=("arbitrary",), vmem_limit_bytes=40 * 2**20)


def first_kernel(z, where, mask_one, mask_two, depot, hub, zone, cap, th1, co1, th2, co2,
                 a_one, a_two, col_out, zone_out, depot_pre, zone_pre,
                 row1, row0, hub_acc, zone1, zone0, hub_two):
    i = pl.program_id(0)
    off_one, off_two = where[1] * z.one_lines, where[0] * z.two_lines

    @pl.when(i == 0)
    def _():
        hub_acc[...] = jnp.zeros_like(hub_acc)
        zone1[...] = jnp.zeros_like(zone1)
        zone0[...] = jnp.zeros_like(zone0)

    for k in range(z.per):
        line = i * z.per + k
        dcol = as_rows(0.25 * depot[pl.ds(line, 1), :])
        row1[...] = jnp.zeros_like(row1)
        row0[...] = jnp.zeros_like(row0)
        keeps = jnp.zeros((1, LANES), F32)
        for j in range(z.one_lines):
            hrow = 0.25 * hub[pl.ds(off_one + j, 1), :]
            m = mask_one[line, j].astype(F32)
            km = m * cap[pl.ds(off_one + j, 1), :].astype(F32)
            keeps = keeps + km
            total = 0.5 * LANES / 8 * jnp.broadcast_to(km, (8, LANES))
            for s in range(0, LANES, SUB):
                th = piece(th1, k * LANES + s, j * LANES)
                co = piece(co1, k * LANES + s, j * LANES)
                t0 = jnp.tanh(0.5 * th)
                t1 = jnp.tanh(0.5 * (th - 0.5 * co) - (dcol[s:s + SUB, :] + hrow))
                k1, k0 = km * t1, km * t0
                row1[s:s + SUB, :] += k1
                row0[s:s + SUB, :] += k0
                total = total + (fold(k1) - 0.5 * fold(k0))
                a_one[pl.ds(k * LANES + s, SUB), pl.ds(j * LANES, LANES)] = (km - k1 * t1).astype(BF16)
            hub_acc[:, j * LANES:(j + 1) * LANES] += total
        half = 0.5 * jnp.sum(keeps)
        line1, line0 = as_line(row1[...]), as_line(row0[...])
        col_out[pl.ds(line, 1), :] = half + line1 - 0.5 * line0
        depot_pre[pl.ds(line, 1), :] = half - 0.5 * line1

    hcol = as_rows(0.25 * hub[pl.ds(off_two + i, 1), :])
    kcol = as_rows(0.25 * cap[pl.ds(off_two + i, 1), :].astype(F32))
    row1[...] = jnp.zeros_like(row1)
    row0[...] = jnp.zeros_like(row0)
    ksum = 0.5 * fold(kcol)

    def lane_tile(j, opened):
        lane = pl.multiple_of(j * LANES, LANES)
        m = mask_two[i, j].astype(F32)
        zrow = 0.25 * zone[pl.ds(j, 1), :]
        sum1 = jnp.zeros((8, LANES), F32)
        sum0 = jnp.zeros((8, LANES), F32)
        for s in range(0, LANES, SUB):
            th = piece(th2, s, lane)
            co = piece(co2, s, lane)
            km = m * kcol[s:s + SUB, :]
            t0 = jnp.tanh(0.5 * th)
            t1 = jnp.tanh(0.5 * (th - 0.5 * co) + (hcol[s:s + SUB, :] + zrow))
            k1, k0 = km * t1, km * t0
            row1[s:s + SUB, :] += k1
            row0[s:s + SUB, :] += k0
            sum1 = sum1 + fold(k1)
            sum0 = sum0 + fold(k0)
            a_two[pl.ds(s, SUB), pl.ds(lane, LANES)] = (km - k1 * t1).astype(BF16)
        zone1[:, pl.ds(lane, LANES)] += sum1 - (2.0 * m) * ksum
        zone0[:, pl.ds(lane, LANES)] += sum0 - (6.0 * m) * ksum
        return opened + m

    opened = lax.fori_loop(0, z.zone_lines, lane_tile, jnp.float32(0.0))
    hub_two[pl.ds(i, 1), :] = as_line(row1[...] - 0.5 * row0[...] + (0.5 * opened) * kcol)

    @pl.when(i == z.steps - 1)
    def _():
        for j in range(z.zone_lines):
            line1 = fold_line(zone1[:, j * LANES:(j + 1) * LANES])
            line0 = fold_line(zone0[:, j * LANES:(j + 1) * LANES])
            zone_out[j:j + 1, :] = line1 - 0.5 * line0
            zone_pre[j:j + 1, :] = -0.5 * line1
        put_hub(z, where, col_out, z.dep_lines, hub_acc, hub_two)


def put_hub(z, where, out, base, hub_acc, hub_two):
    out[base:base + z.hub_lines, :] = jnp.zeros((z.hub_lines, LANES), F32)
    for j in range(z.two_lines):
        out[pl.ds(base + where[0] * z.two_lines + j, 1), :] = -hub_two[j:j + 1, :]
    for j in range(z.one_lines):
        at = base + where[1] * z.one_lines + j
        out[pl.ds(at, 1), :] = out[pl.ds(at, 1), :] + fold_line(hub_acc[:, j * LANES:(j + 1) * LANES])


def first_pass(z, where, mask_one, mask_two, depot, hub, zone, cap, th1, co1, th2, co2):
    return pl.pallas_call(
        functools.partial(first_kernel, z),
        grid=(z.steps,),
        in_specs=[smem(), smem(), smem(), whole(z.dep_lines), whole(z.hub_lines), whole(z.zone_lines),
                  whole(z.hub_lines), z.one(), z.one(), z.two(), z.two()],
        out_specs=[z.one(), z.two(), whole(z.dep_lines + z.hub_lines), whole(z.zone_lines),
                   whole(z.dep_lines), whole(z.zone_lines)],
        out_shape=[jax.ShapeDtypeStruct(th1.shape, BF16), jax.ShapeDtypeStruct(th2.shape, BF16),
                   line_shape(z.dep_lines + z.hub_lines), line_shape(z.zone_lines),
                   line_shape(z.dep_lines), line_shape(z.zone_lines)],
        scratch_shapes=[pltpu.VMEM((LANES, LANES), F32), pltpu.VMEM((LANES, LANES), F32),
                        pltpu.VMEM((8, z.hub_cols), F32), pltpu.VMEM((8, z.zone_cols), F32),
                        pltpu.VMEM((8, z.zone_cols), F32), pltpu.VMEM((z.two_lines, LANES), F32)],
        compiler_params=PARAMS, name="first_pass",
    )(where, mask_one, mask_two, depot, hub, zone, cap, th1, co1, th2, co2)


def second_kernel(z, terms, where, mask_one, mask_two, depot, hub, zone, cap, supply, demand, cot_hub,
                  depot_pre, zone_pre, depot_sum, *rest):
    sums, rest = rest[:terms], rest[terms:]
    (th1, co1, cf1, th2, co2, cf2,
     a_one, a_two, depot_out, zone_out, depot_state, zone_state, hub_state, hub_one_out, hub_two_out,
     rowk, rowa, rowe, hub_acc, zonek, zonea, zonee, shift_d, shift_h, shift_z) = rest
    i = pl.program_id(0)
    off_one, off_two = where[1] * z.one_lines, where[0] * z.two_lines
    dl, zl, hl = z.dep_lines, z.zone_lines, z.hub_lines

    @pl.when(i == 0)
    def _():
        hub_acc[...] = jnp.zeros_like(hub_acc)
        zonek[...] = jnp.zeros_like(zonek)
        zonea[...] = jnp.zeros_like(zonea)
        zonee[...] = jnp.zeros_like(zonee)
        total = sums[0][...]
        for term in sums[1:]:
            total = total + term[...]
        grow_d = jnp.exp(STEP_DUAL * (depot_sum[...] / z.hubs - 0.5 * supply[...].astype(F32)))
        grow_z = jnp.exp(STEP_DUAL * (0.125 * demand[...].astype(F32) - total[hl:, :] / z.hubs))
        new_d, new_z = depot[...] * grow_d, zone[...] * grow_z
        new_h = hub[...] + HUB_RATE * total[:hl, :] / z.deps
        depot_state[0:dl, :] = new_d
        depot_state[dl:2 * dl, :] = grow_d
        zone_state[0:zl, :] = new_z
        zone_state[zl:2 * zl, :] = grow_z
        hub_state[...] = new_h
        shift_d[...] = 0.25 * (depot[...] + new_d)
        shift_h[...] = 0.25 * (hub[...] + new_h)
        shift_z[...] = 0.25 * (zone[...] + new_z)

    push = 2.0 * HUB_RATE / z.deps
    for k in range(z.per):
        line = i * z.per + k
        dcol = as_rows(shift_d[pl.ds(line, 1), :])
        for ref in (rowk, rowa, rowe):
            ref[...] = jnp.zeros_like(ref)
        for j in range(z.one_lines):
            hrow = shift_h[pl.ds(off_one + j, 1), :]
            prow = push * cot_hub[pl.ds(off_one + j, 1), :]
            km = mask_one[line, j].astype(F32) * cap[pl.ds(off_one + j, 1), :].astype(F32)
            total = jnp.zeros((8, LANES), F32)
            for s in range(0, LANES, SUB):
                th = piece(th1, k * LANES + s, j * LANES)
                co = piece(co1, k * LANES + s, j * LANES)
                cf = piece(cf1, k * LANES + s, j * LANES)
                t2 = jnp.tanh(0.5 * (th - co) - (dcol[s:s + SUB, :] + hrow))
                k2 = km * t2
                a2 = km - k2 * t2
                e = (cf + prow) * a2
                rowk[s:s + SUB, :] += k2
                rowa[s:s + SUB, :] += a2
                rowe[s:s + SUB, :] += e
                total = total + fold(e)
                a_one[pl.ds(k * LANES + s, SUB), pl.ds(j * LANES, LANES)] = a2.astype(BF16)
            hub_acc[:, j * LANES:(j + 1) * LANES] += total
        depot_out[pl.ds(line, 1), :] = depot_pre[pl.ds(line, 1), :] + as_line(rowk[...])
        depot_out[pl.ds(dl + line, 1), :] = as_line(rowa[...])
        depot_out[pl.ds(2 * dl + line, 1), :] = as_line(rowe[...])

    hcol = as_rows(shift_h[pl.ds(off_two + i, 1), :])
    pcol = as_rows(push * cot_hub[pl.ds(off_two + i, 1), :])
    kcol = as_rows(0.25 * cap[pl.ds(off_two + i, 1), :].astype(F32))
    rowe[...] = jnp.zeros_like(rowe)

    def lane_tile(j, carry):
        lane = pl.multiple_of(j * LANES, LANES)
        m = mask_two[i, j].astype(F32)
        zrow = shift_z[pl.ds(j, 1), :]
        sumk = jnp.zeros((8, LANES), F32)
        suma = jnp.zeros((8, LANES), F32)
        sume = jnp.zeros((8, LANES), F32)
        for s in range(0, LANES, SUB):
            th = piece(th2, s, lane)
            co = piece(co2, s, lane)
            cf = piece(cf2, s, lane)
            km = m * kcol[s:s + SUB, :]
            t2 = jnp.tanh(0.5 * (th - co) + (hcol[s:s + SUB, :] + zrow))
            k2 = km * t2
            a2 = km - k2 * t2
            e = (cf - pcol[s:s + SUB, :]) * a2
            rowe[s:s + SUB, :] += e
            sumk = sumk + fold(k2)
            suma = suma + fold(a2)
            sume = sume + fold(e)
            a_two[pl.ds(s, SUB), pl.ds(lane, LANES)] = a2.astype(BF16)
        zonek[:, pl.ds(lane, LANES)] += sumk
        zonea[:, pl.ds(lane, LANES)] += suma
        zonee[:, pl.ds(lane, LANES)] += sume
        return carry

    lax.fori_loop(0, zl, lane_tile, 0)
    hub_two_out[pl.ds(i, 1), :] = as_line(rowe[...])

    @pl.when(i == z.steps - 1)
    def _():
        for j in range(zl):
            at = slice(j * LANES, (j + 1) * LANES)
            zone_out[j:j + 1, :] = zone_pre[j:j + 1, :] + fold_line(zonek[:, at])
            zone_out[zl + j:zl + j + 1, :] = fold_line(zonea[:, at])
            zone_out[2 * zl + j:2 * zl + j + 1, :] = fold_line(zonee[:, at])
        for j in range(z.one_lines):
            hub_one_out[j:j + 1, :] = fold_line(hub_acc[:, j * LANES:(j + 1) * LANES])


def second_pass(z, where, mask_one, mask_two, depot, hub, zone, cap, supply, demand, cot_hub,
                depot_pre, zone_pre, depot_sum, sums, th1, co1, cf1, th2, co2, cf2):
    dl, zl, hl = z.dep_lines, z.zone_lines, z.hub_lines
    return pl.pallas_call(
        functools.partial(second_kernel, z, len(sums)),
        grid=(z.steps,),
        in_specs=[smem(), smem(), smem(), whole(dl), whole(hl), whole(zl), whole(hl), whole(dl), whole(zl), whole(hl),
                  whole(dl), whole(zl), whole(dl)] + [whole(hl + zl)] * len(sums)
                 + [z.one()] * 3 + [z.two()] * 3,
        out_specs=[z.one(), z.two(), whole(3 * dl), whole(3 * zl), whole(2 * dl), whole(2 * zl), whole(hl),
                   whole(z.one_lines), whole(z.two_lines)],
        out_shape=[jax.ShapeDtypeStruct(th1.shape, BF16), jax.ShapeDtypeStruct(th2.shape, BF16),
                   line_shape(3 * dl), line_shape(3 * zl), line_shape(2 * dl), line_shape(2 * zl), line_shape(hl),
                   line_shape(z.one_lines), line_shape(z.two_lines)],
        scratch_shapes=[pltpu.VMEM((LANES, LANES), F32)] * 3
                       + [pltpu.VMEM((8, z.hub_cols), F32)] + [pltpu.VMEM((8, z.zone_cols), F32)] * 3
                       + [pltpu.VMEM((dl, LANES), F32), pltpu.VMEM((hl, LANES), F32), pltpu.VMEM((zl, LANES), F32)],
        compiler_params=PARAMS, name="second_pass",
    )(where, mask_one, mask_two, depot, hub, zone, cap, supply, demand, cot_hub, depot_pre, zone_pre, depot_sum,
      *sums, th1, co1, cf1, th2, co2, cf2)


def third_kernel(z, d_terms, z_terms, where, supply, demand, cot_depot, cot_zone, depot_state, zone_state,
                 hub_one_in, hub_two_in, *rest):
    d_sums, rest = rest[:d_terms], rest[d_terms:]
    z_sums, rest = rest[:z_terms], rest[z_terms:]
    a_one, a_two, depot_out, zone_out, hub_out, row, hub_acc, hub_two = rest
    i = pl.program_id(0)
    dl, zl = z.dep_lines, z.zone_lines
    rate = STEP_DUAL / z.hubs

    @pl.when(i == 0)
    def _():
        hub_acc[...] = jnp.zeros_like(hub_acc)
        total = d_sums[0][...]
        for term in d_sums[1:]:
            total = total + term[...]
        grow = jnp.exp(STEP_DUAL * (total[0:dl, :] / z.hubs - 0.5 * supply[...].astype(F32)))
        first, first_grow = depot_state[0:dl, :], depot_state[dl:2 * dl, :]
        push = cot_depot[...] * (first * grow) * rate
        reached = 0.25 * (total[2 * dl:3 * dl, :] + 2.0 * push * total[dl:2 * dl, :])
        adj = cot_depot[...] * grow - STEP_PRIMAL * reached
        depot_out[0:dl, :] = push
        depot_out[dl:2 * dl, :] = adj * first * rate
        depot_out[2 * dl:3 * dl, :] = adj * first_grow - STEP_PRIMAL * reached
        total = z_sums[0][...]
        for term in z_sums[1:]:
            total = total + term[...]
        grow = jnp.exp(STEP_DUAL * (0.125 * demand[...].astype(F32) - total[0:zl, :] / z.hubs))
        first, first_grow = zone_state[0:zl, :], zone_state[zl:2 * zl, :]
        push = -(cot_zone[...] * (first * grow) * rate)
        reached = 0.25 * (total[2 * zl:3 * zl, :] + 2.0 * push * total[zl:2 * zl, :])
        adj = cot_zone[...] * grow + STEP_PRIMAL * reached
        zone_out[0:zl, :] = push
        zone_out[zl:2 * zl, :] = -(adj * first * rate)
        zone_out[2 * zl:3 * zl, :] = adj * first_grow + STEP_PRIMAL * reached

    for k in range(z.per):
        dcol = as_rows(depot_out[pl.ds(i * z.per + k, 1), :])
        for j in range(z.one_lines):
            total = jnp.zeros((8, LANES), F32)
            for s in range(0, LANES, SUB):
                total = total + fold(piece(a_one, k * LANES + s, j * LANES) * dcol[s:s + SUB, :])
            hub_acc[:, j * LANES:(j + 1) * LANES] += total

    for s in range(0, LANES, SUB):
        def lane_tile(j, total):
            return total + piece(a_two, s, pl.multiple_of(j * LANES, LANES)) * zone_out[pl.ds(j, 1), :]

        row[s:s + SUB, :] = lax.fori_loop(0, zl, lane_tile, jnp.zeros((SUB, LANES), F32), unroll=4)
    hub_two[pl.ds(i, 1), :] = -0.25 * (hub_two_in[pl.ds(i, 1), :] + 2.0 * as_line(row[...]))

    @pl.when(i == z.steps - 1)
    def _():
        hub_out[...] = jnp.zeros_like(hub_out)
        for j in range(z.two_lines):
            hub_out[pl.ds(where[0] * z.two_lines + j, 1), :] = -hub_two[j:j + 1, :]
        for j in range(z.one_lines):
            at = where[1] * z.one_lines + j
            line = fold_line(hub_acc[:, j * LANES:(j + 1) * LANES])
            hub_out[pl.ds(at, 1), :] = hub_out[pl.ds(at, 1), :] - 0.25 * (hub_one_in[j:j + 1, :] + 2.0 * line)


def third_pass(z, where, supply, demand, cot_depot, cot_zone, depot_state, zone_state, hub_one, hub_two,
               d_sums, z_sums, a_one, a_two):
    dl, zl, hl = z.dep_lines, z.zone_lines, z.hub_lines
    return pl.pallas_call(
        functools.partial(third_kernel, z, len(d_sums), len(z_sums)),
        grid=(z.steps,),
        in_specs=[smem(), whole(dl), whole(zl), whole(dl), whole(zl), whole(2 * dl), whole(2 * zl),
                  whole(z.one_lines), whole(z.two_lines)]
                 + [whole(3 * dl)] * len(d_sums) + [whole(3 * zl)] * len(z_sums) + [z.one(), z.two()],
        out_specs=[whole(3 * dl), whole(3 * zl), whole(hl)],
        out_shape=[line_shape(3 * dl), line_shape(3 * zl), line_shape(hl)],
        scratch_shapes=[pltpu.VMEM((LANES, LANES), F32), pltpu.VMEM((8, z.hub_cols), F32),
                        pltpu.VMEM((z.two_lines, LANES), F32)],
        compiler_params=PARAMS, name="third_pass",
    )(where, supply, demand, cot_depot, cot_zone, depot_state, zone_state, hub_one, hub_two,
      *d_sums, *z_sums, a_one, a_two)


def fourth_kernel(z, terms, where, cot_hub, depot_push, zone_push, *rest):
    sums, rest = rest[:terms], rest[terms:]
    (a_one, a_two, hub_out, col_out, zone_out, row, hub_acc, zone_acc, hub_two, mix) = rest
    i = pl.program_id(0)
    off_one, off_two = where[1] * z.one_lines, where[0] * z.two_lines
    dl, zl, hl = z.dep_lines, z.zone_lines, z.hub_lines
    rate = HUB_RATE / z.deps

    @pl.when(i == 0)
    def _():
        hub_acc[...] = jnp.zeros_like(hub_acc)
        zone_acc[...] = jnp.zeros_like(zone_acc)
        total = sums[0][...]
        for term in sums[1:]:
            total = total + term[...]
        adj = cot_hub[...] + STEP_PRIMAL * total
        late, early = cot_hub[...] * rate, adj * rate
        hub_out[0:hl, :] = late
        hub_out[hl:2 * hl, :] = early
        hub_out[2 * hl:3 * hl, :] = adj + STEP_PRIMAL * total
        mix[0:hl, :] = 0.25 * (2.0 * early - late)
        mix[hl:hl + dl, :] = 0.25 * (2.0 * depot_push[dl:2 * dl, :] - depot_push[0:dl, :])
        mix[hl + dl:, :] = 0.25 * (2.0 * zone_push[zl:2 * zl, :] - zone_push[0:zl, :])

    for k in range(z.per):
        line = i * z.per + k
        dcol = as_rows(mix[pl.ds(hl + line, 1), :])
        row[...] = jnp.zeros_like(row)
        for j in range(z.one_lines):
            hrow = mix[pl.ds(off_one + j, 1), :]
            total = jnp.zeros((8, LANES), F32)
            for s in range(0, LANES, SUB):
                y = piece(a_one, k * LANES + s, j * LANES) * (dcol[s:s + SUB, :] + hrow)
                row[s:s + SUB, :] += y
                total = total + fold(y)
            hub_acc[:, j * LANES:(j + 1) * LANES] += total
        col_out[pl.ds(line, 1), :] = as_line(row[...])

    hcol = as_rows(mix[pl.ds(off_two + i, 1), :])
    row[...] = jnp.zeros_like(row)

    def lane_tile(j, carry):
        lane = pl.multiple_of(j * LANES, LANES)
        zrow = mix[pl.ds(hl + dl + j, 1), :]
        total = jnp.zeros((8, LANES), F32)
        for s in range(0, LANES, SUB):
            y = piece(a_two, s, lane) * (zrow - hcol[s:s + SUB, :])
            row[s:s + SUB, :] += y
            total = total + fold(y)
        zone_acc[:, pl.ds(lane, LANES)] += total
        return carry

    lax.fori_loop(0, zl, lane_tile, 0)
    hub_two[pl.ds(i, 1), :] = as_line(row[...])

    @pl.when(i == z.steps - 1)
    def _():
        for j in range(zl):
            zone_out[j:j + 1, :] = fold_line(zone_acc[:, j * LANES:(j + 1) * LANES])
        put_hub(z, where, col_out, dl, hub_acc, hub_two)


def fourth_pass(z, where, cot_hub, depot_push, zone_push, sums, a_one, a_two):
    dl, zl, hl = z.dep_lines, z.zone_lines, z.hub_lines
    return pl.pallas_call(
        functools.partial(fourth_kernel, z, len(sums)),
        grid=(z.steps,),
        in_specs=[smem(), whole(hl), whole(3 * dl), whole(3 * zl)] + [whole(hl)] * len(sums) + [z.one(), z.two()],
        out_specs=[whole(3 * hl), whole(dl + hl), whole(zl)],
        out_shape=[line_shape(3 * hl), line_shape(dl + hl), line_shape(zl)],
        scratch_shapes=[pltpu.VMEM((LANES, LANES), F32), pltpu.VMEM((8, z.hub_cols), F32),
                        pltpu.VMEM((8, z.zone_cols), F32), pltpu.VMEM((z.two_lines, LANES), F32),
                        pltpu.VMEM((hl + dl + zl, LANES), F32)],
        compiler_params=PARAMS, name="fourth_pass",
    )(where, cot_hub, depot_push, zone_push, *sums, a_one, a_two)


def result(th, co, cf, shift1, shift2, twice_late, mixed, early, km):
    t0 = jnp.tanh(0.5 * th)
    t1 = jnp.tanh(0.5 * (th - 0.5 * co) + shift1)
    t2 = jnp.tanh(0.5 * (th - co) + shift2)
    last = (cf + twice_late) * (1.0 - t2 * t2)
    middle = mixed * (1.0 - t1 * t1)
    start = early * (1.0 - t0 * t0)
    return km * (last + middle - start), -km * (last + 0.5 * middle)


def final_kernel(z, where, mask_one, mask_two, depot, hub, zone, cap, depot_state, hub_state, zone_state,
                 depot_push, hub_push, zone_push, th1, co1, cf1, th2, co2, cf2,
                 theta_one, cost_one, theta_two, cost_two):
    i = pl.program_id(0)
    off_one, off_two = where[1] * z.one_lines, where[0] * z.two_lines
    dl, zl, hl = z.dep_lines, z.zone_lines, z.hub_lines

    def vectors(line, sign, now, after, push, lines):
        a, b = now[pl.ds(line, 1), :], after[pl.ds(line, 1), :]
        late, early = push[pl.ds(line, 1), :], push[pl.ds(lines + line, 1), :]
        return (0.25 * sign * a, 0.25 * sign * (a + b), 2.0 * late, 2.0 * early - late, early)

    for k in range(z.per):
        line = i * z.per + k
        cols = [as_rows(v) for v in vectors(line, -1.0, depot, depot_state, depot_push, dl)]
        for j in range(z.one_lines):
            rows = vectors(off_one + j, -1.0, hub, hub_state, hub_push, hl)
            km = (0.25 * mask_one[line, j].astype(F32)) * cap[pl.ds(off_one + j, 1), :].astype(F32)
            for s in range(0, LANES, SUB):
                at = (k * LANES + s, j * LANES)
                both = [c[s:s + SUB, :] + r for c, r in zip(cols, rows)]
                theta, cost = result(piece(th1, *at), piece(co1, *at), piece(cf1, *at), *both, km)
                theta_one[pl.ds(at[0], SUB), pl.ds(at[1], LANES)] = theta
                cost_one[pl.ds(at[0], SUB), pl.ds(at[1], LANES)] = cost

    line = off_two + i
    hubs = vectors(line, 1.0, hub, hub_state, hub_push, hl)
    cols = [as_rows(v) for v in (hubs[0], hubs[1], -hubs[2], -hubs[3], -hubs[4])]
    kcol = as_rows(0.0625 * cap[pl.ds(line, 1), :].astype(F32))

    def lane_tile(j, carry):
        lane = pl.multiple_of(j * LANES, LANES)
        rows = vectors(j, 1.0, zone, zone_state, zone_push, zl)
        m = mask_two[i, j].astype(F32)
        for s in range(0, LANES, SUB):
            both = [c[s:s + SUB, :] + r for c, r in zip(cols, rows)]
            theta, cost = result(piece(th2, s, lane), piece(co2, s, lane), piece(cf2, s, lane), *both,
                                 m * kcol[s:s + SUB, :])
            theta_two[pl.ds(s, SUB), pl.ds(lane, LANES)] = theta
            cost_two[pl.ds(s, SUB), pl.ds(lane, LANES)] = cost
        return carry

    lax.fori_loop(0, zl, lane_tile, 0)


def final_pass(z, where, mask_one, mask_two, depot, hub, zone, cap, depot_state, hub_state, zone_state,
               depot_push, hub_push, zone_push, th1, co1, cf1, th2, co2, cf2):
    dl, zl, hl = z.dep_lines, z.zone_lines, z.hub_lines
    return pl.pallas_call(
        functools.partial(final_kernel, z),
        grid=(z.steps,),
        in_specs=[smem(), smem(), smem(), whole(dl), whole(hl), whole(zl), whole(hl), whole(2 * dl), whole(hl),
                  whole(2 * zl), whole(3 * dl), whole(3 * hl), whole(3 * zl)] + [z.one()] * 3 + [z.two()] * 3,
        out_specs=[z.one(), z.one(), z.two(), z.two()],
        out_shape=[jax.ShapeDtypeStruct(th1.shape, F32), jax.ShapeDtypeStruct(th1.shape, F32),
                   jax.ShapeDtypeStruct(th2.shape, F32), jax.ShapeDtypeStruct(th2.shape, F32)],
        compiler_params=PARAMS, name="final_pass",
    )(where, mask_one, mask_two, depot, hub, zone, cap, depot_state, hub_state, zone_state,
      depot_push, hub_push, zone_push, th1, co1, cf1, th2, co2, cf2)


def on_device(rows, cols, theta_one, theta_two, cost_one, cost_two, depot_price, hub_price, zone_price,
              mask_one, mask_two, supply, demand, capacity, cot_flow_one, cot_flow_two,
              cot_depot, cot_hub, cot_zone):
    z = Sizes(*theta_one.shape, *theta_two.shape, hub_price.shape[0], theta_one.shape[0] * rows)
    dl, hl, zl = z.dep_lines, z.hub_lines, z.zone_lines
    where = jnp.stack([lax.axis_index("row"), lax.axis_index("col")]).astype(jnp.int32)
    lines = lambda v: v.reshape(-1, LANES)
    depot, hub, zone, cap = lines(depot_price), lines(hub_price), lines(zone_price), lines(capacity)
    supply, demand = lines(supply), lines(demand)
    cot_depot, cot_hub, cot_zone = lines(cot_depot), lines(cot_hub), lines(cot_zone)

    a1_one, a1_two, col_vec, zone_vec, depot_pre, zone_pre = first_pass(
        z, where, mask_one, mask_two, depot, hub, zone, cap, theta_one, cost_one, theta_two, cost_two)
    col_sum = add_all(col_terms(col_vec, cols))
    row_vec = jnp.concatenate([col_sum[dl:], zone_vec])
    sums = gather_terms(row_vec, "row", rows)
    (a2_one, a2_two, depot_vec, zone_vec, depot_state, zone_state, hub_state, hub_one, hub_two) = second_pass(
        z, where, mask_one, mask_two, depot, hub, zone, cap, supply, demand, cot_hub, depot_pre, zone_pre,
        col_sum[:dl], sums, theta_one, cost_one, cot_flow_one, theta_two, cost_two, cot_flow_two)
    d_sums = col_terms(depot_vec, cols)
    z_sums = gather_terms(zone_vec, "row", rows)
    depot_push, zone_push, hub_vec = third_pass(
        z, where, supply, demand, cot_depot, cot_zone, depot_state, zone_state, hub_one, hub_two,
        d_sums, z_sums, a2_one, a2_two)
    hub_sums = gather_terms(add_all(col_terms(hub_vec, cols)), "row", rows)
    hub_push, col_vec, zone_vec = fourth_pass(z, where, cot_hub, depot_push, zone_push, hub_sums, a1_one, a1_two)
    grad_theta_one, grad_cost_one, grad_theta_two, grad_cost_two = final_pass(
        z, where, mask_one, mask_two, depot, hub, zone, cap, depot_state, hub_state, zone_state,
        depot_push, hub_push, zone_push, theta_one, cost_one, cot_flow_one, theta_two, cost_two, cot_flow_two)
    col_sum = add_all(col_terms(col_vec, cols))
    row_sum = add_all(gather_terms(jnp.concatenate([col_sum[dl:], zone_vec]), "row", rows))
    grad_depot = depot_push[2 * dl:] - STEP_PRIMAL * col_sum[:dl]
    grad_hub = hub_push[2 * hl:] - STEP_PRIMAL * row_sum[:hl]
    grad_zone = zone_push[2 * zl:] + STEP_PRIMAL * row_sum[hl:]
    return (grad_theta_one, grad_theta_two, grad_cost_one, grad_cost_two,
            grad_depot.reshape(-1), grad_hub.reshape(-1), grad_zone.reshape(-1))


def solution(mesh):
    split, row, col, copied = P("row", "col"), P("row"), P("col"), P()
    return jax.shard_map(
        functools.partial(on_device, mesh.shape["row"], mesh.shape["col"]),
        mesh=mesh,
        in_specs=(split, split, split, split, row, copied, col, split, split, row, col, copied, split, split,
                  row, copied, col),
        out_specs=(split, split, split, split, row, copied, col),
        check_vma=False,
    )
```

```python
import functools

import jax
import jax.numpy as jnp
from jax import lax
from jax.experimental import pallas as pl
from jax.experimental.pallas import tpu as pltpu
from jax.sharding import PartitionSpec as P

STEP_PRIMAL = 0.5
STEP_DUAL = 0.5
HUB_RATE = 4.0
LANES = 128
SUB = 32
F32 = jnp.float32
BF16 = jnp.bfloat16


def swap(value, axis, size, distance):
    if size & (size - 1) == 0:
        pairs = [(i, i ^ distance) for i in range(size)]
    else:
        pairs = [(i, (i + distance) % size) for i in range(size)]
    return lax.ppermute(value, axis, pairs)


def gather_terms(value, axis, size, distances=None):
    return [value] + [swap(value, axis, size, k) for k in distances or range(1, size)]


def col_terms(value, size):
    if size & (size - 1) or size < 4:
        return gather_terms(value, "col", size)
    both = plus(value, swap(value, "col", size, 1))
    return gather_terms(both, "col", size, range(2, size, 2))


def plus(*terms):
    def body(*refs):
        refs[-1][...] = add_all([ref[...] for ref in refs[:-1]])

    return pl.pallas_call(
        body, in_specs=[resident()] * len(terms), out_specs=resident(),
        out_shape=jax.ShapeDtypeStruct(terms[0].shape, F32),
        compiler_params=pltpu.CompilerParams(vmem_limit_bytes=2 * 2**20), name="plus")(*terms)


def join(terms, lower, first):
    lines = terms[0].shape[0]

    def body(*refs):
        total = add_all([ref[...] for ref in refs[:-3]])
        refs[-2][...] = total[:first]
        refs[-1][0:lines - first, :] = total[first:]
        refs[-1][lines - first:, :] = refs[-3][...]

    return pl.pallas_call(
        body, in_specs=[resident()] * (len(terms) + 1), out_specs=[resident()] * 2,
        out_shape=[line_shape(first), line_shape(lines - first + lower.shape[0])],
        compiler_params=pltpu.CompilerParams(vmem_limit_bytes=2 * 2**20), name="join")(*terms, lower)


def ends(z, depot_sum, row_terms, depot_push, hub_push, zone_push):
    dl, hl, zl = z.dep_lines, z.hub_lines, z.zone_lines

    def body(depot_in, depot_last, hub_last, zone_last, *refs):
        total = add_all([ref[...] for ref in refs[:-3]])
        refs[-3][...] = depot_last[2 * dl:, :] - STEP_PRIMAL * depot_in[...]
        refs[-2][...] = hub_last[2 * hl:, :] - STEP_PRIMAL * total[:hl]
        refs[-1][...] = zone_last[2 * zl:, :] + STEP_PRIMAL * total[hl:]

    return pl.pallas_call(
        body, in_specs=[resident()] * (len(row_terms) + 4), out_specs=[resident()] * 3,
        out_shape=[line_shape(dl), line_shape(hl), line_shape(zl)],
        compiler_params=pltpu.CompilerParams(vmem_limit_bytes=2 * 2**20), name="ends",
    )(depot_sum, depot_push, hub_push, zone_push, *row_terms)


def add_all(terms):
    total = terms[0]
    for term in terms[1:]:
        total = total + term
    return total


def as_rows(line):
    return jnp.broadcast_to(line, (LANES, LANES)).T


def as_line(block):
    return jnp.sum(block.T, axis=0, keepdims=True)


def fold(value):
    return jnp.sum(value.reshape(-1, 8, LANES), axis=0)


def fold_line(value):
    return jnp.sum(value, axis=0, keepdims=True)


def piece(ref, row, lane):
    return ref[pl.ds(row, SUB), pl.ds(lane, LANES)].astype(F32)


class Sizes:
    def __init__(self, dep_rows, hub_cols, hub_rows, zone_cols, hubs, deps):
        self.dep_rows, self.hub_cols, self.hub_rows, self.zone_cols = dep_rows, hub_cols, hub_rows, zone_cols
        self.hubs, self.deps = hubs, deps
        self.dep_lines, self.one_lines = dep_rows // LANES, hub_cols // LANES
        self.two_lines, self.zone_lines = hub_rows // LANES, zone_cols // LANES
        self.hub_lines = hubs // LANES
        self.steps = self.two_lines
        self.per = self.dep_lines // self.steps
        assert self.per * self.steps == self.dep_lines

    def one(self):
        return pl.BlockSpec((self.per * LANES, self.hub_cols), lambda i: (i, 0))

    def list_shapes(self):
        return [jax.ShapeDtypeStruct((self.steps, self.per * self.one_lines + 1), jnp.int32),
                jax.ShapeDtypeStruct((self.steps, self.zone_lines + 1), jnp.int32)]

    def two(self):
        return pl.BlockSpec((LANES, self.zone_cols), lambda i: (i, 0))


def whole(lines):
    return pl.BlockSpec((lines, LANES), lambda i: (0, 0))


def smem():
    return pl.BlockSpec(memory_space=pltpu.SMEM)


def line_shape(lines):
    return jax.ShapeDtypeStruct((lines, LANES), F32)


def params(mib):
    return pltpu.CompilerParams(dimension_semantics=("arbitrary",), vmem_limit_bytes=mib * 2**20)


def resident():
    return pl.BlockSpec(memory_space=pltpu.VMEM)


def pinned(*arrays):
    return [pltpu.with_memory_space_constraint(array, pltpu.HBM) for array in arrays]


def place():
    return lax.axis_index("row"), lax.axis_index("col")


def rows_of(ref, z, i):
    rows = ref.shape[0] // z.steps
    return ref.at[pl.ds(pl.multiple_of(i * rows, rows), rows), :]


def listed(values, out, line):
    n = jnp.int32(0)
    for j, value in enumerate(values):
        out[line, n + 1] = jnp.int32(j)
        n = n + value
    out[line, 0] = n


def walk(lists, line, body):
    n = lists[line, 0]

    def pair(p, carry):
        body([lists[line, 2 * p + 1], lists[line, 2 * p + 2]])
        return carry

    lax.fori_loop(0, lax.shift_right_logical(n, 1), pair, 0)

    @pl.when(lax.rem(n, 2) == 1)
    def _():
        body([lists[line, n]])


def lane_of(j):
    return pl.multiple_of(j * LANES, LANES)


def scaled(ref, row, lane, scale):
    return (ref[pl.ds(row, SUB), pl.ds(lane, LANES)] * jnp.asarray(scale, BF16)).astype(F32)


def fetched(z, i, arrays, bufs, sems, start=None):
    rows = [array.shape[0] // z.steps for array in arrays]

    def copy(x, step):
        at = pl.ds(pl.multiple_of(step * rows[x], rows[x]), rows[x])
        return pltpu.make_async_copy(arrays[x].at[at, :], bufs[x].at[at, :], sems.at[x, step])

    if start is not None:
        @pl.when(i == 0)
        def _():
            for step in start:
                for x in range(len(arrays)):
                    copy(x, step).start()
        return None
    for x in range(len(arrays)):
        copy(x, i).wait()
    return [buf.at[pl.ds(pl.multiple_of(i * n, n), n), :] for buf, n in zip(bufs, rows)]


def buffers(z, *arrays):
    return [pltpu.VMEM(array.shape, array.dtype) for array in arrays] + [
        pltpu.SemaphoreType.DMA((len(arrays), z.steps))]


def left():
    return pl.BlockSpec(memory_space=pltpu.HBM)


def clear(*refs):
    for ref in refs:
        ref[...] = jnp.zeros_like(ref)


def split_of(z, e):
    return lax.div(e, z.one_lines), lax.rem(e, z.one_lines)


def first_kernel(z, mask_one, mask_two, depot, hub, zone, cap, th1, co1, th2, co2,
                 a_one, a_two, col_out, zone_out, depot_pre, zone_pre, list_one, list_two,
                 row1, row0, both1, both0, shift_one, shift, keep, ksum, keeps, hub_acc, zone1, zone0, hub_two, *bufs):
    i, where = pl.program_id(0), place()
    smalls, bufs = bufs[:5], bufs[5:]
    off_one, off_two = where[1] * z.one_lines, where[0] * z.two_lines
    arrays = (th1, co1, th2, co2)
    small = [pltpu.make_async_copy(a, b, smalls[-1].at[x])
             for x, (a, b) in enumerate(zip((depot, hub, zone, cap), smalls[:-1]))]
    depot, hub, zone, cap = smalls[:-1]

    @pl.when(i == 0)
    def _():
        for copy in small:
            copy.start()
        clear(hub_acc, zone1, zone0)

    fetched(z, i, arrays, bufs[:-1], bufs[-1], range(1))

    @pl.when(i == 0)
    def _():
        for copy in small:
            copy.wait()

    fetched(z, i, arrays, bufs[:-1], bufs[-1], range(1, z.steps))
    a_one, a_two = rows_of(a_one, z, i), rows_of(a_two, z, i)
    clear(row1, row0, both1, both0, keeps)
    for k in range(z.per):
        shift_one[pl.ds(k * LANES, LANES), :] = as_rows(0.25 * depot[pl.ds(i * z.per + k, 1), :])
    shift[...] = as_rows(0.25 * hub[pl.ds(off_two + i, 1), :])
    keep[...] = as_rows(0.25 * cap[pl.ds(off_two + i, 1), :].astype(F32))
    ksum[...] = 0.5 * fold(keep[...])
    listed([mask_one[i * z.per + k, j] for k in range(z.per) for j in range(z.one_lines)], list_one, i)
    listed([mask_two[i, j] for j in range(z.zone_lines)], list_two, i)

    def tiles_one(entries):
        for x, e in enumerate(entries):
            k, j = split_of(z, e)
            lane, base = lane_of(j), lane_of(k)
            hrow = 0.25 * hub[pl.ds(off_one + j, 1), :]
            km = cap[pl.ds(off_one + j, 1), :].astype(F32)
            total = 0.5 * LANES / 8 * jnp.broadcast_to(km, (8, LANES))
            keeps[x, pl.ds(k, 1), :] += km
            for s in range(0, LANES, SUB):
                at = pl.multiple_of(base + s, SUB)
                half = scaled(th1, at, lane, 0.5)
                t0 = jnp.tanh(half)
                t1 = jnp.tanh((half - scaled(co1, at, lane, 0.25)) - (shift_one[pl.ds(at, SUB), :] + hrow))
                k1, k0 = km * t1, km * t0
                row1[x, pl.ds(at, SUB), :] += k1
                row0[x, pl.ds(at, SUB), :] += k0
                total = total + (fold(k1) - 0.5 * fold(k0))
                a_one[pl.ds(at, SUB), pl.ds(lane, LANES)] = (km - k1 * t1).astype(BF16)
            hub_acc[x, :, pl.ds(lane, LANES)] += total

    def tiles_two(js):
        zrows = [0.25 * zone[pl.ds(j, 1), :] for j in js]
        sum1 = [jnp.zeros((8, LANES), F32) for j in js]
        sum0 = [jnp.zeros((8, LANES), F32) for j in js]
        for s in range(0, LANES, SUB):
            hcol, km = shift[s:s + SUB, :], keep[s:s + SUB, :]
            all1, all0 = [], []
            for x, j in enumerate(js):
                lane = lane_of(j)
                half = scaled(th2, s, lane, 0.5)
                t0 = jnp.tanh(half)
                t1 = jnp.tanh((half - scaled(co2, s, lane, 0.25)) + (hcol + zrows[x]))
                k1, k0 = km * t1, km * t0
                all1.append(k1)
                all0.append(k0)
                sum1[x] = sum1[x] + fold(k1)
                sum0[x] = sum0[x] + fold(k0)
                a_two[pl.ds(s, SUB), pl.ds(lane, LANES)] = (km - k1 * t1).astype(BF16)
            both1[s:s + SUB, :] += add_all(all1)
            both0[s:s + SUB, :] += add_all(all0)
        for x, j in enumerate(js):
            zone1[x, :, pl.ds(lane_of(j), LANES)] += sum1[x] - 2.0 * ksum[...]
            zone0[x, :, pl.ds(lane_of(j), LANES)] += sum0[x] - 6.0 * ksum[...]

    th1, co1, th2, co2 = fetched(z, i, arrays, bufs[:-1], bufs[-1])
    walk(list_one, i, tiles_one)
    walk(list_two, i, tiles_two)
    for k in range(z.per):
        line, at = i * z.per + k, pl.ds(k * LANES, LANES)
        line1, line0 = as_line(row1[0, at, :] + row1[1, at, :]), as_line(row0[0, at, :] + row0[1, at, :])
        half = 0.5 * jnp.sum(keeps[0, k:k + 1, :] + keeps[1, k:k + 1, :])
        col_out[pl.ds(line, 1), :] = half + line1 - 0.5 * line0
        depot_pre[pl.ds(line, 1), :] = half - 0.5 * line1
    opened = list_two[i, 0].astype(F32)
    hub_two[pl.ds(i, 1), :] = as_line(both1[...] - 0.5 * both0[...] + (0.5 * opened) * keep[...])

    @pl.when(i == z.steps - 1)
    def _():
        for j in range(z.zone_lines):
            at = slice(j * LANES, (j + 1) * LANES)
            line1, line0 = fold_line(zone1[0, :, at] + zone1[1, :, at]), fold_line(zone0[0, :, at] + zone0[1, :, at])
            zone_out[j:j + 1, :] = line1 - 0.5 * line0
            zone_pre[j:j + 1, :] = -0.5 * line1
        put_hub(z, where, col_out, z.dep_lines, hub_acc, hub_two)


def hub_line(hub_acc, j):
    at = slice(j * LANES, (j + 1) * LANES)
    return fold_line(hub_acc[0, :, at] + hub_acc[1, :, at])


def put_hub(z, where, out, base, hub_acc, hub_two):
    out[base:base + z.hub_lines, :] = jnp.zeros((z.hub_lines, LANES), F32)
    for j in range(z.two_lines):
        out[pl.ds(base + where[0] * z.two_lines + j, 1), :] = -hub_two[j:j + 1, :]
    for j in range(z.one_lines):
        at = base + where[1] * z.one_lines + j
        out[pl.ds(at, 1), :] = out[pl.ds(at, 1), :] + hub_line(hub_acc, j)


def first_pass(z, mask_one, mask_two, depot, hub, zone, cap, th1, co1, th2, co2):
    return pl.pallas_call(
        functools.partial(first_kernel, z),
        grid=(z.steps,),
        in_specs=[smem(), smem()] + [left()] * 8,
        out_specs=[resident(), resident(), whole(z.dep_lines + z.hub_lines), whole(z.zone_lines),
                   whole(z.dep_lines), whole(z.zone_lines), smem(), smem()],
        out_shape=[pltpu.VMEM(th1.shape, BF16), pltpu.VMEM(th2.shape, BF16),
                   line_shape(z.dep_lines + z.hub_lines), line_shape(z.zone_lines),
                   line_shape(z.dep_lines), line_shape(z.zone_lines)] + z.list_shapes(),
        scratch_shapes=[pltpu.VMEM((2, z.per * LANES, LANES), F32)] * 2 + [pltpu.VMEM((LANES, LANES), F32)] * 2
                       + [pltpu.VMEM((z.per * LANES, LANES), F32)] + [pltpu.VMEM((LANES, LANES), F32)] * 2
                       + [pltpu.VMEM((8, LANES), F32), pltpu.VMEM((2, z.per, LANES), F32), pltpu.VMEM((2, 8, z.hub_cols), F32)]
                       + [pltpu.VMEM((2, 8, z.zone_cols), F32)] * 2 + [pltpu.VMEM((z.two_lines, LANES), F32)]
                       + [pltpu.VMEM(v.shape, v.dtype) for v in (depot, hub, zone, cap)]
                       + [pltpu.SemaphoreType.DMA((4,))] + buffers(z, th1, co1, th2, co2),
        compiler_params=params(28), name="first_pass",
    )(mask_one, mask_two, *pinned(depot, hub, zone, cap, th1, co1, th2, co2))


def second_kernel(z, terms, list_one, list_two, depot, hub, zone, cap, supply, demand, cot_hub,
                  depot_pre, zone_pre, depot_sum, *rest):
    sums, rest = rest[:terms], rest[terms:]
    (th1, co1, cf1, th2, co2, cf2,
     a_one, a_two, depot_out, zone_out, depot_state, zone_state, hub_state, hub_one_out, hub_two_out,
     rowk, rowa, rowe, both, shift_one, shift, keep, pushes, hub_acc, zonek, zonea, zonee,
     shift_d, shift_h, shift_z, *bufs) = rest
    arrays = (th1, co1, cf1, th2, co2, cf2)
    i, where = pl.program_id(0), place()
    off_one, off_two = where[1] * z.one_lines, where[0] * z.two_lines
    dl, zl, hl = z.dep_lines, z.zone_lines, z.hub_lines

    fetched(z, i, arrays, bufs[:-1], bufs[-1], range(z.steps))

    a_one, a_two = rows_of(a_one, z, i), rows_of(a_two, z, i)

    @pl.when(i == 0)
    def _():
        clear(hub_acc, zonek, zonea, zonee)
        total = sums[0][...]
        for term in sums[1:]:
            total = total + term[...]
        grow_d = jnp.exp(STEP_DUAL * (depot_sum[...] / z.hubs - 0.5 * supply[...].astype(F32)))
        grow_z = jnp.exp(STEP_DUAL * (0.125 * demand[...].astype(F32) - total[hl:, :] / z.hubs))
        new_d, new_z = depot[...] * grow_d, zone[...] * grow_z
        new_h = hub[...] + HUB_RATE * total[:hl, :] / z.deps
        depot_state[0:dl, :] = new_d
        depot_state[dl:2 * dl, :] = grow_d
        zone_state[0:zl, :] = new_z
        zone_state[zl:2 * zl, :] = grow_z
        hub_state[...] = new_h
        shift_d[...] = 0.25 * (depot[...] + new_d)
        shift_h[...] = 0.25 * (hub[...] + new_h)
        shift_z[...] = 0.25 * (zone[...] + new_z)

    push = 2.0 * HUB_RATE / z.deps
    clear(rowk, rowa, rowe, both)
    for k in range(z.per):
        shift_one[pl.ds(k * LANES, LANES), :] = as_rows(shift_d[pl.ds(i * z.per + k, 1), :])
    shift[...] = as_rows(shift_h[pl.ds(off_two + i, 1), :])
    pushes[...] = as_rows(push * cot_hub[pl.ds(off_two + i, 1), :])
    keep[...] = as_rows(0.25 * cap[pl.ds(off_two + i, 1), :].astype(F32))

    def tiles_one(entries):
        for x, e in enumerate(entries):
            k, j = split_of(z, e)
            lane, base = lane_of(j), lane_of(k)
            hrow = shift_h[pl.ds(off_one + j, 1), :]
            prow = push * cot_hub[pl.ds(off_one + j, 1), :]
            km = cap[pl.ds(off_one + j, 1), :].astype(F32)
            total = jnp.zeros((8, LANES), F32)
            for s in range(0, LANES, SUB):
                at = pl.multiple_of(base + s, SUB)
                t2 = jnp.tanh((scaled(th1, at, lane, 0.5) - scaled(co1, at, lane, 0.5))
                              - (shift_one[pl.ds(at, SUB), :] + hrow))
                k2 = km * t2
                a2 = km - k2 * t2
                e = (piece(cf1, at, lane) + prow) * a2
                rowk[x, pl.ds(at, SUB), :] += k2
                rowa[x, pl.ds(at, SUB), :] += a2
                rowe[x, pl.ds(at, SUB), :] += e
                total = total + fold(e)
                a_one[pl.ds(at, SUB), pl.ds(lane, LANES)] = a2.astype(BF16)
            hub_acc[x, :, pl.ds(lane, LANES)] += total

    def tiles_two(js):
        zrows = [shift_z[pl.ds(j, 1), :] for j in js]
        sumk, suma, sume = ([jnp.zeros((8, LANES), F32) for j in js] for _ in range(3))
        for s in range(0, LANES, SUB):
            hcol, km, pcol = shift[s:s + SUB, :], keep[s:s + SUB, :], pushes[s:s + SUB, :]
            alle = []
            for x, j in enumerate(js):
                lane = lane_of(j)
                t2 = jnp.tanh((scaled(th2, s, lane, 0.5) - scaled(co2, s, lane, 0.5)) + (hcol + zrows[x]))
                k2 = km * t2
                a2 = km - k2 * t2
                e = (piece(cf2, s, lane) - pcol) * a2
                alle.append(e)
                sumk[x] = sumk[x] + fold(k2)
                suma[x] = suma[x] + fold(a2)
                sume[x] = sume[x] + fold(e)
                a_two[pl.ds(s, SUB), pl.ds(lane, LANES)] = a2.astype(BF16)
            both[s:s + SUB, :] += add_all(alle)
        for x, j in enumerate(js):
            zonek[x, :, pl.ds(lane_of(j), LANES)] += sumk[x]
            zonea[x, :, pl.ds(lane_of(j), LANES)] += suma[x]
            zonee[x, :, pl.ds(lane_of(j), LANES)] += sume[x]

    th1, co1, cf1, th2, co2, cf2 = fetched(z, i, arrays, bufs[:-1], bufs[-1])
    walk(list_one, i, tiles_one)
    walk(list_two, i, tiles_two)
    for k in range(z.per):
        line, at = i * z.per + k, pl.ds(k * LANES, LANES)
        depot_out[pl.ds(line, 1), :] = depot_pre[pl.ds(line, 1), :] + as_line(rowk[0, at, :] + rowk[1, at, :])
        depot_out[pl.ds(dl + line, 1), :] = as_line(rowa[0, at, :] + rowa[1, at, :])
        depot_out[pl.ds(2 * dl + line, 1), :] = as_line(rowe[0, at, :] + rowe[1, at, :])
    hub_two_out[pl.ds(i, 1), :] = as_line(both[...])

    @pl.when(i == z.steps - 1)
    def _():
        for j in range(zl):
            at = slice(j * LANES, (j + 1) * LANES)
            zone_out[j:j + 1, :] = zone_pre[j:j + 1, :] + fold_line(zonek[0, :, at] + zonek[1, :, at])
            zone_out[zl + j:zl + j + 1, :] = fold_line(zonea[0, :, at] + zonea[1, :, at])
            zone_out[2 * zl + j:2 * zl + j + 1, :] = fold_line(zonee[0, :, at] + zonee[1, :, at])
        for j in range(z.one_lines):
            hub_one_out[j:j + 1, :] = hub_line(hub_acc, j)


def second_pass(z, list_one, list_two, depot, hub, zone, cap, supply, demand, cot_hub,
                depot_pre, zone_pre, depot_sum, sums, th1, co1, cf1, th2, co2, cf2):
    dl, zl, hl = z.dep_lines, z.zone_lines, z.hub_lines
    return pl.pallas_call(
        functools.partial(second_kernel, z, len(sums)),
        grid=(z.steps,),
        in_specs=[smem(), smem(), whole(dl), whole(hl), whole(zl), whole(hl), whole(dl), whole(zl), whole(hl),
                  whole(dl), whole(zl), whole(dl)] + [whole(hl + zl)] * len(sums)
                 + [left()] * 6,
        out_specs=[resident(), resident(), whole(3 * dl), whole(3 * zl), whole(2 * dl), whole(2 * zl), whole(hl),
                   whole(z.one_lines), whole(z.two_lines)],
        out_shape=[pltpu.VMEM(th1.shape, BF16), pltpu.VMEM(th2.shape, BF16),
                   line_shape(3 * dl), line_shape(3 * zl), line_shape(2 * dl), line_shape(2 * zl), line_shape(hl),
                   line_shape(z.one_lines), line_shape(z.two_lines)],
        scratch_shapes=[pltpu.VMEM((2, z.per * LANES, LANES), F32)] * 3 + [pltpu.VMEM((LANES, LANES), F32)]
                       + [pltpu.VMEM((z.per * LANES, LANES), F32)] + [pltpu.VMEM((LANES, LANES), F32)] * 3
                       + [pltpu.VMEM((2, 8, z.hub_cols), F32)] + [pltpu.VMEM((2, 8, z.zone_cols), F32)] * 3
                       + [pltpu.VMEM((dl, LANES), F32), pltpu.VMEM((hl, LANES), F32), pltpu.VMEM((zl, LANES), F32)]
                       + buffers(z, th1, co1, cf1, th2, co2, cf2),
        compiler_params=params(38), name="second_pass",
    )(list_one, list_two, depot, hub, zone, cap, supply, demand, cot_hub, depot_pre, zone_pre, depot_sum,
      *sums, *pinned(th1, co1, cf1, th2, co2, cf2))


def third_kernel(z, d_terms, z_terms, list_one, list_two, supply, demand, cot_depot, cot_zone, depot_state, zone_state,
                 hub_one_in, hub_two_in, *rest):
    d_sums, rest = rest[:d_terms], rest[d_terms:]
    z_sums, rest = rest[:z_terms], rest[z_terms:]
    a_one, a_two, depot_out, zone_out, hub_out, row, shift_one, hub_acc, hub_two = rest
    i, where = pl.program_id(0), place()
    dl, zl = z.dep_lines, z.zone_lines
    rate = STEP_DUAL / z.hubs

    a_one, a_two = rows_of(a_one, z, i), rows_of(a_two, z, i)

    @pl.when(i == 0)
    def _():
        hub_acc[...] = jnp.zeros_like(hub_acc)
        total = d_sums[0][...]
        for term in d_sums[1:]:
            total = total + term[...]
        grow = jnp.exp(STEP_DUAL * (total[0:dl, :] / z.hubs - 0.5 * supply[...].astype(F32)))
        first, first_grow = depot_state[0:dl, :], depot_state[dl:2 * dl, :]
        push = cot_depot[...] * (first * grow) * rate
        reached = 0.25 * (total[2 * dl:3 * dl, :] + 2.0 * push * total[dl:2 * dl, :])
        adj = cot_depot[...] * grow - STEP_PRIMAL * reached
        depot_out[0:dl, :] = push
        depot_out[dl:2 * dl, :] = adj * first * rate
        depot_out[2 * dl:3 * dl, :] = adj * first_grow - STEP_PRIMAL * reached
        total = z_sums[0][...]
        for term in z_sums[1:]:
            total = total + term[...]
        grow = jnp.exp(STEP_DUAL * (0.125 * demand[...].astype(F32) - total[0:zl, :] / z.hubs))
        first, first_grow = zone_state[0:zl, :], zone_state[zl:2 * zl, :]
        push = -(cot_zone[...] * (first * grow) * rate)
        reached = 0.25 * (total[2 * zl:3 * zl, :] + 2.0 * push * total[zl:2 * zl, :])
        adj = cot_zone[...] * grow + STEP_PRIMAL * reached
        zone_out[0:zl, :] = push
        zone_out[zl:2 * zl, :] = -(adj * first * rate)
        zone_out[2 * zl:3 * zl, :] = adj * first_grow + STEP_PRIMAL * reached

    clear(row)
    for k in range(z.per):
        shift_one[pl.ds(k * LANES, LANES), :] = as_rows(depot_out[pl.ds(i * z.per + k, 1), :])

    def tiles_one(entries):
        for x, e in enumerate(entries):
            k, j = split_of(z, e)
            lane, base = lane_of(j), lane_of(k)
            total = jnp.zeros((8, LANES), F32)
            for s in range(0, LANES, SUB):
                at = pl.multiple_of(base + s, SUB)
                total = total + fold(piece(a_one, at, lane) * shift_one[pl.ds(at, SUB), :])
            hub_acc[x, :, pl.ds(lane, LANES)] += total

    def tiles_two(js):
        zrows = [zone_out[pl.ds(j, 1), :] for j in js]
        for s in range(0, LANES, SUB):
            row[s:s + SUB, :] += add_all([piece(a_two, s, lane_of(j)) * zrows[x] for x, j in enumerate(js)])

    walk(list_one, i, tiles_one)
    walk(list_two, i, tiles_two)
    hub_two[pl.ds(i, 1), :] = -0.25 * (hub_two_in[pl.ds(i, 1), :] + 2.0 * as_line(row[...]))

    @pl.when(i == z.steps - 1)
    def _():
        hub_out[...] = jnp.zeros_like(hub_out)
        for j in range(z.two_lines):
            hub_out[pl.ds(where[0] * z.two_lines + j, 1), :] = -hub_two[j:j + 1, :]
        for j in range(z.one_lines):
            at = where[1] * z.one_lines + j
            line = hub_line(hub_acc, j)
            hub_out[pl.ds(at, 1), :] = hub_out[pl.ds(at, 1), :] - 0.25 * (hub_one_in[j:j + 1, :] + 2.0 * line)


def third_pass(z, list_one, list_two, supply, demand, cot_depot, cot_zone, depot_state, zone_state, hub_one, hub_two,
               d_sums, z_sums, a_one, a_two):
    dl, zl, hl = z.dep_lines, z.zone_lines, z.hub_lines
    return pl.pallas_call(
        functools.partial(third_kernel, z, len(d_sums), len(z_sums)),
        grid=(z.steps,),
        in_specs=[smem(), smem(), whole(dl), whole(zl), whole(dl), whole(zl), whole(2 * dl), whole(2 * zl),
                  whole(z.one_lines), whole(z.two_lines)]
                 + [whole(3 * dl)] * len(d_sums) + [whole(3 * zl)] * len(z_sums) + [resident(), resident()],
        out_specs=[whole(3 * dl), whole(3 * zl), whole(hl)],
        out_shape=[line_shape(3 * dl), line_shape(3 * zl), line_shape(hl)],
        scratch_shapes=[pltpu.VMEM((LANES, LANES), F32), pltpu.VMEM((z.per * LANES, LANES), F32),
                        pltpu.VMEM((2, 8, z.hub_cols), F32), pltpu.VMEM((z.two_lines, LANES), F32)],
        compiler_params=params(6), name="third_pass",
    )(list_one, list_two, supply, demand, cot_depot, cot_zone, depot_state, zone_state, hub_one, hub_two,
      *d_sums, *z_sums, a_one, a_two)


def fourth_kernel(z, terms, list_one, list_two, cot_hub, depot_push, zone_push, *rest):
    sums, rest = rest[:terms], rest[terms:]
    (a_one, a_two, hub_out, col_out, zone_out, row, both, shift_one, shift, hub_acc, zone_acc, hub_two, mix) = rest
    i, where = pl.program_id(0), place()
    off_one, off_two = where[1] * z.one_lines, where[0] * z.two_lines
    dl, zl, hl = z.dep_lines, z.zone_lines, z.hub_lines
    rate = HUB_RATE / z.deps

    a_one, a_two = rows_of(a_one, z, i), rows_of(a_two, z, i)

    @pl.when(i == 0)
    def _():
        hub_acc[...] = jnp.zeros_like(hub_acc)
        zone_acc[...] = jnp.zeros_like(zone_acc)
        total = sums[0][...]
        for term in sums[1:]:
            total = total + term[...]
        adj = cot_hub[...] + STEP_PRIMAL * total
        late, early = cot_hub[...] * rate, adj * rate
        hub_out[0:hl, :] = late
        hub_out[hl:2 * hl, :] = early
        hub_out[2 * hl:3 * hl, :] = adj + STEP_PRIMAL * total
        mix[0:hl, :] = 0.25 * (2.0 * early - late)
        mix[hl:hl + dl, :] = 0.25 * (2.0 * depot_push[dl:2 * dl, :] - depot_push[0:dl, :])
        mix[hl + dl:, :] = 0.25 * (2.0 * zone_push[zl:2 * zl, :] - zone_push[0:zl, :])

    clear(row, both)
    for k in range(z.per):
        shift_one[pl.ds(k * LANES, LANES), :] = as_rows(mix[pl.ds(hl + i * z.per + k, 1), :])
    shift[...] = as_rows(mix[pl.ds(off_two + i, 1), :])

    def tiles_one(entries):
        for x, e in enumerate(entries):
            k, j = split_of(z, e)
            lane, base = lane_of(j), lane_of(k)
            hrow = mix[pl.ds(off_one + j, 1), :]
            total = jnp.zeros((8, LANES), F32)
            for s in range(0, LANES, SUB):
                at = pl.multiple_of(base + s, SUB)
                y = piece(a_one, at, lane) * (shift_one[pl.ds(at, SUB), :] + hrow)
                row[x, pl.ds(at, SUB), :] += y
                total = total + fold(y)
            hub_acc[x, :, pl.ds(lane, LANES)] += total

    def tiles_two(js):
        zrows = [mix[pl.ds(hl + dl + j, 1), :] for j in js]
        totals = [jnp.zeros((8, LANES), F32) for j in js]
        for s in range(0, LANES, SUB):
            ys = [piece(a_two, s, lane_of(j)) * (zrows[x] - shift[s:s + SUB, :]) for x, j in enumerate(js)]
            both[s:s + SUB, :] += add_all(ys)
            totals = [total + fold(y) for total, y in zip(totals, ys)]
        for x, j in enumerate(js):
            zone_acc[x, :, pl.ds(lane_of(j), LANES)] += totals[x]

    walk(list_one, i, tiles_one)
    walk(list_two, i, tiles_two)
    for k in range(z.per):
        at = pl.ds(k * LANES, LANES)
        col_out[pl.ds(i * z.per + k, 1), :] = as_line(row[0, at, :] + row[1, at, :])
    hub_two[pl.ds(i, 1), :] = as_line(both[...])

    @pl.when(i == z.steps - 1)
    def _():
        for j in range(zl):
            zone_out[j:j + 1, :] = hub_line(zone_acc, j)
        put_hub(z, where, col_out, dl, hub_acc, hub_two)


def fourth_pass(z, list_one, list_two, cot_hub, depot_push, zone_push, sums, a_one, a_two):
    dl, zl, hl = z.dep_lines, z.zone_lines, z.hub_lines
    return pl.pallas_call(
        functools.partial(fourth_kernel, z, len(sums)),
        grid=(z.steps,),
        in_specs=[smem(), smem(), whole(hl), whole(3 * dl), whole(3 * zl)] + [whole(hl)] * len(sums) + [resident(), resident()],
        out_specs=[whole(3 * hl), whole(dl + hl), whole(zl)],
        out_shape=[line_shape(3 * hl), line_shape(dl + hl), line_shape(zl)],
        scratch_shapes=[pltpu.VMEM((2, z.per * LANES, LANES), F32), pltpu.VMEM((LANES, LANES), F32),
                        pltpu.VMEM((z.per * LANES, LANES), F32), pltpu.VMEM((LANES, LANES), F32),
                        pltpu.VMEM((2, 8, z.hub_cols), F32), pltpu.VMEM((2, 8, z.zone_cols), F32),
                        pltpu.VMEM((z.two_lines, LANES), F32), pltpu.VMEM((hl + dl + zl, LANES), F32)],
        compiler_params=params(6), name="fourth_pass",
    )(list_one, list_two, cot_hub, depot_push, zone_push, *sums, a_one, a_two)


def result(half, quarter, cf, shift1, shift2, twice_late, mixed, early, km, minus):
    once = half - quarter
    t0 = jnp.tanh(half)
    t1 = jnp.tanh(once + shift1)
    t2 = jnp.tanh((once - quarter) + shift2)
    middle = mixed * (1.0 - t1 * t1)
    last = (cf + twice_late) * (1.0 - t2 * t2) + middle
    return km * (last + (middle - early * (1.0 - t0 * t0))), minus * last


def vectors(line, sign, now, after, push, lines):
    a, b = now[pl.ds(line, 1), :], after[pl.ds(line, 1), :]
    late, early = push[pl.ds(line, 1), :], push[pl.ds(lines + line, 1), :]
    return (0.25 * sign * a, 0.25 * sign * (a + b), 2.0 * late, early - 0.5 * late, early)


def wipe(ref, row, lane):
    ref[pl.ds(row, LANES), pl.ds(lane, LANES)] = jnp.zeros((LANES, LANES), F32)


def final_one_kernel(z, mask, lists, depot, hub, cap, depot_state, hub_state, depot_push, hub_push,
                     th, co, cf, theta_out, cost_out, token, cols, *bufs):
    arrays = (th, co, cf)
    i, where = pl.program_id(0), place()
    off = where[1] * z.one_lines
    fetched(z, i, arrays, bufs[:-1], bufs[-1], range(z.steps))
    token[...] = jnp.zeros_like(token)
    for k in range(z.per):
        for x, v in enumerate(vectors(i * z.per + k, -1.0, depot, depot_state, depot_push, z.dep_lines)):
            cols[x, pl.ds(k * LANES, LANES), :] = as_rows(v)
        for j in range(z.one_lines):
            @pl.when(mask[i * z.per + k, j] == 0)
            def _():
                wipe(theta_out, k * LANES, j * LANES)
                wipe(cost_out, k * LANES, j * LANES)

    def tiles(entries):
        for e in entries:
            k, j = split_of(z, e)
            lane, base = lane_of(j), lane_of(k)
            rows = vectors(off + j, -1.0, hub, hub_state, hub_push, z.hub_lines)
            km = 0.25 * cap[pl.ds(off + j, 1), :].astype(F32)
            for s in range(0, LANES, SUB):
                at = pl.multiple_of(base + s, SUB)
                both = [cols[x, pl.ds(at, SUB), :] + r for x, r in enumerate(rows)]
                theta, cost = result(scaled(th, at, lane, 0.5), scaled(co, at, lane, 0.25), piece(cf, at, lane),
                                     *both, km, -km)
                theta_out[pl.ds(at, SUB), pl.ds(lane, LANES)] = theta
                cost_out[pl.ds(at, SUB), pl.ds(lane, LANES)] = cost

    th, co, cf = fetched(z, i, arrays, bufs[:-1], bufs[-1])
    walk(lists, i, tiles)


def final_two_kernel(z, mask, lists, hub, zone, cap, hub_state, zone_state, hub_push, zone_push,
                     th, co, cf, theta_out, cost_out, cols, *bufs):
    arrays = (th, co, cf)
    i, where = pl.program_id(0), place()
    line = where[0] * z.two_lines + i
    fetched(z, i, arrays, bufs[:-1], bufs[-1], range(z.steps))
    hubs = vectors(line, 1.0, hub, hub_state, hub_push, z.hub_lines)
    km = 0.0625 * cap[pl.ds(line, 1), :].astype(F32)
    for x, v in enumerate((hubs[0], hubs[1], -hubs[2], -hubs[3], -hubs[4], km, -km)):
        cols[x] = as_rows(v)

    def closed(j, carry):
        @pl.when(mask[i, j] == 0)
        def _():
            wipe(theta_out, 0, lane_of(j))
            wipe(cost_out, 0, lane_of(j))
        return carry

    lax.fori_loop(0, z.zone_lines, closed, 0)

    def tiles(js):
        for j in js:
            lane = lane_of(j)
            rows = vectors(j, 1.0, zone, zone_state, zone_push, z.zone_lines)
            for s in range(0, LANES, SUB):
                both = [cols[x, s:s + SUB, :] + r for x, r in enumerate(rows)]
                theta, cost = result(scaled(th, s, lane, 0.5), scaled(co, s, lane, 0.25), piece(cf, s, lane),
                                     *both, cols[5, s:s + SUB, :], cols[6, s:s + SUB, :])
                theta_out[pl.ds(s, SUB), pl.ds(lane, LANES)] = theta
                cost_out[pl.ds(s, SUB), pl.ds(lane, LANES)] = cost

    th, co, cf = fetched(z, i, arrays, bufs[:-1], bufs[-1])
    walk(lists, i, tiles)


def final_one(z, mask, lists, depot, hub, cap, depot_state, hub_state, depot_push, hub_push, th, co, cf):
    dl, hl = z.dep_lines, z.hub_lines
    out = jax.ShapeDtypeStruct(th.shape, F32)
    return pl.pallas_call(
        functools.partial(final_one_kernel, z), grid=(z.steps,),
        in_specs=[smem(), smem(), whole(dl), whole(hl), whole(hl), whole(2 * dl), whole(hl), whole(3 * dl),
                  whole(3 * hl)] + [left()] * 3,
        out_specs=[z.one(), z.one(), whole(8)], out_shape=[out, out, line_shape(8)],
        scratch_shapes=[pltpu.VMEM((5, z.per * LANES, LANES), F32)] + buffers(z, th, co, cf),
        compiler_params=params(14), name="final_one",
    )(mask, lists, depot, hub, cap, depot_state, hub_state, depot_push, hub_push, *pinned(th, co, cf))


def final_two(z, mask, lists, hub, zone, cap, hub_state, zone_state, hub_push, zone_push, th, co, cf):
    zl, hl = z.zone_lines, z.hub_lines
    out = jax.ShapeDtypeStruct(th.shape, F32)
    return pl.pallas_call(
        functools.partial(final_two_kernel, z), grid=(z.steps,),
        in_specs=[smem(), smem(), whole(hl), whole(zl), whole(hl), whole(hl), whole(2 * zl), whole(3 * hl),
                  whole(3 * zl)] + [left()] * 3,
        out_specs=[z.two(), z.two()], out_shape=[out, out],
        scratch_shapes=[pltpu.VMEM((7, LANES, LANES), F32)] + buffers(z, th, co, cf),
        compiler_params=params(38), name="final_two",
    )(mask, lists, hub, zone, cap, hub_state, zone_state, hub_push, zone_push, *pinned(th, co, cf))


def on_device(rows, cols, theta_one, theta_two, cost_one, cost_two, depot_price, hub_price, zone_price,
              mask_one, mask_two, supply, demand, capacity, cot_flow_one, cot_flow_two,
              cot_depot, cot_hub, cot_zone):
    z = Sizes(*theta_one.shape, *theta_two.shape, hub_price.shape[0], theta_one.shape[0] * rows)
    dl, hl, zl = z.dep_lines, z.hub_lines, z.zone_lines
    lines = lambda v: v.reshape(-1, LANES)
    depot, hub, zone, cap = lines(depot_price), lines(hub_price), lines(zone_price), lines(capacity)
    supply, demand = lines(supply), lines(demand)
    cot_depot, cot_hub, cot_zone = lines(cot_depot), lines(cot_hub), lines(cot_zone)

    a1_one, a1_two, col_vec, zone_vec, depot_pre, zone_pre, list_one, list_two = first_pass(
        z, mask_one, mask_two, depot, hub, zone, cap, theta_one, cost_one, theta_two, cost_two)
    depot_sum, row_vec = join(col_terms(col_vec, cols), zone_vec, dl)
    sums = gather_terms(row_vec, "row", rows)
    (a2_one, a2_two, depot_vec, zone_vec, depot_state, zone_state, hub_state, hub_one, hub_two) = second_pass(
        z, list_one, list_two, depot, hub, zone, cap, supply, demand, cot_hub, depot_pre, zone_pre,
        depot_sum, sums, theta_one, cost_one, cot_flow_one, theta_two, cost_two, cot_flow_two)
    d_sums = col_terms(depot_vec, cols)
    z_sums = gather_terms(zone_vec, "row", rows)
    depot_push, zone_push, hub_vec = third_pass(
        z, list_one, list_two, supply, demand, cot_depot, cot_zone, depot_state, zone_state, hub_one, hub_two,
        d_sums, z_sums, a2_one, a2_two)
    hub_sums = gather_terms(plus(*col_terms(hub_vec, cols)), "row", rows)
    hub_push, col_vec, zone_vec = fourth_pass(z, list_one, list_two, cot_hub, depot_push, zone_push, hub_sums,
                                              a1_one, a1_two)
    if cols >= 4 and cols & (cols - 1) == 0:
        col_vec = plus(col_vec, swap(col_vec, "col", cols, 1))
        distances = range(2, cols, 2)
    else:
        distances = range(1, cols)
    col_vec, push = lax.optimization_barrier((col_vec, hub_push))
    terms = gather_terms(col_vec, "col", cols, distances)
    grad_theta_one, grad_cost_one, token = final_one(
        z, mask_one, list_one, depot, hub, cap, depot_state, hub_state, depot_push, push,
        theta_one, cost_one, cot_flow_one)
    *terms, token = lax.optimization_barrier((*terms, token))
    depot_sum, row_vec = join(terms, zone_vec, dl)
    row_vec, push = lax.optimization_barrier((row_vec, hub_push))
    terms = gather_terms(row_vec, "row", rows)
    grad_theta_two, grad_cost_two = final_two(
        z, mask_two, list_two, hub, zone, cap, hub_state, zone_state, push, zone_push,
        theta_two, cost_two, cot_flow_two)
    grad_depot, grad_hub, grad_zone = ends(z, depot_sum, terms, depot_push, hub_push, zone_push)
    return (grad_theta_one, grad_theta_two, grad_cost_one, grad_cost_two,
            grad_depot.reshape(-1), grad_hub.reshape(-1), grad_zone.reshape(-1))


def solution(mesh):
    split, row, col, copied = P("row", "col"), P("row"), P("col"), P()
    return jax.shard_map(
        functools.partial(on_device, mesh.shape["row"], mesh.shape["col"]),
        mesh=mesh,
        in_specs=(split, split, split, split, row, copied, col, split, split, row, col, copied, split, split,
                  row, copied, col),
        out_specs=(split, split, split, split, row, copied, col),
        check_vma=False,
    )
```

```python
import functools

import jax
import jax.numpy as jnp
from jax import lax
from jax.experimental import pallas as pl
from jax.experimental.pallas import tpu as pltpu
from jax.sharding import PartitionSpec as P

STEP_PRIMAL = 0.5
STEP_DUAL = 0.5
HUB_RATE = 4.0
LANES = 128
SUB = 32
F32 = jnp.float32
BF16 = jnp.bfloat16


def swap(value, axis, size, distance):
    if size & (size - 1) == 0:
        pairs = [(i, i ^ distance) for i in range(size)]
    else:
        pairs = [(i, (i + distance) % size) for i in range(size)]
    return lax.ppermute(value, axis, pairs)


def gather_terms(value, axis, size, distances=None):
    return [value] + [swap(value, axis, size, k) for k in distances or range(1, size)]


def col_terms(value, size):
    if size & (size - 1) or size < 4:
        return gather_terms(value, "col", size)
    both = plus(value, swap(value, "col", size, 1))
    return gather_terms(both, "col", size, range(2, size, 2))


def plus(*terms):
    def body(*refs):
        refs[-1][...] = add_all([ref[...] for ref in refs[:-1]])

    return pl.pallas_call(
        body, in_specs=[resident()] * len(terms), out_specs=resident(),
        out_shape=jax.ShapeDtypeStruct(terms[0].shape, F32),
        compiler_params=pltpu.CompilerParams(vmem_limit_bytes=2 * 2**20), name="plus")(*terms)


def join(terms, lower, first, after=()):
    lines = terms[0].shape[0]

    def body(*refs):
        refs = refs[len(after):]
        total = add_all([ref[...] for ref in refs[:-3]])
        refs[-2][...] = total[:first]
        refs[-1][0:lines - first, :] = total[first:]
        refs[-1][lines - first:, :] = refs[-3][...]

    return pl.pallas_call(
        body, in_specs=[resident()] * (len(after) + len(terms) + 1), out_specs=[resident()] * 2,
        out_shape=[line_shape(first), line_shape(lines - first + lower.shape[0])],
        compiler_params=pltpu.CompilerParams(vmem_limit_bytes=2 * 2**20), name="join")(*after, *terms, lower)


def ends(z, depot_sum, row_terms, depot_push, hub_push, zone_push):
    dl, hl, zl = z.dep_lines, z.hub_lines, z.zone_lines

    def body(depot_in, depot_last, hub_last, zone_last, *refs):
        total = add_all([ref[...] for ref in refs[:-3]])
        refs[-3][...] = depot_last[2 * dl:, :] - STEP_PRIMAL * depot_in[...]
        refs[-2][...] = hub_last[2 * hl:, :] - STEP_PRIMAL * total[:hl]
        refs[-1][...] = zone_last[2 * zl:, :] + STEP_PRIMAL * total[hl:]

    return pl.pallas_call(
        body, in_specs=[resident()] * (len(row_terms) + 4), out_specs=[resident()] * 3,
        out_shape=[line_shape(dl), line_shape(hl), line_shape(zl)],
        compiler_params=pltpu.CompilerParams(vmem_limit_bytes=2 * 2**20), name="ends",
    )(depot_sum, depot_push, hub_push, zone_push, *row_terms)


def add_all(terms):
    total = terms[0]
    for term in terms[1:]:
        total = total + term
    return total


def as_rows(line):
    return jnp.broadcast_to(line, (LANES, LANES)).T


def as_line(block):
    return jnp.sum(block.T, axis=0, keepdims=True)


def fold(value):
    return jnp.sum(value.reshape(-1, 8, LANES), axis=0)


def fold_line(value):
    return jnp.sum(value, axis=0, keepdims=True)


def piece(ref, row, lane):
    return ref[pl.ds(row, SUB), pl.ds(lane, LANES)].astype(F32)


class Sizes:
    def __init__(self, dep_rows, hub_cols, hub_rows, zone_cols, hubs, deps):
        self.dep_rows, self.hub_cols, self.hub_rows, self.zone_cols = dep_rows, hub_cols, hub_rows, zone_cols
        self.hubs, self.deps = hubs, deps
        self.dep_lines, self.one_lines = dep_rows // LANES, hub_cols // LANES
        self.two_lines, self.zone_lines = hub_rows // LANES, zone_cols // LANES
        self.hub_lines = hubs // LANES
        self.steps = self.two_lines
        self.per = self.dep_lines // self.steps
        assert self.per * self.steps == self.dep_lines

    def one(self):
        return pl.BlockSpec((self.per * LANES, self.hub_cols), lambda i: (i, 0))

    def list_shapes(self):
        return [jax.ShapeDtypeStruct((self.steps, self.per * self.one_lines + 1), jnp.int32),
                jax.ShapeDtypeStruct((self.steps, self.zone_lines + 1), jnp.int32)]

    def two(self):
        return pl.BlockSpec((LANES, self.zone_cols), lambda i: (i, 0))


def whole(lines):
    return pl.BlockSpec((lines, LANES), lambda i: (0, 0))


def smem():
    return pl.BlockSpec(memory_space=pltpu.SMEM)


def line_shape(lines):
    return jax.ShapeDtypeStruct((lines, LANES), F32)


def params(mib):
    return pltpu.CompilerParams(dimension_semantics=("arbitrary",), vmem_limit_bytes=mib * 2**20)


def resident():
    return pl.BlockSpec(memory_space=pltpu.VMEM)


def pinned(*arrays):
    return [pltpu.with_memory_space_constraint(array, pltpu.HBM) for array in arrays]


def place():
    return lax.axis_index("row"), lax.axis_index("col")


def rows_of(ref, z, i):
    rows = ref.shape[0] // z.steps
    return ref.at[pl.ds(pl.multiple_of(i * rows, rows), rows), :]


def listed(values, out, line):
    n = jnp.int32(0)
    for j, value in enumerate(values):
        out[line, n + 1] = jnp.int32(j)
        n = n + value
    out[line, 0] = n


def walk(lists, line, body):
    n = lists[line, 0]

    def pair(p, carry):
        body([lists[line, 2 * p + 1], lists[line, 2 * p + 2]])
        return carry

    lax.fori_loop(0, lax.shift_right_logical(n, 1), pair, 0)

    @pl.when(lax.rem(n, 2) == 1)
    def _():
        body([lists[line, n]])


def lane_of(j):
    return pl.multiple_of(j * LANES, LANES)


def scaled(ref, row, lane, scale):
    return (ref[pl.ds(row, SUB), pl.ds(lane, LANES)] * jnp.asarray(scale, BF16)).astype(F32)


def fetched(z, i, arrays, bufs, sems, start=None):
    rows = [array.shape[0] // z.steps for array in arrays]

    def copy(x, step):
        at = pl.ds(pl.multiple_of(step * rows[x], rows[x]), rows[x])
        return pltpu.make_async_copy(arrays[x].at[at, :], bufs[x].at[at, :], sems.at[x, step])

    if start is not None:
        @pl.when(i == 0)
        def _():
            for step in start:
                for x in range(len(arrays)):
                    copy(x, step).start()
        return None
    for x in range(len(arrays)):
        copy(x, i).wait()
    return [buf.at[pl.ds(pl.multiple_of(i * n, n), n), :] for buf, n in zip(bufs, rows)]


def buffers(z, *arrays):
    return [pltpu.VMEM(array.shape, array.dtype) for array in arrays] + [
        pltpu.SemaphoreType.DMA((len(arrays), z.steps))]


def left():
    return pl.BlockSpec(memory_space=pltpu.HBM)


def clear(*refs):
    for ref in refs:
        ref[...] = jnp.zeros_like(ref)


def split_of(z, e):
    return lax.div(e, z.one_lines), lax.rem(e, z.one_lines)


def first_kernel(z, mask_one, mask_two, depot, hub, zone, cap, th1, co1, th2, co2,
                 a_one, a_two, col_out, zone_out, depot_pre, zone_pre, list_one, list_two,
                 row1, row0, both1, both0, shift_one, shift, keep, ksum, keeps, hub_acc, zone1, zone0, hub_two, *bufs):
    i, where = pl.program_id(0), place()
    smalls, bufs = bufs[:5], bufs[5:]
    off_one, off_two = where[1] * z.one_lines, where[0] * z.two_lines
    arrays = (th1, co1, th2, co2)
    small = [pltpu.make_async_copy(a, b, smalls[-1].at[x])
             for x, (a, b) in enumerate(zip((depot, hub, zone, cap), smalls[:-1]))]
    depot, hub, zone, cap = smalls[:-1]

    @pl.when(i == 0)
    def _():
        for copy in small:
            copy.start()
        clear(hub_acc, zone1, zone0)

    fetched(z, i, arrays, bufs[:-1], bufs[-1], range(1))

    @pl.when(i == 0)
    def _():
        for copy in small:
            copy.wait()

    fetched(z, i, arrays, bufs[:-1], bufs[-1], range(1, z.steps))
    a_one, a_two = rows_of(a_one, z, i), rows_of(a_two, z, i)
    clear(row1, row0, both1, both0, keeps)
    for k in range(z.per):
        shift_one[pl.ds(k * LANES, LANES), :] = as_rows(0.25 * depot[pl.ds(i * z.per + k, 1), :])
    shift[...] = as_rows(0.25 * hub[pl.ds(off_two + i, 1), :])
    keep[...] = as_rows(0.25 * cap[pl.ds(off_two + i, 1), :].astype(F32))
    ksum[...] = 0.5 * fold(keep[...])
    listed([mask_one[i * z.per + k, j] for k in range(z.per) for j in range(z.one_lines)], list_one, i)
    listed([mask_two[i, j] for j in range(z.zone_lines)], list_two, i)

    def tiles_one(entries):
        for x, e in enumerate(entries):
            k, j = split_of(z, e)
            lane, base = lane_of(j), lane_of(k)
            hrow = 0.25 * hub[pl.ds(off_one + j, 1), :]
            km = cap[pl.ds(off_one + j, 1), :].astype(F32)
            total = 0.5 * LANES / 8 * jnp.broadcast_to(km, (8, LANES))
            keeps[x, pl.ds(k, 1), :] += km
            for s in range(0, LANES, SUB):
                at = pl.multiple_of(base + s, SUB)
                half = scaled(th1, at, lane, 0.5)
                t0 = jnp.tanh(half)
                t1 = jnp.tanh((half - scaled(co1, at, lane, 0.25)) - (shift_one[pl.ds(at, SUB), :] + hrow))
                k1, k0 = km * t1, km * t0
                row1[x, pl.ds(at, SUB), :] += k1
                row0[x, pl.ds(at, SUB), :] += k0
                total = total + (fold(k1) - 0.5 * fold(k0))
                a_one[pl.ds(at, SUB), pl.ds(lane, LANES)] = (km - k1 * t1).astype(BF16)
            hub_acc[x, :, pl.ds(lane, LANES)] += total

    def tiles_two(js):
        zrows = [0.25 * zone[pl.ds(j, 1), :] for j in js]
        sum1 = [jnp.zeros((8, LANES), F32) for j in js]
        sum0 = [jnp.zeros((8, LANES), F32) for j in js]
        for s in range(0, LANES, SUB):
            hcol, km = shift[s:s + SUB, :], keep[s:s + SUB, :]
            all1, all0 = [], []
            for x, j in enumerate(js):
                lane = lane_of(j)
                half = scaled(th2, s, lane, 0.5)
                t0 = jnp.tanh(half)
                t1 = jnp.tanh((half - scaled(co2, s, lane, 0.25)) + (hcol + zrows[x]))
                k1, k0 = km * t1, km * t0
                all1.append(k1)
                all0.append(k0)
                sum1[x] = sum1[x] + fold(k1)
                sum0[x] = sum0[x] + fold(k0)
                a_two[pl.ds(s, SUB), pl.ds(lane, LANES)] = (km - k1 * t1).astype(BF16)
            both1[s:s + SUB, :] += add_all(all1)
            both0[s:s + SUB, :] += add_all(all0)
        for x, j in enumerate(js):
            zone1[x, :, pl.ds(lane_of(j), LANES)] += sum1[x] - 2.0 * ksum[...]
            zone0[x, :, pl.ds(lane_of(j), LANES)] += sum0[x] - 6.0 * ksum[...]

    th1, co1, th2, co2 = fetched(z, i, arrays, bufs[:-1], bufs[-1])
    walk(list_one, i, tiles_one)
    walk(list_two, i, tiles_two)
    for k in range(z.per):
        line, at = i * z.per + k, pl.ds(k * LANES, LANES)
        line1, line0 = as_line(row1[0, at, :] + row1[1, at, :]), as_line(row0[0, at, :] + row0[1, at, :])
        half = 0.5 * jnp.sum(keeps[0, k:k + 1, :] + keeps[1, k:k + 1, :])
        col_out[pl.ds(line, 1), :] = half + line1 - 0.5 * line0
        depot_pre[pl.ds(line, 1), :] = half - 0.5 * line1
    opened = list_two[i, 0].astype(F32)
    hub_two[pl.ds(i, 1), :] = as_line(both1[...] - 0.5 * both0[...] + (0.5 * opened) * keep[...])

    @pl.when(i == z.steps - 1)
    def _():
        for j in range(z.zone_lines):
            at = slice(j * LANES, (j + 1) * LANES)
            line1, line0 = fold_line(zone1[0, :, at] + zone1[1, :, at]), fold_line(zone0[0, :, at] + zone0[1, :, at])
            zone_out[j:j + 1, :] = line1 - 0.5 * line0
            zone_pre[j:j + 1, :] = -0.5 * line1
        put_hub(z, where, col_out, z.dep_lines, hub_acc, hub_two)


def hub_line(hub_acc, j):
    at = slice(j * LANES, (j + 1) * LANES)
    return fold_line(hub_acc[0, :, at] + hub_acc[1, :, at])


def put_hub(z, where, out, base, hub_acc, hub_two):
    out[base:base + z.hub_lines, :] = jnp.zeros((z.hub_lines, LANES), F32)
    for j in range(z.two_lines):
        out[pl.ds(base + where[0] * z.two_lines + j, 1), :] = -hub_two[j:j + 1, :]
    for j in range(z.one_lines):
        at = base + where[1] * z.one_lines + j
        out[pl.ds(at, 1), :] = out[pl.ds(at, 1), :] + hub_line(hub_acc, j)


def first_pass(z, mask_one, mask_two, depot, hub, zone, cap, th1, co1, th2, co2):
    return pl.pallas_call(
        functools.partial(first_kernel, z),
        grid=(z.steps,),
        in_specs=[smem(), smem()] + [left()] * 8,
        out_specs=[resident(), resident(), whole(z.dep_lines + z.hub_lines), whole(z.zone_lines),
                   whole(z.dep_lines), whole(z.zone_lines), smem(), smem()],
        out_shape=[pltpu.VMEM(th1.shape, BF16), pltpu.VMEM(th2.shape, BF16),
                   line_shape(z.dep_lines + z.hub_lines), line_shape(z.zone_lines),
                   line_shape(z.dep_lines), line_shape(z.zone_lines)] + z.list_shapes(),
        scratch_shapes=[pltpu.VMEM((2, z.per * LANES, LANES), F32)] * 2 + [pltpu.VMEM((LANES, LANES), F32)] * 2
                       + [pltpu.VMEM((z.per * LANES, LANES), F32)] + [pltpu.VMEM((LANES, LANES), F32)] * 2
                       + [pltpu.VMEM((8, LANES), F32), pltpu.VMEM((2, z.per, LANES), F32), pltpu.VMEM((2, 8, z.hub_cols), F32)]
                       + [pltpu.VMEM((2, 8, z.zone_cols), F32)] * 2 + [pltpu.VMEM((z.two_lines, LANES), F32)]
                       + [pltpu.VMEM(v.shape, v.dtype) for v in (depot, hub, zone, cap)]
                       + [pltpu.SemaphoreType.DMA((4,))] + buffers(z, th1, co1, th2, co2),
        compiler_params=params(28), name="first_pass",
    )(mask_one, mask_two, *pinned(depot, hub, zone, cap, th1, co1, th2, co2))


def second_kernel(z, terms, list_one, list_two, depot, hub, zone, cap, supply, demand, cot_hub,
                  depot_pre, zone_pre, depot_sum, *rest):
    sums, rest = rest[:terms], rest[terms:]
    (th1, co1, cf1, th2, co2, cf2,
     a_one, a_two, depot_out, zone_out, depot_state, zone_state, hub_state, hub_one_out, hub_two_out,
     rowk, rowa, rowe, both, shift_one, shift, keep, pushes, hub_acc, zonek, zonea, zonee,
     shift_d, shift_h, shift_z, *bufs) = rest
    arrays = (th1, co1, cf1, th2, co2, cf2)
    i, where = pl.program_id(0), place()
    off_one, off_two = where[1] * z.one_lines, where[0] * z.two_lines
    dl, zl, hl = z.dep_lines, z.zone_lines, z.hub_lines

    fetched(z, i, arrays, bufs[:-1], bufs[-1], range(z.steps))

    a_one, a_two = rows_of(a_one, z, i), rows_of(a_two, z, i)

    @pl.when(i == 0)
    def _():
        clear(hub_acc, zonek, zonea, zonee)
        total = sums[0][...]
        for term in sums[1:]:
            total = total + term[...]
        grow_d = jnp.exp(STEP_DUAL * (depot_sum[...] / z.hubs - 0.5 * supply[...].astype(F32)))
        grow_z = jnp.exp(STEP_DUAL * (0.125 * demand[...].astype(F32) - total[hl:, :] / z.hubs))
        new_d, new_z = depot[...] * grow_d, zone[...] * grow_z
        new_h = hub[...] + HUB_RATE * total[:hl, :] / z.deps
        depot_state[0:dl, :] = new_d
        depot_state[dl:2 * dl, :] = grow_d
        zone_state[0:zl, :] = new_z
        zone_state[zl:2 * zl, :] = grow_z
        hub_state[...] = new_h
        shift_d[...] = 0.25 * (depot[...] + new_d)
        shift_h[...] = 0.25 * (hub[...] + new_h)
        shift_z[...] = 0.25 * (zone[...] + new_z)

    push = 2.0 * HUB_RATE / z.deps
    clear(rowk, rowa, rowe, both)
    for k in range(z.per):
        shift_one[pl.ds(k * LANES, LANES), :] = as_rows(shift_d[pl.ds(i * z.per + k, 1), :])
    shift[...] = as_rows(shift_h[pl.ds(off_two + i, 1), :])
    pushes[...] = as_rows(push * cot_hub[pl.ds(off_two + i, 1), :])
    keep[...] = as_rows(0.25 * cap[pl.ds(off_two + i, 1), :].astype(F32))

    def tiles_one(entries):
        for x, e in enumerate(entries):
            k, j = split_of(z, e)
            lane, base = lane_of(j), lane_of(k)
            hrow = shift_h[pl.ds(off_one + j, 1), :]
            prow = push * cot_hub[pl.ds(off_one + j, 1), :]
            km = cap[pl.ds(off_one + j, 1), :].astype(F32)
            total = jnp.zeros((8, LANES), F32)
            for s in range(0, LANES, SUB):
                at = pl.multiple_of(base + s, SUB)
                t2 = jnp.tanh((scaled(th1, at, lane, 0.5) - scaled(co1, at, lane, 0.5))
                              - (shift_one[pl.ds(at, SUB), :] + hrow))
                k2 = km * t2
                a2 = km - k2 * t2
                e = (piece(cf1, at, lane) + prow) * a2
                rowk[x, pl.ds(at, SUB), :] += k2
                rowa[x, pl.ds(at, SUB), :] += a2
                rowe[x, pl.ds(at, SUB), :] += e
                total = total + fold(e)
                a_one[pl.ds(at, SUB), pl.ds(lane, LANES)] = a2.astype(BF16)
            hub_acc[x, :, pl.ds(lane, LANES)] += total

    def tiles_two(js):
        zrows = [shift_z[pl.ds(j, 1), :] for j in js]
        sumk, suma, sume = ([jnp.zeros((8, LANES), F32) for j in js] for _ in range(3))
        for s in range(0, LANES, SUB):
            hcol, km, pcol = shift[s:s + SUB, :], keep[s:s + SUB, :], pushes[s:s + SUB, :]
            alle = []
            for x, j in enumerate(js):
                lane = lane_of(j)
                t2 = jnp.tanh((scaled(th2, s, lane, 0.5) - scaled(co2, s, lane, 0.5)) + (hcol + zrows[x]))
                k2 = km * t2
                a2 = km - k2 * t2
                e = (piece(cf2, s, lane) - pcol) * a2
                alle.append(e)
                sumk[x] = sumk[x] + fold(k2)
                suma[x] = suma[x] + fold(a2)
                sume[x] = sume[x] + fold(e)
                a_two[pl.ds(s, SUB), pl.ds(lane, LANES)] = a2.astype(BF16)
            both[s:s + SUB, :] += add_all(alle)
        for x, j in enumerate(js):
            zonek[x, :, pl.ds(lane_of(j), LANES)] += sumk[x]
            zonea[x, :, pl.ds(lane_of(j), LANES)] += suma[x]
            zonee[x, :, pl.ds(lane_of(j), LANES)] += sume[x]

    th1, co1, cf1, th2, co2, cf2 = fetched(z, i, arrays, bufs[:-1], bufs[-1])
    walk(list_one, i, tiles_one)
    walk(list_two, i, tiles_two)
    for k in range(z.per):
        line, at = i * z.per + k, pl.ds(k * LANES, LANES)
        depot_out[pl.ds(line, 1), :] = depot_pre[pl.ds(line, 1), :] + as_line(rowk[0, at, :] + rowk[1, at, :])
        depot_out[pl.ds(dl + line, 1), :] = as_line(rowa[0, at, :] + rowa[1, at, :])
        depot_out[pl.ds(2 * dl + line, 1), :] = as_line(rowe[0, at, :] + rowe[1, at, :])
    hub_two_out[pl.ds(i, 1), :] = as_line(both[...])

    @pl.when(i == z.steps - 1)
    def _():
        for j in range(zl):
            at = slice(j * LANES, (j + 1) * LANES)
            zone_out[j:j + 1, :] = zone_pre[j:j + 1, :] + fold_line(zonek[0, :, at] + zonek[1, :, at])
            zone_out[zl + j:zl + j + 1, :] = fold_line(zonea[0, :, at] + zonea[1, :, at])
            zone_out[2 * zl + j:2 * zl + j + 1, :] = fold_line(zonee[0, :, at] + zonee[1, :, at])
        for j in range(z.one_lines):
            hub_one_out[j:j + 1, :] = hub_line(hub_acc, j)


def second_pass(z, list_one, list_two, depot, hub, zone, cap, supply, demand, cot_hub,
                depot_pre, zone_pre, depot_sum, sums, th1, co1, cf1, th2, co2, cf2):
    dl, zl, hl = z.dep_lines, z.zone_lines, z.hub_lines
    return pl.pallas_call(
        functools.partial(second_kernel, z, len(sums)),
        grid=(z.steps,),
        in_specs=[smem(), smem(), whole(dl), whole(hl), whole(zl), whole(hl), whole(dl), whole(zl), whole(hl),
                  whole(dl), whole(zl), whole(dl)] + [whole(hl + zl)] * len(sums)
                 + [left()] * 6,
        out_specs=[resident(), resident(), whole(3 * dl), whole(3 * zl), whole(2 * dl), whole(2 * zl), whole(hl),
                   whole(z.one_lines), whole(z.two_lines)],
        out_shape=[pltpu.VMEM(th1.shape, BF16), pltpu.VMEM(th2.shape, BF16),
                   line_shape(3 * dl), line_shape(3 * zl), line_shape(2 * dl), line_shape(2 * zl), line_shape(hl),
                   line_shape(z.one_lines), line_shape(z.two_lines)],
        scratch_shapes=[pltpu.VMEM((2, z.per * LANES, LANES), F32)] * 3 + [pltpu.VMEM((LANES, LANES), F32)]
                       + [pltpu.VMEM((z.per * LANES, LANES), F32)] + [pltpu.VMEM((LANES, LANES), F32)] * 3
                       + [pltpu.VMEM((2, 8, z.hub_cols), F32)] + [pltpu.VMEM((2, 8, z.zone_cols), F32)] * 3
                       + [pltpu.VMEM((dl, LANES), F32), pltpu.VMEM((hl, LANES), F32), pltpu.VMEM((zl, LANES), F32)]
                       + buffers(z, th1, co1, cf1, th2, co2, cf2),
        compiler_params=params(38), name="second_pass",
    )(list_one, list_two, depot, hub, zone, cap, supply, demand, cot_hub, depot_pre, zone_pre, depot_sum,
      *sums, *pinned(th1, co1, cf1, th2, co2, cf2))


def third_kernel(z, d_terms, z_terms, list_one, list_two, supply, demand, cot_depot, cot_zone, depot_state, zone_state,
                 hub_one_in, hub_two_in, *rest):
    d_sums, rest = rest[:d_terms], rest[d_terms:]
    z_sums, rest = rest[:z_terms], rest[z_terms:]
    a_one, a_two, depot_out, zone_out, hub_out, row, shift_one, hub_acc, hub_two = rest
    i, where = pl.program_id(0), place()
    dl, zl = z.dep_lines, z.zone_lines
    rate = STEP_DUAL / z.hubs

    a_one, a_two = rows_of(a_one, z, i), rows_of(a_two, z, i)

    @pl.when(i == 0)
    def _():
        hub_acc[...] = jnp.zeros_like(hub_acc)
        total = d_sums[0][...]
        for term in d_sums[1:]:
            total = total + term[...]
        grow = jnp.exp(STEP_DUAL * (total[0:dl, :] / z.hubs - 0.5 * supply[...].astype(F32)))
        first, first_grow = depot_state[0:dl, :], depot_state[dl:2 * dl, :]
        push = cot_depot[...] * (first * grow) * rate
        reached = 0.25 * (total[2 * dl:3 * dl, :] + 2.0 * push * total[dl:2 * dl, :])
        adj = cot_depot[...] * grow - STEP_PRIMAL * reached
        depot_out[0:dl, :] = push
        depot_out[dl:2 * dl, :] = adj * first * rate
        depot_out[2 * dl:3 * dl, :] = adj * first_grow - STEP_PRIMAL * reached
        total = z_sums[0][...]
        for term in z_sums[1:]:
            total = total + term[...]
        grow = jnp.exp(STEP_DUAL * (0.125 * demand[...].astype(F32) - total[0:zl, :] / z.hubs))
        first, first_grow = zone_state[0:zl, :], zone_state[zl:2 * zl, :]
        push = -(cot_zone[...] * (first * grow) * rate)
        reached = 0.25 * (total[2 * zl:3 * zl, :] + 2.0 * push * total[zl:2 * zl, :])
        adj = cot_zone[...] * grow + STEP_PRIMAL * reached
        zone_out[0:zl, :] = push
        zone_out[zl:2 * zl, :] = -(adj * first * rate)
        zone_out[2 * zl:3 * zl, :] = adj * first_grow + STEP_PRIMAL * reached

    clear(row)
    for k in range(z.per):
        shift_one[pl.ds(k * LANES, LANES), :] = as_rows(depot_out[pl.ds(i * z.per + k, 1), :])

    def tiles_one(entries):
        for x, e in enumerate(entries):
            k, j = split_of(z, e)
            lane, base = lane_of(j), lane_of(k)
            total = jnp.zeros((8, LANES), F32)
            for s in range(0, LANES, SUB):
                at = pl.multiple_of(base + s, SUB)
                total = total + fold(piece(a_one, at, lane) * shift_one[pl.ds(at, SUB), :])
            hub_acc[x, :, pl.ds(lane, LANES)] += total

    def tiles_two(js):
        zrows = [zone_out[pl.ds(j, 1), :] for j in js]
        for s in range(0, LANES, SUB):
            row[s:s + SUB, :] += add_all([piece(a_two, s, lane_of(j)) * zrows[x] for x, j in enumerate(js)])

    walk(list_one, i, tiles_one)
    walk(list_two, i, tiles_two)
    hub_two[pl.ds(i, 1), :] = -0.25 * (hub_two_in[pl.ds(i, 1), :] + 2.0 * as_line(row[...]))

    @pl.when(i == z.steps - 1)
    def _():
        hub_out[...] = jnp.zeros_like(hub_out)
        for j in range(z.two_lines):
            hub_out[pl.ds(where[0] * z.two_lines + j, 1), :] = -hub_two[j:j + 1, :]
        for j in range(z.one_lines):
            at = where[1] * z.one_lines + j
            line = hub_line(hub_acc, j)
            hub_out[pl.ds(at, 1), :] = hub_out[pl.ds(at, 1), :] - 0.25 * (hub_one_in[j:j + 1, :] + 2.0 * line)


def third_pass(z, list_one, list_two, supply, demand, cot_depot, cot_zone, depot_state, zone_state, hub_one, hub_two,
               d_sums, z_sums, a_one, a_two):
    dl, zl, hl = z.dep_lines, z.zone_lines, z.hub_lines
    return pl.pallas_call(
        functools.partial(third_kernel, z, len(d_sums), len(z_sums)),
        grid=(z.steps,),
        in_specs=[smem(), smem(), whole(dl), whole(zl), whole(dl), whole(zl), whole(2 * dl), whole(2 * zl),
                  whole(z.one_lines), whole(z.two_lines)]
                 + [whole(3 * dl)] * len(d_sums) + [whole(3 * zl)] * len(z_sums) + [resident(), resident()],
        out_specs=[whole(3 * dl), whole(3 * zl), whole(hl)],
        out_shape=[line_shape(3 * dl), line_shape(3 * zl), line_shape(hl)],
        scratch_shapes=[pltpu.VMEM((LANES, LANES), F32), pltpu.VMEM((z.per * LANES, LANES), F32),
                        pltpu.VMEM((2, 8, z.hub_cols), F32), pltpu.VMEM((z.two_lines, LANES), F32)],
        compiler_params=params(6), name="third_pass",
    )(list_one, list_two, supply, demand, cot_depot, cot_zone, depot_state, zone_state, hub_one, hub_two,
      *d_sums, *z_sums, a_one, a_two)


def fourth_kernel(z, terms, list_one, list_two, cot_hub, depot_push, zone_push, *rest):
    sums, rest = rest[:terms], rest[terms:]
    (a_one, a_two, hub_out, col_out, zone_out, row, both, shift_one, shift, hub_acc, zone_acc, hub_two, mix) = rest
    i, where = pl.program_id(0), place()
    off_one, off_two = where[1] * z.one_lines, where[0] * z.two_lines
    dl, zl, hl = z.dep_lines, z.zone_lines, z.hub_lines
    rate = HUB_RATE / z.deps

    a_one, a_two = rows_of(a_one, z, i), rows_of(a_two, z, i)

    @pl.when(i == 0)
    def _():
        hub_acc[...] = jnp.zeros_like(hub_acc)
        zone_acc[...] = jnp.zeros_like(zone_acc)
        total = sums[0][...]
        for term in sums[1:]:
            total = total + term[...]
        adj = cot_hub[...] + STEP_PRIMAL * total
        late, early = cot_hub[...] * rate, adj * rate
        hub_out[0:hl, :] = late
        hub_out[hl:2 * hl, :] = early
        hub_out[2 * hl:3 * hl, :] = adj + STEP_PRIMAL * total
        mix[0:hl, :] = 0.25 * (2.0 * early - late)
        mix[hl:hl + dl, :] = 0.25 * (2.0 * depot_push[dl:2 * dl, :] - depot_push[0:dl, :])
        mix[hl + dl:, :] = 0.25 * (2.0 * zone_push[zl:2 * zl, :] - zone_push[0:zl, :])

    clear(row, both)
    for k in range(z.per):
        shift_one[pl.ds(k * LANES, LANES), :] = as_rows(mix[pl.ds(hl + i * z.per + k, 1), :])
    shift[...] = as_rows(mix[pl.ds(off_two + i, 1), :])

    def tiles_one(entries):
        for x, e in enumerate(entries):
            k, j = split_of(z, e)
            lane, base = lane_of(j), lane_of(k)
            hrow = mix[pl.ds(off_one + j, 1), :]
            total = jnp.zeros((8, LANES), F32)
            for s in range(0, LANES, SUB):
                at = pl.multiple_of(base + s, SUB)
                y = piece(a_one, at, lane) * (shift_one[pl.ds(at, SUB), :] + hrow)
                row[x, pl.ds(at, SUB), :] += y
                total = total + fold(y)
            hub_acc[x, :, pl.ds(lane, LANES)] += total

    def tiles_two(js):
        zrows = [mix[pl.ds(hl + dl + j, 1), :] for j in js]
        totals = [jnp.zeros((8, LANES), F32) for j in js]
        for s in range(0, LANES, SUB):
            ys = [piece(a_two, s, lane_of(j)) * (zrows[x] - shift[s:s + SUB, :]) for x, j in enumerate(js)]
            both[s:s + SUB, :] += add_all(ys)
            totals = [total + fold(y) for total, y in zip(totals, ys)]
        for x, j in enumerate(js):
            zone_acc[x, :, pl.ds(lane_of(j), LANES)] += totals[x]

    walk(list_one, i, tiles_one)
    walk(list_two, i, tiles_two)
    for k in range(z.per):
        at = pl.ds(k * LANES, LANES)
        col_out[pl.ds(i * z.per + k, 1), :] = as_line(row[0, at, :] + row[1, at, :])
    hub_two[pl.ds(i, 1), :] = as_line(both[...])

    @pl.when(i == z.steps - 1)
    def _():
        for j in range(zl):
            zone_out[j:j + 1, :] = hub_line(zone_acc, j)
        put_hub(z, where, col_out, dl, hub_acc, hub_two)


def fourth_pass(z, list_one, list_two, cot_hub, depot_push, zone_push, sums, a_one, a_two):
    dl, zl, hl = z.dep_lines, z.zone_lines, z.hub_lines
    return pl.pallas_call(
        functools.partial(fourth_kernel, z, len(sums)),
        grid=(z.steps,),
        in_specs=[smem(), smem(), whole(hl), whole(3 * dl), whole(3 * zl)] + [whole(hl)] * len(sums) + [resident(), resident()],
        out_specs=[whole(3 * hl), whole(dl + hl), whole(zl)],
        out_shape=[line_shape(3 * hl), line_shape(dl + hl), line_shape(zl)],
        scratch_shapes=[pltpu.VMEM((2, z.per * LANES, LANES), F32), pltpu.VMEM((LANES, LANES), F32),
                        pltpu.VMEM((z.per * LANES, LANES), F32), pltpu.VMEM((LANES, LANES), F32),
                        pltpu.VMEM((2, 8, z.hub_cols), F32), pltpu.VMEM((2, 8, z.zone_cols), F32),
                        pltpu.VMEM((z.two_lines, LANES), F32), pltpu.VMEM((hl + dl + zl, LANES), F32)],
        compiler_params=params(6), name="fourth_pass",
    )(list_one, list_two, cot_hub, depot_push, zone_push, *sums, a_one, a_two)


def result(half, quarter, cf, shift1, shift2, twice_late, mixed, early, km, minus):
    once = half - quarter
    t0 = jnp.tanh(half)
    t1 = jnp.tanh(once + shift1)
    t2 = jnp.tanh((once - quarter) + shift2)
    middle = mixed * (1.0 - t1 * t1)
    last = (cf + twice_late) * (1.0 - t2 * t2) + middle
    return km * (last + (middle - early * (1.0 - t0 * t0))), minus * last


def vectors(line, sign, now, after, push, lines):
    a, b = now[pl.ds(line, 1), :], after[pl.ds(line, 1), :]
    late, early = push[pl.ds(line, 1), :], push[pl.ds(lines + line, 1), :]
    return (0.25 * sign * a, 0.25 * sign * (a + b), 2.0 * late, early - 0.5 * late, early)


def wipe(ref, row, lane):
    ref[pl.ds(row, LANES), pl.ds(lane, LANES)] = jnp.zeros((LANES, LANES), F32)


def final_one_kernel(z, mask, lists, depot, hub, cap, depot_state, hub_state, depot_push, hub_push,
                     th, co, cf, theta_out, cost_out, token, cols):
    i, where = pl.program_id(0), place()
    off = where[1] * z.one_lines
    token[...] = jnp.zeros_like(token)
    for k in range(z.per):
        for x, v in enumerate(vectors(i * z.per + k, -1.0, depot, depot_state, depot_push, z.dep_lines)):
            cols[x, pl.ds(k * LANES, LANES), :] = as_rows(v)
        for j in range(z.one_lines):
            @pl.when(mask[i * z.per + k, j] == 0)
            def _():
                wipe(theta_out, k * LANES, j * LANES)
                wipe(cost_out, k * LANES, j * LANES)

    def tiles(entries):
        for e in entries:
            k, j = split_of(z, e)
            lane, base = lane_of(j), lane_of(k)
            rows = vectors(off + j, -1.0, hub, hub_state, hub_push, z.hub_lines)
            km = 0.25 * cap[pl.ds(off + j, 1), :].astype(F32)
            for s in range(0, LANES, SUB):
                at = pl.multiple_of(base + s, SUB)
                both = [cols[x, pl.ds(at, SUB), :] + r for x, r in enumerate(rows)]
                theta, cost = result(scaled(th, at, lane, 0.5), scaled(co, at, lane, 0.25), piece(cf, at, lane),
                                     *both, km, -km)
                theta_out[pl.ds(at, SUB), pl.ds(lane, LANES)] = theta
                cost_out[pl.ds(at, SUB), pl.ds(lane, LANES)] = cost

    th, co, cf = (rows_of(ref, z, i) for ref in (th, co, cf))
    walk(lists, i, tiles)


def final_two_kernel(z, mask, lists, hub, zone, cap, hub_state, zone_state, hub_push, zone_push,
                     th, co, cf, theta_out, cost_out, cols, *bufs):
    arrays = (th, co, cf)
    i, where = pl.program_id(0), place()
    line = where[0] * z.two_lines + i
    fetched(z, i, arrays, bufs[:-1], bufs[-1], range(z.steps))
    hubs = vectors(line, 1.0, hub, hub_state, hub_push, z.hub_lines)
    km = 0.0625 * cap[pl.ds(line, 1), :].astype(F32)
    for x, v in enumerate((hubs[0], hubs[1], -hubs[2], -hubs[3], -hubs[4], km, -km)):
        cols[x] = as_rows(v)

    def closed(j, carry):
        @pl.when(mask[i, j] == 0)
        def _():
            wipe(theta_out, 0, lane_of(j))
            wipe(cost_out, 0, lane_of(j))
        return carry

    lax.fori_loop(0, z.zone_lines, closed, 0)

    def tiles(js):
        for j in js:
            lane = lane_of(j)
            rows = vectors(j, 1.0, zone, zone_state, zone_push, z.zone_lines)
            for s in range(0, LANES, SUB):
                both = [cols[x, s:s + SUB, :] + r for x, r in enumerate(rows)]
                theta, cost = result(scaled(th, s, lane, 0.5), scaled(co, s, lane, 0.25), piece(cf, s, lane),
                                     *both, cols[5, s:s + SUB, :], cols[6, s:s + SUB, :])
                theta_out[pl.ds(s, SUB), pl.ds(lane, LANES)] = theta
                cost_out[pl.ds(s, SUB), pl.ds(lane, LANES)] = cost

    th, co, cf = fetched(z, i, arrays, bufs[:-1], bufs[-1])
    walk(lists, i, tiles)


def final_one(z, mask, lists, depot, hub, cap, depot_state, hub_state, depot_push, hub_push, th, co, cf):
    dl, hl = z.dep_lines, z.hub_lines
    out = jax.ShapeDtypeStruct(th.shape, F32)
    return pl.pallas_call(
        functools.partial(final_one_kernel, z), grid=(z.steps,),
        in_specs=[smem(), smem(), whole(dl), whole(hl), whole(hl), whole(2 * dl), whole(hl), whole(3 * dl),
                  whole(3 * hl)] + [resident()] * 3,
        out_specs=[z.one(), z.one(), whole(8)], out_shape=[out, out, line_shape(8)],
        scratch_shapes=[pltpu.VMEM((5, z.per * LANES, LANES), F32)],
        compiler_params=params(8), name="final_one",
    )(mask, lists, depot, hub, cap, depot_state, hub_state, depot_push, hub_push, th, co, cf)


def final_two(z, mask, lists, hub, zone, cap, hub_state, zone_state, hub_push, zone_push, th, co, cf):
    zl, hl = z.zone_lines, z.hub_lines
    out = jax.ShapeDtypeStruct(th.shape, F32)
    return pl.pallas_call(
        functools.partial(final_two_kernel, z), grid=(z.steps,),
        in_specs=[smem(), smem(), whole(hl), whole(zl), whole(hl), whole(hl), whole(2 * zl), whole(3 * hl),
                  whole(3 * zl)] + [left()] * 3,
        out_specs=[z.two(), z.two()], out_shape=[out, out],
        scratch_shapes=[pltpu.VMEM((7, LANES, LANES), F32)] + buffers(z, th, co, cf),
        compiler_params=params(38), name="final_two",
    )(mask, lists, hub, zone, cap, hub_state, zone_state, hub_push, zone_push, *pinned(th, co, cf))


def on_device(rows, cols, theta_one, theta_two, cost_one, cost_two, depot_price, hub_price, zone_price,
              mask_one, mask_two, supply, demand, capacity, cot_flow_one, cot_flow_two,
              cot_depot, cot_hub, cot_zone):
    z = Sizes(*theta_one.shape, *theta_two.shape, hub_price.shape[0], theta_one.shape[0] * rows)
    dl, hl, zl = z.dep_lines, z.hub_lines, z.zone_lines
    lines = lambda v: v.reshape(-1, LANES)
    depot, hub, zone, cap = lines(depot_price), lines(hub_price), lines(zone_price), lines(capacity)
    supply, demand = lines(supply), lines(demand)
    cot_depot, cot_hub, cot_zone = lines(cot_depot), lines(cot_hub), lines(cot_zone)

    a1_one, a1_two, col_vec, zone_vec, depot_pre, zone_pre, list_one, list_two = first_pass(
        z, mask_one, mask_two, depot, hub, zone, cap, theta_one, cost_one, theta_two, cost_two)
    depot_sum, row_vec = join(col_terms(col_vec, cols), zone_vec, dl)
    sums = gather_terms(row_vec, "row", rows)
    (a2_one, a2_two, depot_vec, zone_vec, depot_state, zone_state, hub_state, hub_one, hub_two) = second_pass(
        z, list_one, list_two, depot, hub, zone, cap, supply, demand, cot_hub, depot_pre, zone_pre,
        depot_sum, sums, theta_one, cost_one, cot_flow_one, theta_two, cost_two, cot_flow_two)
    d_sums = col_terms(depot_vec, cols)
    z_sums = gather_terms(zone_vec, "row", rows)
    depot_push, zone_push, hub_vec = third_pass(
        z, list_one, list_two, supply, demand, cot_depot, cot_zone, depot_state, zone_state, hub_one, hub_two,
        d_sums, z_sums, a2_one, a2_two)
    hub_sums = gather_terms(plus(*col_terms(hub_vec, cols)), "row", rows)
    hub_push, col_vec, zone_vec = fourth_pass(z, list_one, list_two, cot_hub, depot_push, zone_push, hub_sums,
                                              a1_one, a1_two)
    if cols >= 4 and cols & (cols - 1) == 0:
        col_vec = plus(col_vec, swap(col_vec, "col", cols, 1))
        distances = range(2, cols, 2)
    else:
        distances = range(1, cols)
    col_vec, push = lax.optimization_barrier((col_vec, hub_push))
    terms = gather_terms(col_vec, "col", cols, distances)
    grad_theta_one, grad_cost_one, token = final_one(
        z, mask_one, list_one, depot, hub, cap, depot_state, hub_state, depot_push, push,
        theta_one, cost_one, cot_flow_one)
    depot_sum, row_vec = join(terms, zone_vec, dl, [token])
    row_vec, push = lax.optimization_barrier((row_vec, hub_push))
    terms = gather_terms(row_vec, "row", rows)
    grad_theta_two, grad_cost_two = final_two(
        z, mask_two, list_two, hub, zone, cap, hub_state, zone_state, push, zone_push,
        theta_two, cost_two, cot_flow_two)
    grad_depot, grad_hub, grad_zone = ends(z, depot_sum, terms, depot_push, hub_push, zone_push)
    return (grad_theta_one, grad_theta_two, grad_cost_one, grad_cost_two,
            grad_depot.reshape(-1), grad_hub.reshape(-1), grad_zone.reshape(-1))


def solution(mesh):
    split, row, col, copied = P("row", "col"), P("row"), P("col"), P()
    return jax.shard_map(
        functools.partial(on_device, mesh.shape["row"], mesh.shape["col"]),
        mesh=mesh,
        in_specs=(split, split, split, split, row, copied, col, split, split, row, col, copied, split, split,
                  row, copied, col),
        out_specs=(split, split, split, split, row, copied, col),
        check_vma=False,
    )
```

```python
import functools

import jax
import jax.numpy as jnp
from jax import lax
from jax.experimental import pallas as pl
from jax.experimental.pallas import tpu as pltpu
from jax.sharding import PartitionSpec as P

STEP_PRIMAL = 0.5
STEP_DUAL = 0.5
HUB_RATE = 4.0
LANES = 128
SUB = 32
F32 = jnp.float32
BF16 = jnp.bfloat16


def swap(value, axis, size, distance):
    if size & (size - 1) == 0:
        pairs = [(i, i ^ distance) for i in range(size)]
    else:
        pairs = [(i, (i + distance) % size) for i in range(size)]
    return lax.ppermute(value, axis, pairs)


def gather_terms(value, axis, size, distances=None):
    return [value] + [swap(value, axis, size, k) for k in distances or range(1, size)]


def col_terms(value, size):
    if size & (size - 1) or size < 4:
        return gather_terms(value, "col", size)
    both = plus(value, swap(value, "col", size, 1))
    return gather_terms(both, "col", size, range(2, size, 2))


def plus(*terms):
    def body(*refs):
        refs[-1][...] = add_all([ref[...] for ref in refs[:-1]])

    return pl.pallas_call(
        body, in_specs=[resident()] * len(terms), out_specs=resident(),
        out_shape=jax.ShapeDtypeStruct(terms[0].shape, F32),
        compiler_params=pltpu.CompilerParams(vmem_limit_bytes=2 * 2**20), name="plus")(*terms)


def join(terms, lower, first, after=()):
    lines = terms[0].shape[0]

    def body(*refs):
        refs = refs[len(after):]
        total = add_all([ref[...] for ref in refs[:-3]])
        refs[-2][...] = total[:first]
        refs[-1][0:lines - first, :] = total[first:]
        refs[-1][lines - first:, :] = refs[-3][...]

    return pl.pallas_call(
        body, in_specs=[resident()] * (len(after) + len(terms) + 1), out_specs=[resident()] * 2,
        out_shape=[line_shape(first), line_shape(lines - first + lower.shape[0])],
        compiler_params=pltpu.CompilerParams(vmem_limit_bytes=2 * 2**20), name="join")(*after, *terms, lower)


def ends(z, depot_sum, row_terms, depot_push, hub_push, zone_push):
    dl, hl, zl = z.dep_lines, z.hub_lines, z.zone_lines

    def body(depot_in, depot_last, hub_last, zone_last, *refs):
        total = add_all([ref[...] for ref in refs[:-3]])
        refs[-3][...] = depot_last[2 * dl:, :] - STEP_PRIMAL * depot_in[...]
        refs[-2][...] = hub_last[2 * hl:, :] - STEP_PRIMAL * total[:hl]
        refs[-1][...] = zone_last[2 * zl:, :] + STEP_PRIMAL * total[hl:]

    return pl.pallas_call(
        body, in_specs=[resident()] * (len(row_terms) + 4), out_specs=[resident()] * 3,
        out_shape=[line_shape(dl), line_shape(hl), line_shape(zl)],
        compiler_params=pltpu.CompilerParams(vmem_limit_bytes=2 * 2**20), name="ends",
    )(depot_sum, depot_push, hub_push, zone_push, *row_terms)


def add_all(terms):
    total = terms[0]
    for term in terms[1:]:
        total = total + term
    return total


def as_rows(line):
    return jnp.broadcast_to(line, (LANES, LANES)).T


def as_line(block):
    return jnp.sum(block.T, axis=0, keepdims=True)


def fold(value):
    return jnp.sum(value.reshape(-1, 8, LANES), axis=0)


def fold_line(value):
    return jnp.sum(value, axis=0, keepdims=True)


def piece(ref, row, lane):
    return ref[pl.ds(row, SUB), pl.ds(lane, LANES)].astype(F32)


class Sizes:
    def __init__(self, dep_rows, hub_cols, hub_rows, zone_cols, hubs, deps):
        self.dep_rows, self.hub_cols, self.hub_rows, self.zone_cols = dep_rows, hub_cols, hub_rows, zone_cols
        self.hubs, self.deps = hubs, deps
        self.dep_lines, self.one_lines = dep_rows // LANES, hub_cols // LANES
        self.two_lines, self.zone_lines = hub_rows // LANES, zone_cols // LANES
        self.hub_lines = hubs // LANES
        self.steps = self.two_lines
        self.per = self.dep_lines // self.steps
        assert self.per * self.steps == self.dep_lines

    def one(self):
        return pl.BlockSpec((self.per * LANES, self.hub_cols), lambda i: (i, 0))

    def list_shapes(self):
        return [jax.ShapeDtypeStruct((self.steps, self.per * self.one_lines + 1), jnp.int32),
                jax.ShapeDtypeStruct((self.steps, self.zone_lines + 1), jnp.int32)]

    def two(self):
        return pl.BlockSpec((LANES, self.zone_cols), lambda i: (i, 0))


def whole(lines):
    return pl.BlockSpec((lines, LANES), lambda i: (0, 0))


def smem():
    return pl.BlockSpec(memory_space=pltpu.SMEM)


def line_shape(lines):
    return jax.ShapeDtypeStruct((lines, LANES), F32)


def params(mib):
    return pltpu.CompilerParams(dimension_semantics=("arbitrary",), vmem_limit_bytes=mib * 2**20)


def resident():
    return pl.BlockSpec(memory_space=pltpu.VMEM)


def pinned(*arrays):
    return [pltpu.with_memory_space_constraint(array, pltpu.HBM) for array in arrays]


def place():
    return lax.axis_index("row"), lax.axis_index("col")


def rows_of(ref, z, i):
    rows = ref.shape[0] // z.steps
    return ref.at[pl.ds(pl.multiple_of(i * rows, rows), rows), :]


def listed(values, out, line):
    n = jnp.int32(0)
    for j, value in enumerate(values):
        out[line, n + 1] = jnp.int32(j)
        n = n + value
    out[line, 0] = n


def walk(lists, line, body, width=2):
    n = lists[line, 0]

    def group(start, size):
        body([lists[line, start + 1 + x] for x in range(size)])

    def full(p, carry):
        group(width * p, width)
        return carry

    lax.fori_loop(0, lax.div(n, width), full, 0)
    size = width // 2
    while size:
        rest = lax.rem(n, 2 * size)

        @pl.when(rest >= size)
        def _():
            group(n - rest, size)

        size //= 2


def lane_of(j):
    return pl.multiple_of(j * LANES, LANES)


def scaled(ref, row, lane, scale):
    return (ref[pl.ds(row, SUB), pl.ds(lane, LANES)] * jnp.asarray(scale, BF16)).astype(F32)


def fetched(z, i, arrays, bufs, sems, start=None, only=None):
    rows = [array.shape[0] // z.steps for array in arrays]

    def copy(x, step):
        at = pl.ds(pl.multiple_of(step * rows[x], rows[x]), rows[x])
        return pltpu.make_async_copy(arrays[x].at[at, :], bufs[x].at[at, :], sems.at[x, step])

    if start is not None:
        @pl.when(i == 0)
        def _():
            for step in start:
                for x in range(len(arrays)):
                    copy(x, step).start()
        return None
    only = range(len(arrays)) if only is None else only
    for x in only:
        copy(x, i).wait()
    return [bufs[x].at[pl.ds(pl.multiple_of(i * rows[x], rows[x]), rows[x]), :] for x in only]


def buffers(z, *arrays):
    return [pltpu.VMEM(array.shape, array.dtype) for array in arrays] + [
        pltpu.SemaphoreType.DMA((len(arrays), z.steps))]


def left():
    return pl.BlockSpec(memory_space=pltpu.HBM)


def clear(*refs):
    for ref in refs:
        ref[...] = jnp.zeros_like(ref)


def split_of(z, e):
    return lax.div(e, z.one_lines), lax.rem(e, z.one_lines)


def first_kernel(z, mask_one, mask_two, depot, hub, zone, cap, th1, co1, th2, co2,
                 a_one, a_two, col_out, zone_out, depot_pre, zone_pre, list_one, list_two,
                 row1, row0, both1, both0, shift_one, shift, keep, ksum, keeps, hub_acc, zone1, zone0, hub_two, *bufs):
    i, where = pl.program_id(0), place()
    smalls, bufs = bufs[:5], bufs[5:]
    off_one, off_two = where[1] * z.one_lines, where[0] * z.two_lines
    arrays = (th1, co1, th2, co2)
    small = [pltpu.make_async_copy(a, b, smalls[-1].at[x])
             for x, (a, b) in enumerate(zip((depot, hub, zone, cap), smalls[:-1]))]
    depot, hub, zone, cap = smalls[:-1]

    @pl.when(i == 0)
    def _():
        for copy in small:
            copy.start()
        clear(hub_acc, zone1, zone0)

    fetched(z, i, arrays, bufs[:-1], bufs[-1], range(1))

    @pl.when(i == 0)
    def _():
        for copy in small:
            copy.wait()

    fetched(z, i, arrays, bufs[:-1], bufs[-1], range(1, z.steps))
    a_one, a_two = rows_of(a_one, z, i), rows_of(a_two, z, i)
    clear(row1, row0, both1, both0, keeps)
    for k in range(z.per):
        shift_one[pl.ds(k * LANES, LANES), :] = as_rows(0.25 * depot[pl.ds(i * z.per + k, 1), :])
    shift[...] = as_rows(0.25 * hub[pl.ds(off_two + i, 1), :])
    keep[...] = as_rows(0.25 * cap[pl.ds(off_two + i, 1), :].astype(F32))
    ksum[...] = 0.5 * fold(keep[...])
    listed([mask_one[j, i * z.per + k] for k in range(z.per) for j in range(z.one_lines)], list_one, i)
    listed([mask_two[i, j] for j in range(z.zone_lines)], list_two, i)

    def tiles_one(entries):
        for x, e in enumerate(entries):
            k, j = split_of(z, e)
            lane, base = lane_of(j), lane_of(k)
            hrow = 0.25 * hub[pl.ds(off_one + j, 1), :]
            km = cap[pl.ds(off_one + j, 1), :].astype(F32)
            total = 0.5 * LANES / 8 * jnp.broadcast_to(km, (8, LANES))
            keeps[x, pl.ds(k, 1), :] += km
            for s in range(0, LANES, SUB):
                at = pl.multiple_of(base + s, SUB)
                half = scaled(th1, at, lane, 0.5)
                t0 = jnp.tanh(half)
                t1 = jnp.tanh((half - scaled(co1, at, lane, 0.25)) - (shift_one[pl.ds(at, SUB), :] + hrow))
                k1, k0 = km * t1, km * t0
                row1[x, pl.ds(at, SUB), :] += k1
                row0[x, pl.ds(at, SUB), :] += k0
                total = total + (fold(k1) - 0.5 * fold(k0))
                a_one[pl.ds(at, SUB), pl.ds(lane, LANES)] = (km - k1 * t1).astype(BF16)
            hub_acc[x, :, pl.ds(lane, LANES)] += total

    def tiles_two(js):
        zrows = [0.25 * zone[pl.ds(j, 1), :] for j in js]
        sum1 = [jnp.zeros((8, LANES), F32) for j in js]
        sum0 = [jnp.zeros((8, LANES), F32) for j in js]
        for s in range(0, LANES, SUB):
            hcol, km = shift[s:s + SUB, :], keep[s:s + SUB, :]
            all1, all0 = [], []
            for x, j in enumerate(js):
                lane = lane_of(j)
                half = scaled(th2, s, lane, 0.5)
                t0 = jnp.tanh(half)
                t1 = jnp.tanh((half - scaled(co2, s, lane, 0.25)) + (hcol + zrows[x]))
                k1, k0 = km * t1, km * t0
                all1.append(k1)
                all0.append(k0)
                sum1[x] = sum1[x] + fold(k1)
                sum0[x] = sum0[x] + fold(k0)
                a_two[pl.ds(s, SUB), pl.ds(lane, LANES)] = (km - k1 * t1).astype(BF16)
            both1[s:s + SUB, :] += add_all(all1)
            both0[s:s + SUB, :] += add_all(all0)
        for x, j in enumerate(js):
            zone1[x % 2, :, pl.ds(lane_of(j), LANES)] += sum1[x] - 2.0 * ksum[...]
            zone0[x % 2, :, pl.ds(lane_of(j), LANES)] += sum0[x] - 6.0 * ksum[...]

    th1, co1 = fetched(z, i, arrays, bufs[:-1], bufs[-1], only=(0, 1))
    walk(list_one, i, tiles_one)
    th2, co2 = fetched(z, i, arrays, bufs[:-1], bufs[-1], only=(2, 3))
    walk(list_two, i, tiles_two, 4)
    for k in range(z.per):
        line, at = i * z.per + k, pl.ds(k * LANES, LANES)
        line1, line0 = as_line(row1[0, at, :] + row1[1, at, :]), as_line(row0[0, at, :] + row0[1, at, :])
        half = 0.5 * jnp.sum(keeps[0, k:k + 1, :] + keeps[1, k:k + 1, :])
        col_out[pl.ds(line, 1), :] = half + line1 - 0.5 * line0
        depot_pre[pl.ds(line, 1), :] = half - 0.5 * line1
    opened = list_two[i, 0].astype(F32)
    hub_two[pl.ds(i, 1), :] = as_line(both1[...] - 0.5 * both0[...] + (0.5 * opened) * keep[...])

    @pl.when(i == z.steps - 1)
    def _():
        for j in range(z.zone_lines):
            at = slice(j * LANES, (j + 1) * LANES)
            line1, line0 = fold_line(zone1[0, :, at] + zone1[1, :, at]), fold_line(zone0[0, :, at] + zone0[1, :, at])
            zone_out[j:j + 1, :] = line1 - 0.5 * line0
            zone_pre[j:j + 1, :] = -0.5 * line1
        put_hub(z, where, col_out, z.dep_lines, hub_acc, hub_two)


def hub_line(hub_acc, j):
    at = slice(j * LANES, (j + 1) * LANES)
    return fold_line(hub_acc[0, :, at] + hub_acc[1, :, at])


def put_hub(z, where, out, base, hub_acc, hub_two):
    out[base:base + z.hub_lines, :] = jnp.zeros((z.hub_lines, LANES), F32)
    for j in range(z.two_lines):
        out[pl.ds(base + where[0] * z.two_lines + j, 1), :] = -hub_two[j:j + 1, :]
    for j in range(z.one_lines):
        at = base + where[1] * z.one_lines + j
        out[pl.ds(at, 1), :] = out[pl.ds(at, 1), :] + hub_line(hub_acc, j)


def first_pass(z, mask_one, mask_two, depot, hub, zone, cap, th1, co1, th2, co2):
    return pl.pallas_call(
        functools.partial(first_kernel, z),
        grid=(z.steps,),
        in_specs=[smem(), smem()] + [left()] * 8,
        out_specs=[resident(), resident(), whole(z.dep_lines + z.hub_lines), whole(z.zone_lines),
                   whole(z.dep_lines), whole(z.zone_lines), smem(), smem()],
        out_shape=[pltpu.VMEM(th1.shape, BF16), pltpu.VMEM(th2.shape, BF16),
                   line_shape(z.dep_lines + z.hub_lines), line_shape(z.zone_lines),
                   line_shape(z.dep_lines), line_shape(z.zone_lines)] + z.list_shapes(),
        scratch_shapes=[pltpu.VMEM((2, z.per * LANES, LANES), F32)] * 2 + [pltpu.VMEM((LANES, LANES), F32)] * 2
                       + [pltpu.VMEM((z.per * LANES, LANES), F32)] + [pltpu.VMEM((LANES, LANES), F32)] * 2
                       + [pltpu.VMEM((8, LANES), F32), pltpu.VMEM((2, z.per, LANES), F32), pltpu.VMEM((2, 8, z.hub_cols), F32)]
                       + [pltpu.VMEM((2, 8, z.zone_cols), F32)] * 2 + [pltpu.VMEM((z.two_lines, LANES), F32)]
                       + [pltpu.VMEM(v.shape, v.dtype) for v in (depot, hub, zone, cap)]
                       + [pltpu.SemaphoreType.DMA((4,))] + buffers(z, th1, co1, th2, co2),
        compiler_params=params(28), name="first_pass",
    )(mask_one, mask_two, *pinned(depot, hub, zone, cap, th1, co1, th2, co2))


def second_kernel(z, terms, list_one, list_two, depot, hub, zone, cap, supply, demand, cot_hub,
                  depot_pre, zone_pre, depot_sum, *rest):
    sums, rest = rest[:terms], rest[terms:]
    (th1, co1, cf1, th2, co2, cf2,
     a_one, a_two, depot_out, zone_out, depot_state, zone_state, hub_state, hub_one_out, hub_two_out,
     rowk, rowa, rowe, both, shift_one, shift, keep, pushes, hub_acc, zonek, zonea, zonee,
     shift_d, shift_h, shift_z, *bufs) = rest
    arrays = (th1, co1, cf1, th2, co2, cf2)
    i, where = pl.program_id(0), place()
    off_one, off_two = where[1] * z.one_lines, where[0] * z.two_lines
    dl, zl, hl = z.dep_lines, z.zone_lines, z.hub_lines

    fetched(z, i, arrays, bufs[:-1], bufs[-1], range(z.steps))

    a_one, a_two = rows_of(a_one, z, i), rows_of(a_two, z, i)

    @pl.when(i == 0)
    def _():
        clear(hub_acc, zonek, zonea, zonee)
        total = sums[0][...]
        for term in sums[1:]:
            total = total + term[...]
        grow_d = jnp.exp(STEP_DUAL * (depot_sum[...] / z.hubs - 0.5 * supply[...].astype(F32)))
        grow_z = jnp.exp(STEP_DUAL * (0.125 * demand[...].astype(F32) - total[hl:, :] / z.hubs))
        new_d, new_z = depot[...] * grow_d, zone[...] * grow_z
        new_h = hub[...] + HUB_RATE * total[:hl, :] / z.deps
        depot_state[0:dl, :] = new_d
        depot_state[dl:2 * dl, :] = grow_d
        zone_state[0:zl, :] = new_z
        zone_state[zl:2 * zl, :] = grow_z
        hub_state[...] = new_h
        shift_d[...] = 0.25 * (depot[...] + new_d)
        shift_h[...] = 0.25 * (hub[...] + new_h)
        shift_z[...] = 0.25 * (zone[...] + new_z)

    push = 2.0 * HUB_RATE / z.deps
    clear(rowk, rowa, rowe, both)
    for k in range(z.per):
        shift_one[pl.ds(k * LANES, LANES), :] = as_rows(shift_d[pl.ds(i * z.per + k, 1), :])
    shift[...] = as_rows(shift_h[pl.ds(off_two + i, 1), :])
    pushes[...] = as_rows(push * cot_hub[pl.ds(off_two + i, 1), :])
    keep[...] = as_rows(0.25 * cap[pl.ds(off_two + i, 1), :].astype(F32))

    def tiles_one(entries):
        for x, e in enumerate(entries):
            k, j = split_of(z, e)
            lane, base = lane_of(j), lane_of(k)
            hrow = shift_h[pl.ds(off_one + j, 1), :]
            prow = push * cot_hub[pl.ds(off_one + j, 1), :]
            km = cap[pl.ds(off_one + j, 1), :].astype(F32)
            total = jnp.zeros((8, LANES), F32)
            for s in range(0, LANES, SUB):
                at = pl.multiple_of(base + s, SUB)
                t2 = jnp.tanh((scaled(th1, at, lane, 0.5) - scaled(co1, at, lane, 0.5))
                              - (shift_one[pl.ds(at, SUB), :] + hrow))
                k2 = km * t2
                a2 = km - k2 * t2
                e = (piece(cf1, at, lane) + prow) * a2
                rowk[x, pl.ds(at, SUB), :] += k2
                rowa[x, pl.ds(at, SUB), :] += a2
                rowe[x, pl.ds(at, SUB), :] += e
                total = total + fold(e)
                a_one[pl.ds(at, SUB), pl.ds(lane, LANES)] = a2.astype(BF16)
            hub_acc[x, :, pl.ds(lane, LANES)] += total

    def tiles_two(js):
        zrows = [shift_z[pl.ds(j, 1), :] for j in js]
        sumk, suma, sume = ([jnp.zeros((8, LANES), F32) for j in js] for _ in range(3))
        for s in range(0, LANES, SUB):
            hcol, km, pcol = shift[s:s + SUB, :], keep[s:s + SUB, :], pushes[s:s + SUB, :]
            alle = []
            for x, j in enumerate(js):
                lane = lane_of(j)
                t2 = jnp.tanh((scaled(th2, s, lane, 0.5) - scaled(co2, s, lane, 0.5)) + (hcol + zrows[x]))
                k2 = km * t2
                a2 = km - k2 * t2
                e = (piece(cf2, s, lane) - pcol) * a2
                alle.append(e)
                sumk[x] = sumk[x] + fold(k2)
                suma[x] = suma[x] + fold(a2)
                sume[x] = sume[x] + fold(e)
                a_two[pl.ds(s, SUB), pl.ds(lane, LANES)] = a2.astype(BF16)
            both[s:s + SUB, :] += add_all(alle)
        for x, j in enumerate(js):
            zonek[x % 2, :, pl.ds(lane_of(j), LANES)] += sumk[x]
            zonea[x % 2, :, pl.ds(lane_of(j), LANES)] += suma[x]
            zonee[x % 2, :, pl.ds(lane_of(j), LANES)] += sume[x]

    th1, co1, cf1 = fetched(z, i, arrays, bufs[:-1], bufs[-1], only=(0, 1, 2))
    walk(list_one, i, tiles_one)
    th2, co2, cf2 = fetched(z, i, arrays, bufs[:-1], bufs[-1], only=(3, 4, 5))
    walk(list_two, i, tiles_two, 4)
    for k in range(z.per):
        line, at = i * z.per + k, pl.ds(k * LANES, LANES)
        depot_out[pl.ds(line, 1), :] = depot_pre[pl.ds(line, 1), :] + as_line(rowk[0, at, :] + rowk[1, at, :])
        depot_out[pl.ds(dl + line, 1), :] = as_line(rowa[0, at, :] + rowa[1, at, :])
        depot_out[pl.ds(2 * dl + line, 1), :] = as_line(rowe[0, at, :] + rowe[1, at, :])
    hub_two_out[pl.ds(i, 1), :] = as_line(both[...])

    @pl.when(i == z.steps - 1)
    def _():
        for j in range(zl):
            at = slice(j * LANES, (j + 1) * LANES)
            zone_out[j:j + 1, :] = zone_pre[j:j + 1, :] + fold_line(zonek[0, :, at] + zonek[1, :, at])
            zone_out[zl + j:zl + j + 1, :] = fold_line(zonea[0, :, at] + zonea[1, :, at])
            zone_out[2 * zl + j:2 * zl + j + 1, :] = fold_line(zonee[0, :, at] + zonee[1, :, at])
        for j in range(z.one_lines):
            hub_one_out[j:j + 1, :] = hub_line(hub_acc, j)


def second_pass(z, list_one, list_two, depot, hub, zone, cap, supply, demand, cot_hub,
                depot_pre, zone_pre, depot_sum, sums, th1, co1, cf1, th2, co2, cf2):
    dl, zl, hl = z.dep_lines, z.zone_lines, z.hub_lines
    return pl.pallas_call(
        functools.partial(second_kernel, z, len(sums)),
        grid=(z.steps,),
        in_specs=[smem(), smem(), whole(dl), whole(hl), whole(zl), whole(hl), whole(dl), whole(zl), whole(hl),
                  whole(dl), whole(zl), whole(dl)] + [whole(hl + zl)] * len(sums)
                 + [left()] * 6,
        out_specs=[resident(), resident(), whole(3 * dl), whole(3 * zl), whole(2 * dl), whole(2 * zl), whole(hl),
                   whole(z.one_lines), whole(z.two_lines)],
        out_shape=[pltpu.VMEM(th1.shape, BF16), pltpu.VMEM(th2.shape, BF16),
                   line_shape(3 * dl), line_shape(3 * zl), line_shape(2 * dl), line_shape(2 * zl), line_shape(hl),
                   line_shape(z.one_lines), line_shape(z.two_lines)],
        scratch_shapes=[pltpu.VMEM((2, z.per * LANES, LANES), F32)] * 3 + [pltpu.VMEM((LANES, LANES), F32)]
                       + [pltpu.VMEM((z.per * LANES, LANES), F32)] + [pltpu.VMEM((LANES, LANES), F32)] * 3
                       + [pltpu.VMEM((2, 8, z.hub_cols), F32)] + [pltpu.VMEM((2, 8, z.zone_cols), F32)] * 3
                       + [pltpu.VMEM((dl, LANES), F32), pltpu.VMEM((hl, LANES), F32), pltpu.VMEM((zl, LANES), F32)]
                       + buffers(z, th1, co1, cf1, th2, co2, cf2),
        compiler_params=params(38), name="second_pass",
    )(list_one, list_two, depot, hub, zone, cap, supply, demand, cot_hub, depot_pre, zone_pre, depot_sum,
      *sums, *pinned(th1, co1, cf1, th2, co2, cf2))


def third_kernel(z, d_terms, z_terms, list_one, list_two, supply, demand, cot_depot, cot_zone, depot_state, zone_state,
                 hub_one_in, hub_two_in, *rest):
    d_sums, rest = rest[:d_terms], rest[d_terms:]
    z_sums, rest = rest[:z_terms], rest[z_terms:]
    a_one, a_two, depot_out, zone_out, hub_out, row, shift_one, hub_acc, hub_two = rest
    i, where = pl.program_id(0), place()
    dl, zl = z.dep_lines, z.zone_lines
    rate = STEP_DUAL / z.hubs

    a_one, a_two = rows_of(a_one, z, i), rows_of(a_two, z, i)

    @pl.when(i == 0)
    def _():
        hub_acc[...] = jnp.zeros_like(hub_acc)
        total = d_sums[0][...]
        for term in d_sums[1:]:
            total = total + term[...]
        grow = jnp.exp(STEP_DUAL * (total[0:dl, :] / z.hubs - 0.5 * supply[...].astype(F32)))
        first, first_grow = depot_state[0:dl, :], depot_state[dl:2 * dl, :]
        push = cot_depot[...] * (first * grow) * rate
        reached = 0.25 * (total[2 * dl:3 * dl, :] + 2.0 * push * total[dl:2 * dl, :])
        adj = cot_depot[...] * grow - STEP_PRIMAL * reached
        depot_out[0:dl, :] = push
        depot_out[dl:2 * dl, :] = adj * first * rate
        depot_out[2 * dl:3 * dl, :] = adj * first_grow - STEP_PRIMAL * reached
        total = z_sums[0][...]
        for term in z_sums[1:]:
            total = total + term[...]
        grow = jnp.exp(STEP_DUAL * (0.125 * demand[...].astype(F32) - total[0:zl, :] / z.hubs))
        first, first_grow = zone_state[0:zl, :], zone_state[zl:2 * zl, :]
        push = -(cot_zone[...] * (first * grow) * rate)
        reached = 0.25 * (total[2 * zl:3 * zl, :] + 2.0 * push * total[zl:2 * zl, :])
        adj = cot_zone[...] * grow + STEP_PRIMAL * reached
        zone_out[0:zl, :] = push
        zone_out[zl:2 * zl, :] = -(adj * first * rate)
        zone_out[2 * zl:3 * zl, :] = adj * first_grow + STEP_PRIMAL * reached

    clear(row)
    for k in range(z.per):
        shift_one[pl.ds(k * LANES, LANES), :] = as_rows(depot_out[pl.ds(i * z.per + k, 1), :])

    def tiles_one(entries):
        for x, e in enumerate(entries):
            k, j = split_of(z, e)
            lane, base = lane_of(j), lane_of(k)
            total = jnp.zeros((8, LANES), F32)
            for s in range(0, LANES, SUB):
                at = pl.multiple_of(base + s, SUB)
                total = total + fold(piece(a_one, at, lane) * shift_one[pl.ds(at, SUB), :])
            hub_acc[x, :, pl.ds(lane, LANES)] += total

    def tiles_two(js):
        zrows = [zone_out[pl.ds(j, 1), :] for j in js]
        for s in range(0, LANES, SUB):
            row[s:s + SUB, :] += add_all([piece(a_two, s, lane_of(j)) * zrows[x] for x, j in enumerate(js)])

    walk(list_one, i, tiles_one)
    walk(list_two, i, tiles_two, 4)
    hub_two[pl.ds(i, 1), :] = -0.25 * (hub_two_in[pl.ds(i, 1), :] + 2.0 * as_line(row[...]))

    @pl.when(i == z.steps - 1)
    def _():
        hub_out[...] = jnp.zeros_like(hub_out)
        for j in range(z.two_lines):
            hub_out[pl.ds(where[0] * z.two_lines + j, 1), :] = -hub_two[j:j + 1, :]
        for j in range(z.one_lines):
            at = where[1] * z.one_lines + j
            line = hub_line(hub_acc, j)
            hub_out[pl.ds(at, 1), :] = hub_out[pl.ds(at, 1), :] - 0.25 * (hub_one_in[j:j + 1, :] + 2.0 * line)


def third_pass(z, list_one, list_two, supply, demand, cot_depot, cot_zone, depot_state, zone_state, hub_one, hub_two,
               d_sums, z_sums, a_one, a_two):
    dl, zl, hl = z.dep_lines, z.zone_lines, z.hub_lines
    return pl.pallas_call(
        functools.partial(third_kernel, z, len(d_sums), len(z_sums)),
        grid=(z.steps,),
        in_specs=[smem(), smem(), whole(dl), whole(zl), whole(dl), whole(zl), whole(2 * dl), whole(2 * zl),
                  whole(z.one_lines), whole(z.two_lines)]
                 + [whole(3 * dl)] * len(d_sums) + [whole(3 * zl)] * len(z_sums) + [resident(), resident()],
        out_specs=[whole(3 * dl), whole(3 * zl), whole(hl)],
        out_shape=[line_shape(3 * dl), line_shape(3 * zl), line_shape(hl)],
        scratch_shapes=[pltpu.VMEM((LANES, LANES), F32), pltpu.VMEM((z.per * LANES, LANES), F32),
                        pltpu.VMEM((2, 8, z.hub_cols), F32), pltpu.VMEM((z.two_lines, LANES), F32)],
        compiler_params=params(6), name="third_pass",
    )(list_one, list_two, supply, demand, cot_depot, cot_zone, depot_state, zone_state, hub_one, hub_two,
      *d_sums, *z_sums, a_one, a_two)


def fourth_kernel(z, terms, list_one, list_two, cot_hub, depot_push, zone_push, *rest):
    sums, rest = rest[:terms], rest[terms:]
    (a_one, a_two, hub_out, col_out, zone_out, row, both, shift_one, shift, hub_acc, zone_acc, hub_two, mix) = rest
    i, where = pl.program_id(0), place()
    off_one, off_two = where[1] * z.one_lines, where[0] * z.two_lines
    dl, zl, hl = z.dep_lines, z.zone_lines, z.hub_lines
    rate = HUB_RATE / z.deps

    a_one, a_two = rows_of(a_one, z, i), rows_of(a_two, z, i)

    @pl.when(i == 0)
    def _():
        hub_acc[...] = jnp.zeros_like(hub_acc)
        zone_acc[...] = jnp.zeros_like(zone_acc)
        total = sums[0][...]
        for term in sums[1:]:
            total = total + term[...]
        adj = cot_hub[...] + STEP_PRIMAL * total
        late, early = cot_hub[...] * rate, adj * rate
        hub_out[0:hl, :] = late
        hub_out[hl:2 * hl, :] = early
        hub_out[2 * hl:3 * hl, :] = adj + STEP_PRIMAL * total
        mix[0:hl, :] = 0.25 * (2.0 * early - late)
        mix[hl:hl + dl, :] = 0.25 * (2.0 * depot_push[dl:2 * dl, :] - depot_push[0:dl, :])
        mix[hl + dl:, :] = 0.25 * (2.0 * zone_push[zl:2 * zl, :] - zone_push[0:zl, :])

    clear(row, both)
    for k in range(z.per):
        shift_one[pl.ds(k * LANES, LANES), :] = as_rows(mix[pl.ds(hl + i * z.per + k, 1), :])
    shift[...] = as_rows(mix[pl.ds(off_two + i, 1), :])

    def tiles_one(entries):
        for x, e in enumerate(entries):
            k, j = split_of(z, e)
            lane, base = lane_of(j), lane_of(k)
            hrow = mix[pl.ds(off_one + j, 1), :]
            total = jnp.zeros((8, LANES), F32)
            for s in range(0, LANES, SUB):
                at = pl.multiple_of(base + s, SUB)
                y = piece(a_one, at, lane) * (shift_one[pl.ds(at, SUB), :] + hrow)
                row[x, pl.ds(at, SUB), :] += y
                total = total + fold(y)
            hub_acc[x, :, pl.ds(lane, LANES)] += total

    def tiles_two(js):
        zrows = [mix[pl.ds(hl + dl + j, 1), :] for j in js]
        totals = [jnp.zeros((8, LANES), F32) for j in js]
        for s in range(0, LANES, SUB):
            ys = [piece(a_two, s, lane_of(j)) * (zrows[x] - shift[s:s + SUB, :]) for x, j in enumerate(js)]
            both[s:s + SUB, :] += add_all(ys)
            totals = [total + fold(y) for total, y in zip(totals, ys)]
        for x, j in enumerate(js):
            zone_acc[x % 2, :, pl.ds(lane_of(j), LANES)] += totals[x]

    walk(list_one, i, tiles_one)
    walk(list_two, i, tiles_two, 4)
    for k in range(z.per):
        at = pl.ds(k * LANES, LANES)
        col_out[pl.ds(i * z.per + k, 1), :] = as_line(row[0, at, :] + row[1, at, :])
    hub_two[pl.ds(i, 1), :] = as_line(both[...])

    @pl.when(i == z.steps - 1)
    def _():
        for j in range(zl):
            zone_out[j:j + 1, :] = hub_line(zone_acc, j)
        put_hub(z, where, col_out, dl, hub_acc, hub_two)


def fourth_pass(z, list_one, list_two, cot_hub, depot_push, zone_push, sums, a_one, a_two):
    dl, zl, hl = z.dep_lines, z.zone_lines, z.hub_lines
    return pl.pallas_call(
        functools.partial(fourth_kernel, z, len(sums)),
        grid=(z.steps,),
        in_specs=[smem(), smem(), whole(hl), whole(3 * dl), whole(3 * zl)] + [whole(hl)] * len(sums) + [resident(), resident()],
        out_specs=[whole(3 * hl), whole(dl + hl), whole(zl)],
        out_shape=[line_shape(3 * hl), line_shape(dl + hl), line_shape(zl)],
        scratch_shapes=[pltpu.VMEM((2, z.per * LANES, LANES), F32), pltpu.VMEM((LANES, LANES), F32),
                        pltpu.VMEM((z.per * LANES, LANES), F32), pltpu.VMEM((LANES, LANES), F32),
                        pltpu.VMEM((2, 8, z.hub_cols), F32), pltpu.VMEM((2, 8, z.zone_cols), F32),
                        pltpu.VMEM((z.two_lines, LANES), F32), pltpu.VMEM((hl + dl + zl, LANES), F32)],
        compiler_params=params(6), name="fourth_pass",
    )(list_one, list_two, cot_hub, depot_push, zone_push, *sums, a_one, a_two)


def result(half, quarter, cf, shift1, shift2, twice_late, mixed, early, km, minus):
    once = half - quarter
    t0 = jnp.tanh(half)
    t1 = jnp.tanh(once + shift1)
    t2 = jnp.tanh((once - quarter) + shift2)
    middle = mixed * (1.0 - t1 * t1)
    last = (cf + twice_late) * (1.0 - t2 * t2) + middle
    return km * (last + (middle - early * (1.0 - t0 * t0))), minus * last


def vectors(line, sign, now, after, push, lines):
    a, b = now[pl.ds(line, 1), :], after[pl.ds(line, 1), :]
    late, early = push[pl.ds(line, 1), :], push[pl.ds(lines + line, 1), :]
    return (0.25 * sign * a, 0.25 * sign * (a + b), 2.0 * late, early - 0.5 * late, early)


def wipe(ref, row, lane):
    ref[pl.ds(row, LANES), pl.ds(lane, LANES)] = jnp.zeros((LANES, LANES), F32)


def final_one_kernel(z, mask, lists, depot, hub, cap, depot_state, hub_state, depot_push, hub_push,
                     th, co, cf, theta_out, cost_out, token, cols):
    i, where = pl.program_id(0), place()
    off = where[1] * z.one_lines
    token[...] = jnp.zeros_like(token)
    for k in range(z.per):
        for x, v in enumerate(vectors(i * z.per + k, -1.0, depot, depot_state, depot_push, z.dep_lines)):
            cols[x, pl.ds(k * LANES, LANES), :] = as_rows(v)
        for j in range(z.one_lines):
            @pl.when(mask[j, i * z.per + k] == 0)
            def _():
                wipe(theta_out, k * LANES, j * LANES)
                wipe(cost_out, k * LANES, j * LANES)

    def tiles(entries):
        for e in entries:
            k, j = split_of(z, e)
            lane, base = lane_of(j), lane_of(k)
            rows = vectors(off + j, -1.0, hub, hub_state, hub_push, z.hub_lines)
            km = 0.25 * cap[pl.ds(off + j, 1), :].astype(F32)
            for s in range(0, LANES, SUB):
                at = pl.multiple_of(base + s, SUB)
                both = [cols[x, pl.ds(at, SUB), :] + r for x, r in enumerate(rows)]
                theta, cost = result(scaled(th, at, lane, 0.5), scaled(co, at, lane, 0.25), piece(cf, at, lane),
                                     *both, km, -km)
                theta_out[pl.ds(at, SUB), pl.ds(lane, LANES)] = theta
                cost_out[pl.ds(at, SUB), pl.ds(lane, LANES)] = cost

    th, co, cf = (rows_of(ref, z, i) for ref in (th, co, cf))
    walk(lists, i, tiles)


def final_two_kernel(z, mask, lists, hub, zone, cap, hub_state, zone_state, hub_push, zone_push,
                     th, co, cf, theta_out, cost_out, cols, *bufs):
    arrays = (th, co, cf)
    i, where = pl.program_id(0), place()
    line = where[0] * z.two_lines + i
    fetched(z, i, arrays, bufs[:-1], bufs[-1], range(z.steps))
    hubs = vectors(line, 1.0, hub, hub_state, hub_push, z.hub_lines)
    km = 0.0625 * cap[pl.ds(line, 1), :].astype(F32)
    for x, v in enumerate((hubs[0], hubs[1], -hubs[2], -hubs[3], -hubs[4], km, -km)):
        cols[x] = as_rows(v)

    def closed(j, carry):
        @pl.when(mask[i, j] == 0)
        def _():
            wipe(theta_out, 0, lane_of(j))
            wipe(cost_out, 0, lane_of(j))
        return carry

    lax.fori_loop(0, z.zone_lines, closed, 0)

    def tiles(js):
        for j in js:
            lane = lane_of(j)
            rows = vectors(j, 1.0, zone, zone_state, zone_push, z.zone_lines)
            for s in range(0, LANES, SUB):
                both = [cols[x, s:s + SUB, :] + r for x, r in enumerate(rows)]
                theta, cost = result(scaled(th, s, lane, 0.5), scaled(co, s, lane, 0.25), piece(cf, s, lane),
                                     *both, cols[5, s:s + SUB, :], cols[6, s:s + SUB, :])
                theta_out[pl.ds(s, SUB), pl.ds(lane, LANES)] = theta
                cost_out[pl.ds(s, SUB), pl.ds(lane, LANES)] = cost

    th, co, cf = fetched(z, i, arrays, bufs[:-1], bufs[-1])
    walk(lists, i, tiles)


def final_one(z, mask, lists, depot, hub, cap, depot_state, hub_state, depot_push, hub_push, th, co, cf):
    dl, hl = z.dep_lines, z.hub_lines
    out = jax.ShapeDtypeStruct(th.shape, F32)
    return pl.pallas_call(
        functools.partial(final_one_kernel, z), grid=(z.steps,),
        in_specs=[smem(), smem(), whole(dl), whole(hl), whole(hl), whole(2 * dl), whole(hl), whole(3 * dl),
                  whole(3 * hl)] + [resident()] * 3,
        out_specs=[z.one(), z.one(), whole(8)], out_shape=[out, out, line_shape(8)],
        scratch_shapes=[pltpu.VMEM((5, z.per * LANES, LANES), F32)],
        compiler_params=params(8), name="final_one",
    )(mask, lists, depot, hub, cap, depot_state, hub_state, depot_push, hub_push, th, co, cf)


def final_two(z, mask, lists, hub, zone, cap, hub_state, zone_state, hub_push, zone_push, th, co, cf):
    zl, hl = z.zone_lines, z.hub_lines
    out = jax.ShapeDtypeStruct(th.shape, F32)
    return pl.pallas_call(
        functools.partial(final_two_kernel, z), grid=(z.steps,),
        in_specs=[smem(), smem(), whole(hl), whole(zl), whole(hl), whole(hl), whole(2 * zl), whole(3 * hl),
                  whole(3 * zl)] + [left()] * 3,
        out_specs=[z.two(), z.two()], out_shape=[out, out],
        scratch_shapes=[pltpu.VMEM((7, LANES, LANES), F32)] + buffers(z, th, co, cf),
        compiler_params=params(38), name="final_two",
    )(mask, lists, hub, zone, cap, hub_state, zone_state, hub_push, zone_push, *pinned(th, co, cf))


def on_device(rows, cols, theta_one, theta_two, cost_one, cost_two, depot_price, hub_price, zone_price,
              mask_one, mask_two, supply, demand, capacity, cot_flow_one, cot_flow_two,
              cot_depot, cot_hub, cot_zone):
    z = Sizes(*theta_one.shape, *theta_two.shape, hub_price.shape[0], theta_one.shape[0] * rows)
    dl, hl, zl = z.dep_lines, z.hub_lines, z.zone_lines
    lines = lambda v: v.reshape(-1, LANES)
    mask_one, = pinned(mask_one.T)
    mask_two, = pinned(mask_two)
    depot, hub, zone, cap = lines(depot_price), lines(hub_price), lines(zone_price), lines(capacity)
    supply, demand = lines(supply), lines(demand)
    cot_depot, cot_hub, cot_zone = lines(cot_depot), lines(cot_hub), lines(cot_zone)

    a1_one, a1_two, col_vec, zone_vec, depot_pre, zone_pre, list_one, list_two = first_pass(
        z, mask_one, mask_two, depot, hub, zone, cap, theta_one, cost_one, theta_two, cost_two)
    depot_sum, row_vec = join(col_terms(col_vec, cols), zone_vec, dl)
    sums = gather_terms(row_vec, "row", rows)
    (a2_one, a2_two, depot_vec, zone_vec, depot_state, zone_state, hub_state, hub_one, hub_two) = second_pass(
        z, list_one, list_two, depot, hub, zone, cap, supply, demand, cot_hub, depot_pre, zone_pre,
        depot_sum, sums, theta_one, cost_one, cot_flow_one, theta_two, cost_two, cot_flow_two)
    d_sums = col_terms(depot_vec, cols)
    z_sums = gather_terms(zone_vec, "row", rows)
    depot_push, zone_push, hub_vec = third_pass(
        z, list_one, list_two, supply, demand, cot_depot, cot_zone, depot_state, zone_state, hub_one, hub_two,
        d_sums, z_sums, a2_one, a2_two)
    hub_sums = gather_terms(plus(*col_terms(hub_vec, cols)), "row", rows)
    hub_push, col_vec, zone_vec = fourth_pass(z, list_one, list_two, cot_hub, depot_push, zone_push, hub_sums,
                                              a1_one, a1_two)
    if cols >= 4 and cols & (cols - 1) == 0:
        col_vec = plus(col_vec, swap(col_vec, "col", cols, 1))
        distances = range(2, cols, 2)
    else:
        distances = range(1, cols)
    col_vec, push = lax.optimization_barrier((col_vec, hub_push))
    terms = gather_terms(col_vec, "col", cols, distances)
    grad_theta_one, grad_cost_one, token = final_one(
        z, mask_one, list_one, depot, hub, cap, depot_state, hub_state, depot_push, push,
        theta_one, cost_one, cot_flow_one)
    depot_sum, row_vec = join(terms, zone_vec, dl, [token])
    row_vec, push = lax.optimization_barrier((row_vec, hub_push))
    terms = gather_terms(row_vec, "row", rows)
    grad_theta_two, grad_cost_two = final_two(
        z, mask_two, list_two, hub, zone, cap, hub_state, zone_state, push, zone_push,
        theta_two, cost_two, cot_flow_two)
    grad_depot, grad_hub, grad_zone = ends(z, depot_sum, terms, depot_push, hub_push, zone_push)
    return (grad_theta_one, grad_theta_two, grad_cost_one, grad_cost_two,
            grad_depot.reshape(-1), grad_hub.reshape(-1), grad_zone.reshape(-1))


def solution(mesh):
    split, row, col, copied = P("row", "col"), P("row"), P("col"), P()
    return jax.shard_map(
        functools.partial(on_device, mesh.shape["row"], mesh.shape["col"]),
        mesh=mesh,
        in_specs=(split, split, split, split, row, copied, col, split, split, row, col, copied, split, split,
                  row, copied, col),
        out_specs=(split, split, split, split, row, copied, col),
        check_vma=False,
    )
```

```python
import functools

import jax
import jax.numpy as jnp
from jax import lax
from jax.experimental import pallas as pl
from jax.experimental.pallas import tpu as pltpu
from jax.sharding import PartitionSpec as P

STEP_PRIMAL = 0.5
STEP_DUAL = 0.5
HUB_RATE = 4.0
LANES = 128
SUB = 32
F32 = jnp.float32
BF16 = jnp.bfloat16


def swap(value, axis, size, distance):
    if size & (size - 1) == 0:
        pairs = [(i, i ^ distance) for i in range(size)]
    else:
        pairs = [(i, (i + distance) % size) for i in range(size)]
    return lax.ppermute(value, axis, pairs)


def gather_terms(value, axis, size, distances=None):
    return [value] + [swap(value, axis, size, k) for k in distances or range(1, size)]


def col_terms(value, size):
    if size & (size - 1) or size < 4:
        return gather_terms(value, "col", size)
    both = plus(value, swap(value, "col", size, 1))
    return gather_terms(both, "col", size, range(2, size, 2))


def plus(*terms):
    def body(*refs):
        refs[-1][...] = add_all([ref[...] for ref in refs[:-1]])

    return pl.pallas_call(
        body, in_specs=[resident()] * len(terms), out_specs=resident(),
        out_shape=jax.ShapeDtypeStruct(terms[0].shape, F32),
        compiler_params=pltpu.CompilerParams(vmem_limit_bytes=2 * 2**20), name="plus")(*terms)


def join(terms, lower, first, after=()):
    lines = terms[0].shape[0]

    def body(*refs):
        refs = refs[len(after):]
        total = add_all([ref[...] for ref in refs[:-3]])
        refs[-2][...] = total[:first]
        refs[-1][0:lines - first, :] = total[first:]
        refs[-1][lines - first:, :] = refs[-3][...]

    return pl.pallas_call(
        body, in_specs=[resident()] * (len(after) + len(terms) + 1), out_specs=[resident()] * 2,
        out_shape=[line_shape(first), line_shape(lines - first + lower.shape[0])],
        compiler_params=pltpu.CompilerParams(vmem_limit_bytes=2 * 2**20), name="join")(*after, *terms, lower)


def ends(z, depot_sum, row_terms, depot_push, hub_push, zone_push):
    dl, hl, zl = z.dep_lines, z.hub_lines, z.zone_lines

    def body(depot_in, depot_last, hub_last, zone_last, *refs):
        total = add_all([ref[...] for ref in refs[:-3]])
        refs[-3][...] = depot_last[2 * dl:, :] - STEP_PRIMAL * depot_in[...]
        refs[-2][...] = hub_last[2 * hl:, :] - STEP_PRIMAL * total[:hl]
        refs[-1][...] = zone_last[2 * zl:, :] + STEP_PRIMAL * total[hl:]

    return pl.pallas_call(
        body, in_specs=[resident()] * (len(row_terms) + 4), out_specs=[resident()] * 3,
        out_shape=[line_shape(dl), line_shape(hl), line_shape(zl)],
        compiler_params=pltpu.CompilerParams(vmem_limit_bytes=2 * 2**20), name="ends",
    )(depot_sum, depot_push, hub_push, zone_push, *row_terms)


def add_all(terms):
    total = terms[0]
    for term in terms[1:]:
        total = total + term
    return total


def as_rows(line):
    return jnp.broadcast_to(line, (LANES, LANES)).T


def as_line(block):
    return jnp.sum(block.T, axis=0, keepdims=True)


def fold(value):
    return jnp.sum(value.reshape(-1, 8, LANES), axis=0)


def fold_line(value):
    return jnp.sum(value, axis=0, keepdims=True)


def piece(ref, row, lane):
    return ref[pl.ds(row, SUB), pl.ds(lane, LANES)].astype(F32)


class Sizes:
    def __init__(self, dep_rows, hub_cols, hub_rows, zone_cols, hubs, deps):
        self.dep_rows, self.hub_cols, self.hub_rows, self.zone_cols = dep_rows, hub_cols, hub_rows, zone_cols
        self.hubs, self.deps = hubs, deps
        self.dep_lines, self.one_lines = dep_rows // LANES, hub_cols // LANES
        self.two_lines, self.zone_lines = hub_rows // LANES, zone_cols // LANES
        self.hub_lines = hubs // LANES
        self.steps = self.two_lines
        self.per = self.dep_lines // self.steps
        assert self.per * self.steps == self.dep_lines

    def one(self):
        return pl.BlockSpec((self.per * LANES, self.hub_cols), lambda i: (i, 0))

    def list_shapes(self):
        return [jax.ShapeDtypeStruct((self.steps, self.per * self.one_lines + 1), jnp.int32),
                jax.ShapeDtypeStruct((self.steps, self.zone_lines + 1), jnp.int32)]

    def two(self):
        return pl.BlockSpec((LANES, self.zone_cols), lambda i: (i, 0))


def whole(lines):
    return pl.BlockSpec((lines, LANES), lambda i: (0, 0))


def smem():
    return pl.BlockSpec(memory_space=pltpu.SMEM)


def line_shape(lines):
    return jax.ShapeDtypeStruct((lines, LANES), F32)


def params(mib):
    return pltpu.CompilerParams(dimension_semantics=("arbitrary",), vmem_limit_bytes=mib * 2**20)


def resident():
    return pl.BlockSpec(memory_space=pltpu.VMEM)


def pinned(*arrays):
    return [pltpu.with_memory_space_constraint(array, pltpu.HBM) for array in arrays]


def place():
    return lax.axis_index("row"), lax.axis_index("col")


def rows_of(ref, z, i):
    rows = ref.shape[0] // z.steps
    return ref.at[pl.ds(pl.multiple_of(i * rows, rows), rows), :]


def listed(values, out, line):
    n = jnp.int32(0)
    for j, value in enumerate(values):
        out[line, n + 1] = jnp.int32(j)
        n = n + value
    out[line, 0] = n


def walk(lists, line, body, width=2):
    n = lists[line, 0]

    def group(start, size):
        body([lists[line, start + 1 + x] for x in range(size)])

    def full(p, carry):
        group(width * p, width)
        return carry

    lax.fori_loop(0, lax.div(n, width), full, 0)
    size = width // 2
    while size:
        rest = lax.rem(n, 2 * size)

        @pl.when(rest >= size)
        def _():
            group(n - rest, size)

        size //= 2


def lane_of(j):
    return pl.multiple_of(j * LANES, LANES)


def scaled(ref, row, lane, scale):
    return (ref[pl.ds(row, SUB), pl.ds(lane, LANES)] * jnp.asarray(scale, BF16)).astype(F32)


def fetched(z, i, arrays, bufs, sems, start=None, only=None):
    rows = [array.shape[0] // z.steps for array in arrays]

    def copy(x, step):
        at = pl.ds(pl.multiple_of(step * rows[x], rows[x]), rows[x])
        return pltpu.make_async_copy(arrays[x].at[at, :], bufs[x].at[at, :], sems.at[x, step])

    if start is not None:
        @pl.when(i == 0)
        def _():
            for step in start:
                for x in range(len(arrays)):
                    copy(x, step).start()
        return None
    only = range(len(arrays)) if only is None else only
    for x in only:
        copy(x, i).wait()
    return [bufs[x].at[pl.ds(pl.multiple_of(i * rows[x], rows[x]), rows[x]), :] for x in only]


def buffers(z, *arrays):
    return [pltpu.VMEM(array.shape, array.dtype) for array in arrays] + [
        pltpu.SemaphoreType.DMA((len(arrays), z.steps))]


def left():
    return pl.BlockSpec(memory_space=pltpu.HBM)


def clear(*refs):
    for ref in refs:
        ref[...] = jnp.zeros_like(ref)


def split_of(z, e):
    return lax.div(e, z.one_lines), lax.rem(e, z.one_lines)


def first_kernel(z, mask_one, mask_two, depot, hub, zone, cap, th1, co1, th2, co2,
                 a_one, a_two, col_out, zone_out, depot_pre, zone_pre, list_one, list_two,
                 row1, row0, both1, both0, shift_one, shift, keep, ksum, keeps, hub_acc, zone1, zone0, hub_two, *bufs):
    i, where = pl.program_id(0), place()
    smalls, bufs = bufs[:5], bufs[5:]
    off_one, off_two = where[1] * z.one_lines, where[0] * z.two_lines
    arrays = (th1, co1, th2, co2)
    small = [pltpu.make_async_copy(a, b, smalls[-1].at[x])
             for x, (a, b) in enumerate(zip((depot, hub, zone, cap), smalls[:-1]))]
    depot, hub, zone, cap = smalls[:-1]

    @pl.when(i == 0)
    def _():
        for copy in small:
            copy.start()
        clear(hub_acc, zone1, zone0)

    fetched(z, i, arrays, bufs[:-1], bufs[-1], range(1))

    @pl.when(i == 0)
    def _():
        for copy in small:
            copy.wait()

    fetched(z, i, arrays, bufs[:-1], bufs[-1], range(1, z.steps))
    a_one, a_two = rows_of(a_one, z, i), rows_of(a_two, z, i)
    clear(row1, row0, both1, both0, keeps)
    for k in range(z.per):
        shift_one[pl.ds(k * LANES, LANES), :] = as_rows(0.25 * depot[pl.ds(i * z.per + k, 1), :])
    shift[...] = as_rows(0.25 * hub[pl.ds(off_two + i, 1), :])
    keep[...] = as_rows(0.25 * cap[pl.ds(off_two + i, 1), :].astype(F32))
    ksum[...] = 0.5 * fold(keep[...])
    listed([mask_one[j, i * z.per + k] for k in range(z.per) for j in range(z.one_lines)], list_one, i)
    listed([mask_two[i, j] for j in range(z.zone_lines)], list_two, i)

    def tiles_one(entries):
        for x, e in enumerate(entries):
            k, j = split_of(z, e)
            lane, base = lane_of(j), lane_of(k)
            hrow = 0.25 * hub[pl.ds(off_one + j, 1), :]
            km = cap[pl.ds(off_one + j, 1), :].astype(F32)
            total = 0.5 * LANES / 8 * jnp.broadcast_to(km, (8, LANES))
            keeps[x, pl.ds(k, 1), :] += km
            for s in range(0, LANES, SUB):
                at = pl.multiple_of(base + s, SUB)
                half = scaled(th1, at, lane, 0.5)
                t0 = jnp.tanh(half)
                t1 = jnp.tanh((half - scaled(co1, at, lane, 0.25)) - (shift_one[pl.ds(at, SUB), :] + hrow))
                k1, k0 = km * t1, km * t0
                row1[x, pl.ds(at, SUB), :] += k1
                row0[x, pl.ds(at, SUB), :] += k0
                total = total + (fold(k1) - 0.5 * fold(k0))
                a_one[pl.ds(at, SUB), pl.ds(lane, LANES)] = (km - k1 * t1).astype(BF16)
            hub_acc[x, :, pl.ds(lane, LANES)] += total

    def tiles_two(js):
        zrows = [0.25 * zone[pl.ds(j, 1), :] for j in js]
        sum1 = [jnp.zeros((8, LANES), F32) for j in js]
        sum0 = [jnp.zeros((8, LANES), F32) for j in js]
        for s in range(0, LANES, SUB):
            hcol, km = shift[s:s + SUB, :], keep[s:s + SUB, :]
            all1, all0 = [], []
            for x, j in enumerate(js):
                lane = lane_of(j)
                half = scaled(th2, s, lane, 0.5)
                t0 = jnp.tanh(half)
                t1 = jnp.tanh((half - scaled(co2, s, lane, 0.25)) + (hcol + zrows[x]))
                k1, k0 = km * t1, km * t0
                all1.append(k1)
                all0.append(k0)
                sum1[x] = sum1[x] + fold(k1)
                sum0[x] = sum0[x] + fold(k0)
                a_two[pl.ds(s, SUB), pl.ds(lane, LANES)] = (km - k1 * t1).astype(BF16)
            both1[s:s + SUB, :] += add_all(all1)
            both0[s:s + SUB, :] += add_all(all0)
        for x, j in enumerate(js):
            zone1[x % 2, :, pl.ds(lane_of(j), LANES)] += sum1[x] - 2.0 * ksum[...]
            zone0[x % 2, :, pl.ds(lane_of(j), LANES)] += sum0[x] - 6.0 * ksum[...]

    th1, co1 = fetched(z, i, arrays, bufs[:-1], bufs[-1], only=(0, 1))
    walk(list_one, i, tiles_one)
    th2, co2 = fetched(z, i, arrays, bufs[:-1], bufs[-1], only=(2, 3))
    walk(list_two, i, tiles_two, 4)
    for k in range(z.per):
        line, at = i * z.per + k, pl.ds(k * LANES, LANES)
        line1, line0 = as_line(row1[0, at, :] + row1[1, at, :]), as_line(row0[0, at, :] + row0[1, at, :])
        half = 0.5 * jnp.sum(keeps[0, k:k + 1, :] + keeps[1, k:k + 1, :])
        col_out[pl.ds(line, 1), :] = half + line1 - 0.5 * line0
        depot_pre[pl.ds(line, 1), :] = half - 0.5 * line1
    opened = list_two[i, 0].astype(F32)
    hub_two[pl.ds(i, 1), :] = as_line(both1[...] - 0.5 * both0[...] + (0.5 * opened) * keep[...])

    @pl.when(i == z.steps - 1)
    def _():
        for j in range(z.zone_lines):
            at = slice(j * LANES, (j + 1) * LANES)
            line1, line0 = fold_line(zone1[0, :, at] + zone1[1, :, at]), fold_line(zone0[0, :, at] + zone0[1, :, at])
            zone_out[j:j + 1, :] = line1 - 0.5 * line0
            zone_pre[j:j + 1, :] = -0.5 * line1
        put_hub(z, where, col_out, z.dep_lines, hub_acc, hub_two)


def hub_line(hub_acc, j):
    at = slice(j * LANES, (j + 1) * LANES)
    return fold_line(hub_acc[0, :, at] + hub_acc[1, :, at])


def put_hub(z, where, out, base, hub_acc, hub_two):
    out[base:base + z.hub_lines, :] = jnp.zeros((z.hub_lines, LANES), F32)
    for j in range(z.two_lines):
        out[pl.ds(base + where[0] * z.two_lines + j, 1), :] = -hub_two[j:j + 1, :]
    for j in range(z.one_lines):
        at = base + where[1] * z.one_lines + j
        out[pl.ds(at, 1), :] = out[pl.ds(at, 1), :] + hub_line(hub_acc, j)


def first_pass(z, mask_one, mask_two, depot, hub, zone, cap, th1, co1, th2, co2):
    return pl.pallas_call(
        functools.partial(first_kernel, z),
        grid=(z.steps,),
        in_specs=[smem(), smem()] + [left()] * 8,
        out_specs=[resident(), resident(), whole(z.dep_lines + z.hub_lines), whole(z.zone_lines),
                   whole(z.dep_lines), whole(z.zone_lines), smem(), smem()],
        out_shape=[pltpu.VMEM(th1.shape, BF16), pltpu.VMEM(th2.shape, BF16),
                   line_shape(z.dep_lines + z.hub_lines), line_shape(z.zone_lines),
                   line_shape(z.dep_lines), line_shape(z.zone_lines)] + z.list_shapes(),
        scratch_shapes=[pltpu.VMEM((2, z.per * LANES, LANES), F32)] * 2 + [pltpu.VMEM((LANES, LANES), F32)] * 2
                       + [pltpu.VMEM((z.per * LANES, LANES), F32)] + [pltpu.VMEM((LANES, LANES), F32)] * 2
                       + [pltpu.VMEM((8, LANES), F32), pltpu.VMEM((2, z.per, LANES), F32), pltpu.VMEM((2, 8, z.hub_cols), F32)]
                       + [pltpu.VMEM((2, 8, z.zone_cols), F32)] * 2 + [pltpu.VMEM((z.two_lines, LANES), F32)]
                       + [pltpu.VMEM(v.shape, v.dtype) for v in (depot, hub, zone, cap)]
                       + [pltpu.SemaphoreType.DMA((4,))] + buffers(z, th1, co1, th2, co2),
        compiler_params=params(28), name="first_pass",
    )(mask_one, mask_two, *pinned(depot, hub, zone, cap, th1, co1, th2, co2))


def second_kernel(z, terms, list_one, list_two, depot, hub, zone, cap, supply, demand, cot_hub,
                  depot_pre, zone_pre, depot_sum, *rest):
    sums, rest = rest[:terms], rest[terms:]
    (th1, co1, cf1, th2, co2, cf2,
     a_one, a_two, depot_out, zone_out, depot_state, zone_state, hub_state, hub_one_out, hub_two_out,
     rowk, rowa, rowe, both, shift_one, shift, keep, pushes, hub_acc, zonek, zonea, zonee,
     shift_d, shift_h, shift_z, *bufs) = rest
    arrays = (th1, co1, cf1, th2, co2, cf2)
    i, where = pl.program_id(0), place()
    off_one, off_two = where[1] * z.one_lines, where[0] * z.two_lines
    dl, zl, hl = z.dep_lines, z.zone_lines, z.hub_lines

    fetched(z, i, arrays, bufs[:-1], bufs[-1], range(z.steps))

    a_one, a_two = rows_of(a_one, z, i), rows_of(a_two, z, i)

    @pl.when(i == 0)
    def _():
        clear(hub_acc, zonek, zonea, zonee)
        total = sums[0][...]
        for term in sums[1:]:
            total = total + term[...]
        grow_d = jnp.exp(STEP_DUAL * (depot_sum[...] / z.hubs - 0.5 * supply[...].astype(F32)))
        grow_z = jnp.exp(STEP_DUAL * (0.125 * demand[...].astype(F32) - total[hl:, :] / z.hubs))
        new_d, new_z = depot[...] * grow_d, zone[...] * grow_z
        new_h = hub[...] + HUB_RATE * total[:hl, :] / z.deps
        depot_state[0:dl, :] = new_d
        depot_state[dl:2 * dl, :] = grow_d
        zone_state[0:zl, :] = new_z
        zone_state[zl:2 * zl, :] = grow_z
        hub_state[...] = new_h
        shift_d[...] = 0.25 * (depot[...] + new_d)
        shift_h[...] = 0.25 * (hub[...] + new_h)
        shift_z[...] = 0.25 * (zone[...] + new_z)

    push = 2.0 * HUB_RATE / z.deps
    clear(rowk, rowa, rowe, both)
    for k in range(z.per):
        shift_one[pl.ds(k * LANES, LANES), :] = as_rows(shift_d[pl.ds(i * z.per + k, 1), :])
    shift[...] = as_rows(shift_h[pl.ds(off_two + i, 1), :])
    pushes[...] = as_rows(push * cot_hub[pl.ds(off_two + i, 1), :])
    keep[...] = as_rows(0.25 * cap[pl.ds(off_two + i, 1), :].astype(F32))

    def tiles_one(entries):
        for x, e in enumerate(entries):
            k, j = split_of(z, e)
            lane, base = lane_of(j), lane_of(k)
            hrow = shift_h[pl.ds(off_one + j, 1), :]
            prow = push * cot_hub[pl.ds(off_one + j, 1), :]
            km = cap[pl.ds(off_one + j, 1), :].astype(F32)
            total = jnp.zeros((8, LANES), F32)
            for s in range(0, LANES, SUB):
                at = pl.multiple_of(base + s, SUB)
                t2 = jnp.tanh((scaled(th1, at, lane, 0.5) - scaled(co1, at, lane, 0.5))
                              - (shift_one[pl.ds(at, SUB), :] + hrow))
                k2 = km * t2
                a2 = km - k2 * t2
                e = (piece(cf1, at, lane) + prow) * a2
                rowk[x, pl.ds(at, SUB), :] += k2
                rowa[x, pl.ds(at, SUB), :] += a2
                rowe[x, pl.ds(at, SUB), :] += e
                total = total + fold(e)
                a_one[pl.ds(at, SUB), pl.ds(lane, LANES)] = a2.astype(BF16)
            hub_acc[x, :, pl.ds(lane, LANES)] += total

    def tiles_two(js):
        zrows = [shift_z[pl.ds(j, 1), :] for j in js]
        sumk, suma, sume = ([jnp.zeros((8, LANES), F32) for j in js] for _ in range(3))
        for s in range(0, LANES, SUB):
            hcol, km, pcol = shift[s:s + SUB, :], keep[s:s + SUB, :], pushes[s:s + SUB, :]
            alle = []
            for x, j in enumerate(js):
                lane = lane_of(j)
                t2 = jnp.tanh((scaled(th2, s, lane, 0.5) - scaled(co2, s, lane, 0.5)) + (hcol + zrows[x]))
                k2 = km * t2
                a2 = km - k2 * t2
                e = (piece(cf2, s, lane) - pcol) * a2
                alle.append(e)
                sumk[x] = sumk[x] + fold(k2)
                suma[x] = suma[x] + fold(a2)
                sume[x] = sume[x] + fold(e)
                a_two[pl.ds(s, SUB), pl.ds(lane, LANES)] = a2.astype(BF16)
            both[s:s + SUB, :] += add_all(alle)
        for x, j in enumerate(js):
            zonek[x % 2, :, pl.ds(lane_of(j), LANES)] += sumk[x]
            zonea[x % 2, :, pl.ds(lane_of(j), LANES)] += suma[x]
            zonee[x % 2, :, pl.ds(lane_of(j), LANES)] += sume[x]

    th1, co1, cf1 = fetched(z, i, arrays, bufs[:-1], bufs[-1], only=(0, 1, 2))
    walk(list_one, i, tiles_one)
    th2, co2, cf2 = fetched(z, i, arrays, bufs[:-1], bufs[-1], only=(3, 4, 5))
    walk(list_two, i, tiles_two, 4)
    for k in range(z.per):
        line, at = i * z.per + k, pl.ds(k * LANES, LANES)
        depot_out[pl.ds(line, 1), :] = depot_pre[pl.ds(line, 1), :] + as_line(rowk[0, at, :] + rowk[1, at, :])
        depot_out[pl.ds(dl + line, 1), :] = as_line(rowa[0, at, :] + rowa[1, at, :])
        depot_out[pl.ds(2 * dl + line, 1), :] = as_line(rowe[0, at, :] + rowe[1, at, :])
    hub_two_out[pl.ds(i, 1), :] = as_line(both[...])

    @pl.when(i == z.steps - 1)
    def _():
        for j in range(zl):
            at = slice(j * LANES, (j + 1) * LANES)
            zone_out[j:j + 1, :] = zone_pre[j:j + 1, :] + fold_line(zonek[0, :, at] + zonek[1, :, at])
            zone_out[zl + j:zl + j + 1, :] = fold_line(zonea[0, :, at] + zonea[1, :, at])
            zone_out[2 * zl + j:2 * zl + j + 1, :] = fold_line(zonee[0, :, at] + zonee[1, :, at])
        for j in range(z.one_lines):
            hub_one_out[j:j + 1, :] = hub_line(hub_acc, j)


def second_pass(z, list_one, list_two, depot, hub, zone, cap, supply, demand, cot_hub,
                depot_pre, zone_pre, depot_sum, sums, th1, co1, cf1, th2, co2, cf2):
    dl, zl, hl = z.dep_lines, z.zone_lines, z.hub_lines
    return pl.pallas_call(
        functools.partial(second_kernel, z, len(sums)),
        grid=(z.steps,),
        in_specs=[smem(), smem(), whole(dl), whole(hl), whole(zl), whole(hl), whole(dl), whole(zl), whole(hl),
                  whole(dl), whole(zl), whole(dl)] + [whole(hl + zl)] * len(sums)
                 + [left()] * 6,
        out_specs=[resident(), resident(), whole(3 * dl), whole(3 * zl), whole(2 * dl), whole(2 * zl), whole(hl),
                   whole(z.one_lines), whole(z.two_lines)],
        out_shape=[pltpu.VMEM(th1.shape, BF16), pltpu.VMEM(th2.shape, BF16),
                   line_shape(3 * dl), line_shape(3 * zl), line_shape(2 * dl), line_shape(2 * zl), line_shape(hl),
                   line_shape(z.one_lines), line_shape(z.two_lines)],
        scratch_shapes=[pltpu.VMEM((2, z.per * LANES, LANES), F32)] * 3 + [pltpu.VMEM((LANES, LANES), F32)]
                       + [pltpu.VMEM((z.per * LANES, LANES), F32)] + [pltpu.VMEM((LANES, LANES), F32)] * 3
                       + [pltpu.VMEM((2, 8, z.hub_cols), F32)] + [pltpu.VMEM((2, 8, z.zone_cols), F32)] * 3
                       + [pltpu.VMEM((dl, LANES), F32), pltpu.VMEM((hl, LANES), F32), pltpu.VMEM((zl, LANES), F32)]
                       + buffers(z, th1, co1, cf1, th2, co2, cf2),
        compiler_params=params(38), name="second_pass",
    )(list_one, list_two, depot, hub, zone, cap, supply, demand, cot_hub, depot_pre, zone_pre, depot_sum,
      *sums, *pinned(th1, co1, cf1, th2, co2, cf2))


def third_kernel(z, d_terms, z_terms, list_one, list_two, supply, demand, cot_depot, cot_zone, depot_state, zone_state,
                 hub_one_in, hub_two_in, *rest):
    d_sums, rest = rest[:d_terms], rest[d_terms:]
    z_sums, rest = rest[:z_terms], rest[z_terms:]
    a_one, a_two, depot_out, zone_out, hub_out, row, shift_one, hub_acc, hub_two = rest
    i, where = pl.program_id(0), place()
    dl, zl = z.dep_lines, z.zone_lines
    rate = STEP_DUAL / z.hubs

    a_one, a_two = rows_of(a_one, z, i), rows_of(a_two, z, i)

    @pl.when(i == 0)
    def _():
        hub_acc[...] = jnp.zeros_like(hub_acc)
        total = d_sums[0][...]
        for term in d_sums[1:]:
            total = total + term[...]
        grow = jnp.exp(STEP_DUAL * (total[0:dl, :] / z.hubs - 0.5 * supply[...].astype(F32)))
        first, first_grow = depot_state[0:dl, :], depot_state[dl:2 * dl, :]
        push = cot_depot[...] * (first * grow) * rate
        reached = 0.25 * (total[2 * dl:3 * dl, :] + 2.0 * push * total[dl:2 * dl, :])
        adj = cot_depot[...] * grow - STEP_PRIMAL * reached
        depot_out[0:dl, :] = push
        depot_out[dl:2 * dl, :] = adj * first * rate
        depot_out[2 * dl:3 * dl, :] = adj * first_grow - STEP_PRIMAL * reached
        total = z_sums[0][...]
        for term in z_sums[1:]:
            total = total + term[...]
        grow = jnp.exp(STEP_DUAL * (0.125 * demand[...].astype(F32) - total[0:zl, :] / z.hubs))
        first, first_grow = zone_state[0:zl, :], zone_state[zl:2 * zl, :]
        push = -(cot_zone[...] * (first * grow) * rate)
        reached = 0.25 * (total[2 * zl:3 * zl, :] + 2.0 * push * total[zl:2 * zl, :])
        adj = cot_zone[...] * grow + STEP_PRIMAL * reached
        zone_out[0:zl, :] = push
        zone_out[zl:2 * zl, :] = -(adj * first * rate)
        zone_out[2 * zl:3 * zl, :] = adj * first_grow + STEP_PRIMAL * reached

    clear(row)
    for k in range(z.per):
        shift_one[pl.ds(k * LANES, LANES), :] = as_rows(depot_out[pl.ds(i * z.per + k, 1), :])

    def tiles_one(entries):
        for x, e in enumerate(entries):
            k, j = split_of(z, e)
            lane, base = lane_of(j), lane_of(k)
            total = jnp.zeros((8, LANES), F32)
            for s in range(0, LANES, SUB):
                at = pl.multiple_of(base + s, SUB)
                total = total + fold(piece(a_one, at, lane) * shift_one[pl.ds(at, SUB), :])
            hub_acc[x, :, pl.ds(lane, LANES)] += total

    def tiles_two(js):
        zrows = [zone_out[pl.ds(j, 1), :] for j in js]
        for s in range(0, LANES, SUB):
            row[s:s + SUB, :] += add_all([piece(a_two, s, lane_of(j)) * zrows[x] for x, j in enumerate(js)])

    walk(list_one, i, tiles_one)
    walk(list_two, i, tiles_two, 4)
    hub_two[pl.ds(i, 1), :] = -0.25 * (hub_two_in[pl.ds(i, 1), :] + 2.0 * as_line(row[...]))

    @pl.when(i == z.steps - 1)
    def _():
        hub_out[...] = jnp.zeros_like(hub_out)
        for j in range(z.two_lines):
            hub_out[pl.ds(where[0] * z.two_lines + j, 1), :] = -hub_two[j:j + 1, :]
        for j in range(z.one_lines):
            at = where[1] * z.one_lines + j
            line = hub_line(hub_acc, j)
            hub_out[pl.ds(at, 1), :] = hub_out[pl.ds(at, 1), :] - 0.25 * (hub_one_in[j:j + 1, :] + 2.0 * line)


def third_pass(z, list_one, list_two, supply, demand, cot_depot, cot_zone, depot_state, zone_state, hub_one, hub_two,
               d_sums, z_sums, a_one, a_two):
    dl, zl, hl = z.dep_lines, z.zone_lines, z.hub_lines
    return pl.pallas_call(
        functools.partial(third_kernel, z, len(d_sums), len(z_sums)),
        grid=(z.steps,),
        in_specs=[smem(), smem(), whole(dl), whole(zl), whole(dl), whole(zl), whole(2 * dl), whole(2 * zl),
                  whole(z.one_lines), whole(z.two_lines)]
                 + [whole(3 * dl)] * len(d_sums) + [whole(3 * zl)] * len(z_sums) + [resident(), resident()],
        out_specs=[whole(3 * dl), whole(3 * zl), whole(hl)],
        out_shape=[line_shape(3 * dl), line_shape(3 * zl), line_shape(hl)],
        scratch_shapes=[pltpu.VMEM((LANES, LANES), F32), pltpu.VMEM((z.per * LANES, LANES), F32),
                        pltpu.VMEM((2, 8, z.hub_cols), F32), pltpu.VMEM((z.two_lines, LANES), F32)],
        compiler_params=params(6), name="third_pass",
    )(list_one, list_two, supply, demand, cot_depot, cot_zone, depot_state, zone_state, hub_one, hub_two,
      *d_sums, *z_sums, a_one, a_two)


def fourth_kernel(z, terms, list_one, list_two, cot_hub, depot_push, zone_push, *rest):
    sums, rest = rest[:terms], rest[terms:]
    (a_one, a_two, hub_out, col_out, zone_out, row, both, shift_one, shift, hub_acc, zone_acc, hub_two, mix) = rest
    i, where = pl.program_id(0), place()
    off_one, off_two = where[1] * z.one_lines, where[0] * z.two_lines
    dl, zl, hl = z.dep_lines, z.zone_lines, z.hub_lines
    rate = HUB_RATE / z.deps

    a_one, a_two = rows_of(a_one, z, i), rows_of(a_two, z, i)

    @pl.when(i == 0)
    def _():
        hub_acc[...] = jnp.zeros_like(hub_acc)
        zone_acc[...] = jnp.zeros_like(zone_acc)
        total = sums[0][...]
        for term in sums[1:]:
            total = total + term[...]
        adj = cot_hub[...] + STEP_PRIMAL * total
        late, early = cot_hub[...] * rate, adj * rate
        hub_out[0:hl, :] = late
        hub_out[hl:2 * hl, :] = early
        hub_out[2 * hl:3 * hl, :] = adj + STEP_PRIMAL * total
        mix[0:hl, :] = 0.25 * (2.0 * early - late)
        mix[hl:hl + dl, :] = 0.25 * (2.0 * depot_push[dl:2 * dl, :] - depot_push[0:dl, :])
        mix[hl + dl:, :] = 0.25 * (2.0 * zone_push[zl:2 * zl, :] - zone_push[0:zl, :])

    clear(row, both)
    for k in range(z.per):
        shift_one[pl.ds(k * LANES, LANES), :] = as_rows(mix[pl.ds(hl + i * z.per + k, 1), :])
    shift[...] = as_rows(mix[pl.ds(off_two + i, 1), :])

    def tiles_one(entries):
        for x, e in enumerate(entries):
            k, j = split_of(z, e)
            lane, base = lane_of(j), lane_of(k)
            hrow = mix[pl.ds(off_one + j, 1), :]
            total = jnp.zeros((8, LANES), F32)
            for s in range(0, LANES, SUB):
                at = pl.multiple_of(base + s, SUB)
                y = piece(a_one, at, lane) * (shift_one[pl.ds(at, SUB), :] + hrow)
                row[x, pl.ds(at, SUB), :] += y
                total = total + fold(y)
            hub_acc[x, :, pl.ds(lane, LANES)] += total

    def tiles_two(js):
        zrows = [mix[pl.ds(hl + dl + j, 1), :] for j in js]
        totals = [jnp.zeros((8, LANES), F32) for j in js]
        for s in range(0, LANES, SUB):
            ys = [piece(a_two, s, lane_of(j)) * (zrows[x] - shift[s:s + SUB, :]) for x, j in enumerate(js)]
            both[s:s + SUB, :] += add_all(ys)
            totals = [total + fold(y) for total, y in zip(totals, ys)]
        for x, j in enumerate(js):
            zone_acc[x % 2, :, pl.ds(lane_of(j), LANES)] += totals[x]

    walk(list_one, i, tiles_one)
    walk(list_two, i, tiles_two, 4)
    for k in range(z.per):
        at = pl.ds(k * LANES, LANES)
        col_out[pl.ds(i * z.per + k, 1), :] = as_line(row[0, at, :] + row[1, at, :])
    hub_two[pl.ds(i, 1), :] = as_line(both[...])

    @pl.when(i == z.steps - 1)
    def _():
        for j in range(zl):
            zone_out[j:j + 1, :] = hub_line(zone_acc, j)
        put_hub(z, where, col_out, dl, hub_acc, hub_two)


def fourth_pass(z, list_one, list_two, cot_hub, depot_push, zone_push, sums, a_one, a_two):
    dl, zl, hl = z.dep_lines, z.zone_lines, z.hub_lines
    return pl.pallas_call(
        functools.partial(fourth_kernel, z, len(sums)),
        grid=(z.steps,),
        in_specs=[smem(), smem(), whole(hl), whole(3 * dl), whole(3 * zl)] + [whole(hl)] * len(sums) + [resident(), resident()],
        out_specs=[whole(3 * hl), whole(dl + hl), whole(zl)],
        out_shape=[line_shape(3 * hl), line_shape(dl + hl), line_shape(zl)],
        scratch_shapes=[pltpu.VMEM((2, z.per * LANES, LANES), F32), pltpu.VMEM((LANES, LANES), F32),
                        pltpu.VMEM((z.per * LANES, LANES), F32), pltpu.VMEM((LANES, LANES), F32),
                        pltpu.VMEM((2, 8, z.hub_cols), F32), pltpu.VMEM((2, 8, z.zone_cols), F32),
                        pltpu.VMEM((z.two_lines, LANES), F32), pltpu.VMEM((hl + dl + zl, LANES), F32)],
        compiler_params=params(6), name="fourth_pass",
    )(list_one, list_two, cot_hub, depot_push, zone_push, *sums, a_one, a_two)


def result(half, quarter, cf, shift1, shift2, twice_late, mixed, early, km, minus):
    once = half - quarter
    t0 = jnp.tanh(half)
    t1 = jnp.tanh(once + shift1)
    t2 = jnp.tanh((once - quarter) + shift2)
    middle = mixed * (1.0 - t1 * t1)
    last = (cf + twice_late) * (1.0 - t2 * t2) + middle
    return km * (last + (middle - early * (1.0 - t0 * t0))), minus * last


def vectors(line, sign, now, after, push, lines):
    a, b = now[pl.ds(line, 1), :], after[pl.ds(line, 1), :]
    late, early = push[pl.ds(line, 1), :], push[pl.ds(lines + line, 1), :]
    return (0.25 * sign * a, 0.25 * sign * (a + b), 2.0 * late, early - 0.5 * late, early)


def wipe(ref, row, lane):
    ref[pl.ds(row, LANES), pl.ds(lane, LANES)] = jnp.zeros((LANES, LANES), F32)


def final_one_kernel(z, mask, lists, depot, hub, cap, depot_state, hub_state, depot_push, hub_push,
                     th, co, cf, theta_out, cost_out, token, cols):
    i, where = pl.program_id(0), place()
    off = where[1] * z.one_lines
    token[...] = jnp.zeros_like(token)
    for k in range(z.per):
        for x, v in enumerate(vectors(i * z.per + k, -1.0, depot, depot_state, depot_push, z.dep_lines)):
            cols[x, pl.ds(k * LANES, LANES), :] = as_rows(v)
        for j in range(z.one_lines):
            @pl.when(mask[j, i * z.per + k] == 0)
            def _():
                wipe(theta_out, k * LANES, j * LANES)
                wipe(cost_out, k * LANES, j * LANES)

    def tiles(entries):
        for e in entries:
            k, j = split_of(z, e)
            lane, base = lane_of(j), lane_of(k)
            rows = vectors(off + j, -1.0, hub, hub_state, hub_push, z.hub_lines)
            km = 0.25 * cap[pl.ds(off + j, 1), :].astype(F32)
            for s in range(0, LANES, SUB):
                at = pl.multiple_of(base + s, SUB)
                both = [cols[x, pl.ds(at, SUB), :] + r for x, r in enumerate(rows)]
                theta, cost = result(scaled(th, at, lane, 0.5), scaled(co, at, lane, 0.25), piece(cf, at, lane),
                                     *both, km, -km)
                theta_out[pl.ds(at, SUB), pl.ds(lane, LANES)] = theta
                cost_out[pl.ds(at, SUB), pl.ds(lane, LANES)] = cost

    th, co, cf = (rows_of(ref, z, i) for ref in (th, co, cf))
    walk(lists, i, tiles)


def final_two_kernel(z, mask, lists, hub, zone, cap, hub_state, zone_state, hub_push, zone_push,
                     th, co, cf, theta_out, cost_out, cols, *bufs):
    arrays = (th, co, cf)
    i, where = pl.program_id(0), place()
    line = where[0] * z.two_lines + i
    fetched(z, i, arrays, bufs[:-1], bufs[-1], range(z.steps))
    hubs = vectors(line, 1.0, hub, hub_state, hub_push, z.hub_lines)
    km = 0.0625 * cap[pl.ds(line, 1), :].astype(F32)
    first, both, late, early, keep = (as_rows(v) for v in (hubs[0], hubs[1], -hubs[2], -hubs[4], km))
    for x, v in enumerate((first, both, late, early - 0.25 * late, early, keep, -keep)):
        cols[x] = v

    def closed(j, carry):
        @pl.when(mask[i, j] == 0)
        def _():
            wipe(theta_out, 0, lane_of(j))
            wipe(cost_out, 0, lane_of(j))
        return carry

    lax.fori_loop(0, z.zone_lines, closed, 0)

    def tiles(js):
        for j in js:
            lane = lane_of(j)
            rows = vectors(j, 1.0, zone, zone_state, zone_push, z.zone_lines)
            for s in range(0, LANES, SUB):
                both = [cols[x, s:s + SUB, :] + r for x, r in enumerate(rows)]
                theta, cost = result(scaled(th, s, lane, 0.5), scaled(co, s, lane, 0.25), piece(cf, s, lane),
                                     *both, cols[5, s:s + SUB, :], cols[6, s:s + SUB, :])
                theta_out[pl.ds(s, SUB), pl.ds(lane, LANES)] = theta
                cost_out[pl.ds(s, SUB), pl.ds(lane, LANES)] = cost

    th, co, cf = fetched(z, i, arrays, bufs[:-1], bufs[-1])
    walk(lists, i, tiles)


def final_one(z, mask, lists, depot, hub, cap, depot_state, hub_state, depot_push, hub_push, th, co, cf):
    dl, hl = z.dep_lines, z.hub_lines
    out = jax.ShapeDtypeStruct(th.shape, F32)
    return pl.pallas_call(
        functools.partial(final_one_kernel, z), grid=(z.steps,),
        in_specs=[smem(), smem(), whole(dl), whole(hl), whole(hl), whole(2 * dl), whole(hl), whole(3 * dl),
                  whole(3 * hl)] + [resident()] * 3,
        out_specs=[z.one(), z.one(), whole(8)], out_shape=[out, out, line_shape(8)],
        scratch_shapes=[pltpu.VMEM((5, z.per * LANES, LANES), F32)],
        compiler_params=params(8), name="final_one",
    )(mask, lists, depot, hub, cap, depot_state, hub_state, depot_push, hub_push, th, co, cf)


def final_two(z, mask, lists, hub, zone, cap, hub_state, zone_state, hub_push, zone_push, th, co, cf):
    zl, hl = z.zone_lines, z.hub_lines
    out = jax.ShapeDtypeStruct(th.shape, F32)
    return pl.pallas_call(
        functools.partial(final_two_kernel, z), grid=(z.steps,),
        in_specs=[smem(), smem(), whole(hl), whole(zl), whole(hl), whole(hl), whole(2 * zl), whole(3 * hl),
                  whole(3 * zl)] + [left()] * 3,
        out_specs=[z.two(), z.two()], out_shape=[out, out],
        scratch_shapes=[pltpu.VMEM((7, LANES, LANES), F32)] + buffers(z, th, co, cf),
        compiler_params=params(38), name="final_two",
    )(mask, lists, hub, zone, cap, hub_state, zone_state, hub_push, zone_push, *pinned(th, co, cf))


def on_device(rows, cols, theta_one, theta_two, cost_one, cost_two, depot_price, hub_price, zone_price,
              mask_one, mask_two, supply, demand, capacity, cot_flow_one, cot_flow_two,
              cot_depot, cot_hub, cot_zone):
    z = Sizes(*theta_one.shape, *theta_two.shape, hub_price.shape[0], theta_one.shape[0] * rows)
    dl, hl, zl = z.dep_lines, z.hub_lines, z.zone_lines
    lines = lambda v: v.reshape(-1, LANES)
    mask_one, = pinned(mask_one.T)
    mask_two, = pinned(mask_two)
    depot, hub, zone, cap = lines(depot_price), lines(hub_price), lines(zone_price), lines(capacity)
    supply, demand = lines(supply), lines(demand)
    cot_depot, cot_hub, cot_zone = lines(cot_depot), lines(cot_hub), lines(cot_zone)

    a1_one, a1_two, col_vec, zone_vec, depot_pre, zone_pre, list_one, list_two = first_pass(
        z, mask_one, mask_two, depot, hub, zone, cap, theta_one, cost_one, theta_two, cost_two)
    depot_sum, row_vec = join(col_terms(col_vec, cols), zone_vec, dl)
    sums = gather_terms(row_vec, "row", rows)
    (a2_one, a2_two, depot_vec, zone_vec, depot_state, zone_state, hub_state, hub_one, hub_two) = second_pass(
        z, list_one, list_two, depot, hub, zone, cap, supply, demand, cot_hub, depot_pre, zone_pre,
        depot_sum, sums, theta_one, cost_one, cot_flow_one, theta_two, cost_two, cot_flow_two)
    d_sums = col_terms(depot_vec, cols)
    z_sums = gather_terms(zone_vec, "row", rows)
    depot_push, zone_push, hub_vec = third_pass(
        z, list_one, list_two, supply, demand, cot_depot, cot_zone, depot_state, zone_state, hub_one, hub_two,
        d_sums, z_sums, a2_one, a2_two)
    hub_sums = gather_terms(plus(*col_terms(hub_vec, cols)), "row", rows)
    hub_push, col_vec, zone_vec = fourth_pass(z, list_one, list_two, cot_hub, depot_push, zone_push, hub_sums,
                                              a1_one, a1_two)
    if cols >= 4 and cols & (cols - 1) == 0:
        col_vec = plus(col_vec, swap(col_vec, "col", cols, 1))
        distances = range(2, cols, 2)
    else:
        distances = range(1, cols)
    col_vec, push = lax.optimization_barrier((col_vec, hub_push))
    terms = gather_terms(col_vec, "col", cols, distances)
    grad_theta_one, grad_cost_one, token = final_one(
        z, mask_one, list_one, depot, hub, cap, depot_state, hub_state, depot_push, push,
        theta_one, cost_one, cot_flow_one)
    depot_sum, row_vec = join(terms, zone_vec, dl, [token])
    row_vec, push = lax.optimization_barrier((row_vec, hub_push))
    terms = gather_terms(row_vec, "row", rows)
    grad_theta_two, grad_cost_two = final_two(
        z, mask_two, list_two, hub, zone, cap, hub_state, zone_state, push, zone_push,
        theta_two, cost_two, cot_flow_two)
    grad_depot, grad_hub, grad_zone = ends(z, depot_sum, terms, depot_push, hub_push, zone_push)
    return (grad_theta_one, grad_theta_two, grad_cost_one, grad_cost_two,
            grad_depot.reshape(-1), grad_hub.reshape(-1), grad_zone.reshape(-1))


def solution(mesh):
    split, row, col, copied = P("row", "col"), P("row"), P("col"), P()
    return jax.shard_map(
        functools.partial(on_device, mesh.shape["row"], mesh.shape["col"]),
        mesh=mesh,
        in_specs=(split, split, split, split, row, copied, col, split, split, row, col, copied, split, split,
                  row, copied, col),
        out_specs=(split, split, split, split, row, copied, col),
        check_vma=False,
    )
```
